256 devices in a mesh: seq: 8 (over z), dp: 32 (over y, x, core).
Axes of the slice: x: 4, y: 4, z: 8, core: 2. Of those that a mesh axis runs over, the one named last changes fastest.
Arguments:
- frames: bfloat16 [32, 64, 8, 32, 128], P('dp', 'seq'), may hold values from -6 to 6
- clip_ids: int32 [32, 64], P('dp'), may hold values from 0 to 8, never falling along the last dimension, each value on 1 to 20 neighbouring positions
- cotangent: bfloat16 [32, 64, 8, 32, 128], P('dp', 'seq'), may hold values from -6 to 6
- conv1_weight: bfloat16 [3456, 128], replicated, may hold values from -0.109375 to 0.109375
- conv2_weight: bfloat16 [3456, 128], replicated, may hold values from -0.109375 to 0.109375
Outputs:
- block_out: bfloat16 [32, 64, 8, 32, 128], P('dp', 'seq')
- input_grad: bfloat16 [32, 64, 8, 32, 128], P('dp', 'seq')
- conv1_grad: float32 [3456, 128], P('dp')
- conv2_grad: float32 [3456, 128], P('dp')
The draws below stay inside these ranges and needn't reach their ends.
Inputs may be any that keep to these rules, and one draw needn't show every extreme that they name: `clip_ids`: in each row the clip numbers never fall; each clip covers 1 to 20 consecutive frames, and one covers exactly that many.
All inputs are finite; a program needn't handle non-finite values.
Results may differ from the reference program's by a relative error of at most 0.0055.
Values may be sent and summed in bfloat16 or wider, within the bound.
No kernel may reach another device: no remote copies, remote signals or barrier semaphores. Data moves between devices by JAX's collectives and lax.ppermute only.
A program may use at most 128 MiB of HBM per device.

```python
import math
import jax
import jax.numpy as jnp
import numpy as np
from jax import lax

C = 128
GROUPS = 32
F_DEV = 8
HT = 8
WT = 32
BATCH = 32
FRAMES = 64
N_SEQ = 8


def block_scale(stream_key, shape, cuts, low, largest):
    def one(dim, shards_of):
        draws = jax.random.uniform(jax.random.fold_in(jax.random.fold_in(stream_key, 6), dim), (shards_of,), jnp.float32, low / len(cuts), largest / len(cuts))
        return jnp.repeat(jnp.exp(draws), shape[dim] // shards_of).reshape((-1,) + (1,) * (len(shape) - dim - 1))

    factor_of = one(*cuts[0])
    for cut in cuts[1:]:
        factor_of = factor_of * one(*cut)
    return factor_of


def split_up(amount, total, reach, skew):
    portions = [(1 << 20) // math.isqrt(grade ** skew) + 1 for grade in range(2, amount + 1)]
    surplus, holding = total - reach - (amount - 1), [1] * (amount - 1)
    while surplus > 0:
        candidates = [i for i in range(amount - 1) if holding[i] < reach]
        mass, left = sum([portions[i] for i in candidates]), surplus
        for i in candidates:
            more = min(reach - holding[i], max(1, left * portions[i] // mass), surplus)
            holding[i] = holding[i] + more
            surplus = surplus - more
    return np.array([reach] + holding)


def ragged_sizes(stream_key, number_of, total, bound, slope):
    if number_of == 2:
        one = jax.random.randint(stream_key, (), max(1, total - bound), min(bound, total - 1) + 1)
        return jnp.stack([one, total - one])
    tallies = jnp.asarray(split_up(number_of, total, bound, slope), jnp.int32)
    pairs = (number_of - 1) // 2
    source_of, taker = tallies[1:1 + 2 * pairs:2], tallies[2:2 + 2 * pairs:2]
    slack = jnp.minimum(source_of - 1, bound - taker)
    shifted = jax.random.randint(jax.random.fold_in(stream_key, 1), (pairs,), 0, 1 << 20) % (slack + 1)
    tallies = tallies.at[1:1 + 2 * pairs:2].set(source_of - shifted).at[2:2 + 2 * pairs:2].set(taker + shifted)
    return tallies[jax.random.permutation(jax.random.fold_in(stream_key, 2), number_of)]


def noise(key, dims, deviation, limit, split=(), kind=jnp.bfloat16):
    result = jax.random.normal(key, dims, jnp.float32) * deviation
    if len(split) > 0:
        result = block_scale(key, dims, split, -0.22, 0.18) * result
    return jnp.clip(result, min=-limit, max=limit).astype(kind)


def setup_inputs(seed: int = 0) -> dict:
    keys = jax.random.split(jax.random.key(seed), 6)
    return {
        "frames": noise(keys[0], (BATCH, FRAMES, HT, WT, C), 1.0, 6.0, ((0, 32), (1, 8))),
        "clip_ids": jax.vmap(lambda own: jnp.searchsorted(jnp.cumsum(ragged_sizes(own, N_SEQ + 1, FRAMES, 2 * F_DEV + 4, 1)), jnp.arange(FRAMES), side="right"))(jax.random.split(keys[1], BATCH)).reshape((BATCH, FRAMES)).astype(jnp.int32),
        "cotangent": noise(keys[2], (BATCH, FRAMES, HT, WT, C), 1.0, 6.0, ((0, 32), (1, 8))),
        "conv1_weight": noise(keys[3], (27 * C, C), (27 * C) ** -0.5, 0.109375),
        "conv2_weight": noise(keys[4], (27 * C, C), (27 * C) ** -0.5, 0.109375),
    }


def patches(frame_block):
    height, width_cells = (frame_block.shape[1], frame_block.shape[2])
    padded = jnp.pad(frame_block, ((0, 0), (1, 1), (1, 1), (0, 0)))
    pieces = [padded[:, row_off:row_off + height, col_off:col_off + width_cells, :] for row_off in range(3) for col_off in range(3)]
    merged = jnp.concatenate(pieces, axis=-1)
    return merged.reshape(-1, merged.shape[-1])

def back_patches(frame_block):
    height, width_cells = (frame_block.shape[1], frame_block.shape[2])
    padded = jnp.pad(frame_block, ((0, 0), (1, 1), (1, 1), (0, 0)))
    pieces = [padded[:, 2 - row_off:2 - row_off + height, 2 - col_off:2 - col_off + width_cells, :] for row_off in range(3) for col_off in range(3)]
    merged = jnp.concatenate(pieces, axis=-1)
    return merged.reshape(-1, merged.shape[-1])

def tap_mask(clip_list):
    length = clip_list.shape[0] - 2
    current = clip_list[2:]
    first_tap = clip_list[0:length] == current
    second_tap = clip_list[1:length + 1] == current
    return jnp.stack([first_tap, second_tap, jnp.ones_like(first_tap)], axis=1)

def causal_conv(window, usable_taps, weight):
    length = window.shape[0] - 2
    channels = window.shape[-1]
    summed = jnp.zeros((length,) + window.shape[1:], jnp.float32)
    for offset in range(3):
        patch_rows = patches(window[offset:offset + length])
        block_weight = weight[offset * 9 * channels:(offset + 1) * 9 * channels]
        contrib = jnp.dot(patch_rows, block_weight, preferred_element_type=jnp.float32).reshape(summed.shape)
        summed = summed + jnp.where(usable_taps[:, offset][:, None, None, None], contrib, jnp.float32(0.0))
    return summed

def causal_conv_grad(window, upstream, usable_taps, weight):
    length = upstream.shape[0]
    channels = upstream.shape[-1]
    window_grad = jnp.zeros(window.shape, jnp.float32)
    tap_grads = []
    for offset in range(3):
        masked_grad = jnp.where(usable_taps[:, offset][:, None, None, None], upstream, jnp.zeros_like(upstream))
        patch_rows = patches(window[offset:offset + length])
        tap_grads.append(lax.dot_general(patch_rows, masked_grad.reshape(-1, channels), (((0,), (0,)), ((), ())), preferred_element_type=jnp.float32))
        block_weight = weight[offset * 9 * channels:(offset + 1) * 9 * channels]
        flipped = block_weight.reshape(3, 3, channels, channels).transpose(0, 1, 3, 2).reshape(9 * channels, channels)
        contrib = jnp.dot(back_patches(masked_grad), flipped, preferred_element_type=jnp.float32).reshape(upstream.shape)
        window_grad = window_grad.at[offset:offset + length].add(contrib)
    return (window_grad, jnp.concatenate(tap_grads, axis=0))

def norm_silu(activation):
    length, height, width_cells, channels = activation.shape
    grouped = activation.reshape(length, height * width_cells, GROUPS, channels // GROUPS)
    center = lax.optimization_barrier(jnp.mean(grouped, axis=(1, 3), keepdims=True))
    spread = lax.optimization_barrier(jnp.mean((grouped - center) * (grouped - center), axis=(1, 3), keepdims=True))
    normed = (grouped - center) * lax.rsqrt(spread + 1e-06)
    return jax.nn.silu(normed).reshape(activation.shape)

def reference(frames, clip_ids, cotangent, conv1_weight, conv2_weight):
    edge = jnp.zeros((2,) + frames.shape[2:], jnp.bfloat16)

    def per_batch(batch_inputs):
        local_frames, clip_list, upstream = batch_inputs
        usable_taps = tap_mask(jnp.concatenate([jnp.full((2,), -1, jnp.int32), clip_list.astype(jnp.int32)]))
        window = jnp.concatenate([edge, local_frames], axis=0)
        activation = causal_conv(window, usable_taps, conv1_weight)
        hidden = norm_silu(activation).astype(jnp.bfloat16)
        hidden_window = jnp.concatenate([edge, hidden], axis=0)
        block_out = (local_frames.astype(jnp.float32) + causal_conv(hidden_window, usable_taps, conv2_weight)).astype(jnp.bfloat16)
        hidden_grad_window, second_grad = causal_conv_grad(hidden_window, upstream, usable_taps, conv2_weight)
        unused, pullback = jax.vjp(norm_silu, activation)
        act_grad = pullback(hidden_grad_window[2:])[0].astype(jnp.bfloat16)
        input_grad_window, first_grad = causal_conv_grad(window, act_grad, usable_taps, conv1_weight)
        input_grad = (upstream.astype(jnp.float32) + input_grad_window[2:]).astype(jnp.bfloat16)
        return (block_out, input_grad, first_grad, second_grad)
    results = lax.map(per_batch, (frames, clip_ids, cotangent))
    grad_scale = jnp.float32(1.0) / jnp.sqrt(jnp.float32(frames.shape[0] * frames.shape[1] * frames.shape[2] * frames.shape[3]))
    conv1_grad = lax.optimization_barrier(jnp.sum(results[2], axis=0)) * grad_scale
    conv2_grad = lax.optimization_barrier(jnp.sum(results[3], axis=0)) * grad_scale
    return (results[0], results[1], conv1_grad, conv2_grad)
```

```python
import functools

import jax
import jax.numpy as jnp
from jax import lax
from jax.sharding import PartitionSpec as P

GROUPS = 32


def shifted(value, axis, steps):
    count = lax.axis_size(axis)
    first, last = (max(0, -steps), min(count, count - steps))
    return lax.ppermute(value, axis, [(source, source + steps) for source in range(first, last)])


def patches(frame_block):
    height, width_cells = (frame_block.shape[1], frame_block.shape[2])
    padded = jnp.pad(frame_block, ((0, 0), (1, 1), (1, 1), (0, 0)))
    pieces = [
        padded[:, row_off : row_off + height, col_off : col_off + width_cells, :]
        for row_off in range(3)
        for col_off in range(3)
    ]
    merged = jnp.concatenate(pieces, axis=-1)
    return merged.reshape(-1, merged.shape[-1])


def back_patches(frame_block):
    height, width_cells = (frame_block.shape[1], frame_block.shape[2])
    padded = jnp.pad(frame_block, ((0, 0), (1, 1), (1, 1), (0, 0)))
    pieces = [
        padded[:, 2 - row_off : 2 - row_off + height, 2 - col_off : 2 - col_off + width_cells, :]
        for row_off in range(3)
        for col_off in range(3)
    ]
    merged = jnp.concatenate(pieces, axis=-1)
    return merged.reshape(-1, merged.shape[-1])


def tap_mask(clip_list):
    length = clip_list.shape[0] - 2
    current = clip_list[2:]
    first_tap = clip_list[0:length] == current
    second_tap = clip_list[1 : length + 1] == current
    return jnp.stack([first_tap, second_tap, jnp.ones_like(first_tap)], axis=1)


def causal_conv(window, usable_taps, weight):
    length = window.shape[0] - 2
    channels = window.shape[-1]
    summed = jnp.zeros((length,) + window.shape[1:], jnp.float32)
    for offset in range(3):
        patch_rows = patches(window[offset : offset + length])
        block_weight = weight[offset * 9 * channels : (offset + 1) * 9 * channels]
        contrib = jnp.dot(patch_rows, block_weight, preferred_element_type=jnp.float32).reshape(
            summed.shape
        )
        summed = summed + jnp.where(
            usable_taps[:, offset][:, None, None, None], contrib, jnp.float32(0.0)
        )
    return summed


def causal_conv_grad(window, upstream, usable_taps, weight):
    length = upstream.shape[0]
    channels = upstream.shape[-1]
    window_grad = jnp.zeros(window.shape, jnp.float32)
    tap_grads = []
    for offset in range(3):
        masked_grad = jnp.where(
            usable_taps[:, offset][:, None, None, None], upstream, jnp.zeros_like(upstream)
        )
        patch_rows = patches(window[offset : offset + length])
        tap_grads.append(
            lax.dot_general(
                patch_rows,
                masked_grad.reshape(-1, channels),
                (((0,), (0,)), ((), ())),
                preferred_element_type=jnp.float32,
            )
        )
        block_weight = weight[offset * 9 * channels : (offset + 1) * 9 * channels]
        flipped = (
            block_weight.reshape(3, 3, channels, channels)
            .transpose(0, 1, 3, 2)
            .reshape(9 * channels, channels)
        )
        contrib = jnp.dot(
            back_patches(masked_grad), flipped, preferred_element_type=jnp.float32
        ).reshape(upstream.shape)
        window_grad = window_grad.at[offset : offset + length].add(contrib)
    return (window_grad, jnp.concatenate(tap_grads, axis=0))


def norm_silu(activation):
    length, height, width_cells, channels = activation.shape
    grouped = activation.reshape(length, height * width_cells, GROUPS, channels // GROUPS)
    center = jnp.mean(grouped, axis=(1, 3), keepdims=True)
    spread = jnp.mean((grouped - center) * (grouped - center), axis=(1, 3), keepdims=True)
    normed = (grouped - center) * lax.rsqrt(spread + 1e-06)
    return jax.nn.silu(normed).reshape(activation.shape)


def dp_permute(value, target):
    return lax.ppermute(value, "dp", [(source, target(source)) for source in range(32)])


def scatter_sum(blocks, axis, own, target):
    total = lax.dynamic_index_in_dim(blocks, own, axis, keepdims=False)
    for step in range(1, 4):
        sent = lax.dynamic_index_in_dim(blocks, (own + step) % 4, axis, keepdims=False)
        total = total + dp_permute(sent.astype(jnp.bfloat16), functools.partial(target, step)).astype(
            jnp.float32
        )
    return total


def reduce_rows(partial):
    index = lax.axis_index("dp")
    core, x, y = index % 2, (index // 2) % 4, index // 8
    blocks = partial.reshape(4, 4, 2, 108, 128)
    kept = lax.dynamic_index_in_dim(blocks, core, 2, keepdims=False)
    sent = lax.dynamic_index_in_dim(blocks, 1 - core, 2, keepdims=False)
    kept = kept + dp_permute(sent.astype(jnp.bfloat16), lambda d: d ^ 1).astype(jnp.float32)
    kept = scatter_sum(kept, 1, x, lambda step, d: (d // 8) * 8 + (d % 8 + 2 * step) % 8)
    kept = scatter_sum(kept, 0, y, lambda step, d: (d + 8 * step) % 32)
    near = [
        lax.ppermute(kept, "seq", [(z, (z // 4) * 4 + (z + step) % 4) for z in range(8)])
        for step in (1, 2, 3)
    ]
    kept = (kept + near[1]) + (near[0] + near[2])
    return kept + lax.ppermute(kept, "seq", [(z, z ^ 4) for z in range(8)])


def onto_tail(returned, frame_count):
    leading = jnp.zeros((frame_count - 2,) + returned.shape[1:], jnp.float32)
    return jnp.concatenate([leading, returned], axis=0)


def per_device(frames, clip_ids, cotangent, conv1_weight, conv2_weight):
    local_frames = frames[0]
    upstream = cotangent[0]
    frame_count = local_frames.shape[0]
    first_frame = lax.axis_index("seq") * frame_count
    padded_clips = jnp.concatenate([jnp.full((4,), -1, jnp.int32), clip_ids[0]])
    cache_frames = shifted(local_frames[-2:], "seq", 1)
    window = jnp.concatenate([cache_frames, local_frames], axis=0)
    clip_list = lax.dynamic_slice_in_dim(padded_clips, first_frame + 2, frame_count + 2)
    usable_taps = tap_mask(clip_list)
    activation = causal_conv(window, usable_taps, conv1_weight)
    hidden = norm_silu(activation).astype(jnp.bfloat16)
    hidden_cache = shifted(hidden[-2:], "seq", 1)
    hidden_window = jnp.concatenate([hidden_cache, hidden], axis=0)
    block_out = (
        local_frames.astype(jnp.float32) + causal_conv(hidden_window, usable_taps, conv2_weight)
    ).astype(jnp.bfloat16)
    hidden_grad_window, second_grad = causal_conv_grad(
        hidden_window, upstream, usable_taps, conv2_weight
    )
    hidden_back = shifted(hidden_grad_window[:2].astype(jnp.bfloat16), "seq", -1).astype(
        jnp.float32
    )
    hidden_grad = hidden_grad_window[2:] + onto_tail(hidden_back, frame_count)
    unused, pullback = jax.vjp(norm_silu, activation)
    act_grad = pullback(hidden_grad)[0].astype(jnp.bfloat16)
    input_grad_window, first_grad = causal_conv_grad(window, act_grad, usable_taps, conv1_weight)
    returned = shifted(input_grad_window[:2].astype(jnp.bfloat16), "seq", -1).astype(jnp.float32)
    input_grad = (
        upstream.astype(jnp.float32) + input_grad_window[2:] + onto_tail(returned, frame_count)
    ).astype(jnp.bfloat16)
    total_rows = (
        lax.axis_size("dp")
        * lax.axis_size("seq")
        * frame_count
        * local_frames.shape[1]
        * local_frames.shape[2]
    )
    grad_scale = jnp.float32(1.0) / jnp.sqrt(jnp.float32(total_rows))
    summed_first, summed_second = (reduce_rows(first_grad), reduce_rows(second_grad))
    return (
        block_out[None],
        input_grad[None],
        summed_first * grad_scale,
        summed_second * grad_scale,
    )


def solution(mesh):
    return jax.shard_map(
        per_device,
        mesh=mesh,
        in_specs=(
            P("dp", "seq", None, None, None),
            P("dp", None),
            P("dp", "seq", None, None, None),
            P(),
            P(),
        ),
        out_specs=(
            P("dp", "seq", None, None, None),
            P("dp", "seq", None, None, None),
            P("dp", None),
            P("dp", None),
        ),
        check_vma=False,
    )
```

```python
import functools

import jax
import jax.numpy as jnp
from jax import lax
from jax.experimental import pallas as pl
from jax.experimental.pallas import tpu as pltpu
from jax.sharding import PartitionSpec as P

C = 128
GROUP = 4
F = 8
HT = 8
WT = 32
POS = HT * WT
NONE = F + 2
BF16 = jnp.bfloat16
F32 = jnp.float32
VMEM_LIMIT = 56 * 1024 * 1024


def column(rows):
    return lax.broadcasted_iota(jnp.int32, (rows, C), 0) % WT


def shift_down(value):
    return jnp.where(column(POS) == 0, 0.0, pltpu.roll(value, 1, 0))


def shift_up(value):
    return jnp.where(column(POS) == WT - 1, 0.0, pltpu.roll(value, POS - 1, 0))


def row_pieces(frame):
    edge = jnp.zeros((WT, C), frame.dtype)
    return [
        jnp.concatenate([edge, frame[: POS - WT]], axis=0),
        frame,
        jnp.concatenate([frame[WT:], edge], axis=0),
    ]


def conv_frame(window, slots, weight):
    pieces = []
    for slot in slots:
        pieces += row_pieces(window[slot])
    taps = jnp.dot(jnp.concatenate(pieces, axis=1), weight[...], preferred_element_type=F32)
    return shift_down(taps[:, :C]) + taps[:, C : 2 * C] + shift_up(taps[:, 2 * C :])


def forward_weight(weight_ref, out_ref):
    for outer in range(9):
        for b in range(3):
            out_ref[outer * C : (outer + 1) * C, b * C : (b + 1) * C] = weight_ref[
                (outer * 3 + b) * C : (outer * 3 + b + 1) * C, :
            ]


def adjoint_weight(weight_ref, out_ref):
    for outer in range(9):
        for b in range(3):
            tap = 26 - (outer * 3 + b)
            out_ref[outer * C : (outer + 1) * C, b * C : (b + 1) * C] = weight_ref[
                tap * C : (tap + 1) * C, :
            ].T


def group_mean(sums):
    lane = lax.broadcasted_iota(jnp.int32, sums.shape, 1)
    pairs = sums + jnp.where(lane % 2 == 0, pltpu.roll(sums, C - 1, 1), pltpu.roll(sums, 1, 1))
    quads = pairs + jnp.where(lane % 4 < 2, pltpu.roll(pairs, C - 2, 1), pltpu.roll(pairs, 2, 1))
    return quads * (1.0 / (GROUP * POS))


def main_kernel(
    core_ref,
    past_ref,
    next_ref,
    frames_ref,
    cache_ref,
    cot_ref,
    cot_next_ref,
    weight1_ref,
    weight2_ref,
    hidden_ref,
    act_grad_ref,
    keep_ref,
    send_ref,
    window,
    cot_window,
    conv_weight,
    back_weight,
    act,
    slope,
    cot_shifted,
    cot_taps,
    frame_t,
    frame_taps,
    hidden_t,
    grad_shifted,
    grads,
):
    zero = jnp.zeros((POS, C), BF16)
    for f in range(2):
        window[f] = cache_ref[f]
        cot_window[F + f] = cot_next_ref[f]
    for f in range(F):
        window[2 + f] = frames_ref[f]
        cot_window[f] = cot_ref[f]
    window[NONE] = zero
    cot_window[NONE] = zero
    forward_weight(weight1_ref, conv_weight)
    adjoint_weight(weight2_ref, back_weight)

    sums = []
    for t in range(F):
        out = conv_frame(window, [past_ref[t, k] for k in range(3)], conv_weight)
        act[t] = out
        sums.append(jnp.sum(out, axis=0, keepdims=True))
    center = group_mean(jnp.concatenate(sums, axis=0))
    sums = []
    for t in range(F):
        away = act[t] - center[t : t + 1]
        sums.append(jnp.sum(away * away, axis=0, keepdims=True))
    scale = lax.rsqrt(group_mean(jnp.concatenate(sums, axis=0)) + 1e-06)
    for t in range(F):
        normed = (act[t] - center[t : t + 1]) * scale[t : t + 1]
        gate = 1.0 / (1.0 + jnp.exp(-normed))
        hidden = (normed * gate).astype(BF16)
        hidden_ref[t] = hidden
        act[t] = normed
        slope[t] = gate * (1.0 + normed * (1.0 - gate))
        for a, piece in enumerate(row_pieces(hidden)):
            hidden_t[a * C : (a + 1) * C, t * POS : (t + 1) * POS] = piece.T

    first, second = [], []
    for t in range(F):
        grad = conv_frame(cot_window, [next_ref[t, q] for q in range(3)], back_weight) * slope[t]
        slope[t] = grad
        first.append(jnp.sum(grad, axis=0, keepdims=True))
        second.append(jnp.sum(grad * act[t], axis=0, keepdims=True))
    first = group_mean(jnp.concatenate(first, axis=0))
    second = group_mean(jnp.concatenate(second, axis=0))
    for t in range(F):
        grad = scale[t : t + 1] * (slope[t] - first[t : t + 1] - act[t] * second[t : t + 1])
        rounded = grad.astype(BF16)
        act_grad_ref[t] = rounded
        wide = rounded.astype(F32)
        grad_shifted[t * POS : (t + 1) * POS, :C] = shift_up(wide).astype(BF16)
        grad_shifted[t * POS : (t + 1) * POS, C : 2 * C] = rounded
        grad_shifted[t * POS : (t + 1) * POS, 2 * C :] = shift_down(wide).astype(BF16)

    for f in range(F + 2):
        wide = cot_window[f].astype(F32)
        cot_shifted[f, :, :C] = shift_up(wide).astype(BF16)
        cot_shifted[f, :, C : 2 * C] = cot_window[f]
        cot_shifted[f, :, 2 * C :] = shift_down(wide).astype(BF16)
    cot_shifted[NONE] = jnp.zeros((POS, 3 * C), BF16)
    for s in range(F):
        for k in range(3):
            cot_taps[s * POS : (s + 1) * POS, 3 * C * k : 3 * C * (k + 1)] = cot_shifted[
                next_ref[s, 2 - k]
            ]
    second_grad = jnp.dot(hidden_t[...], cot_taps[...], preferred_element_type=F32)
    for k in range(3):
        for a in range(3):
            for b in range(3):
                tap = (k * 3 + a) * 3 + b
                grads[1, tap * C : (tap + 1) * C] = second_grad[
                    a * C : (a + 1) * C, (k * 3 + b) * C : (k * 3 + b + 1) * C
                ]

    for f in range(F + 2):
        for a, piece in enumerate(row_pieces(window[f])):
            frame_t[f, a * C : (a + 1) * C, :] = piece.T
    frame_t[NONE] = jnp.zeros((3 * C, POS), BF16)
    for t in range(F):
        for k in range(3):
            frame_taps[3 * C * k : 3 * C * (k + 1), t * POS : (t + 1) * POS] = frame_t[
                past_ref[t, k]
            ]
    first_grad = jnp.dot(frame_taps[...], grad_shifted[...], preferred_element_type=F32)
    for outer in range(9):
        for b in range(3):
            tap = outer * 3 + b
            grads[0, tap * C : (tap + 1) * C] = first_grad[
                outer * C : (outer + 1) * C, b * C : (b + 1) * C
            ]

    own = core_ref[0] == 0
    for g in range(2):
        for m in range(16):
            low = grads[g, 216 * m : 216 * m + 108]
            high = grads[g, 216 * m + 108 : 216 * m + 216]
            keep_ref[g, m] = jnp.where(own, low, high)
            send_ref[g, m] = jnp.where(own, high, low).astype(BF16)


def conv_kernel(adjoint, slot_ref, frames_ref, cache_ref, weight_ref, base_ref, out_ref, window, weight):
    for f in range(2):
        window[F + f if adjoint else f] = cache_ref[f]
    for f in range(F):
        window[f if adjoint else 2 + f] = frames_ref[f]
    window[NONE] = jnp.zeros((POS, C), BF16)
    (adjoint_weight if adjoint else forward_weight)(weight_ref, weight)
    for t in range(F):
        out = conv_frame(window, [slot_ref[t, k] for k in range(3)], weight)
        out_ref[t] = (base_ref[t].astype(F32) + out).astype(BF16)


def add_kernel(own_ref, keep_ref, *refs):
    received, (kept_ref, *sent_refs) = refs[:-4], refs[-4:]
    own = own_ref[0]
    outer = keep_ref.shape[1]
    for g in range(2):
        for m in range(outer):
            for step in range(4):
                block = lax.rem(own + step, 4)
                total = keep_ref[g, m, block]
                for part in received:
                    total = total + part[g, m, block].astype(F32)
                if step == 0:
                    kept_ref[g, m] = total
                else:
                    sent_refs[step - 1][g, m] = total.astype(BF16)


SMEM = pl.BlockSpec(memory_space=pltpu.SMEM)
VMEM = pl.BlockSpec(memory_space=pltpu.VMEM)


def call(kernel, operands, scalars, outs, scratch=(), flops=0, moved=0):
    return pl.pallas_call(
        kernel,
        out_shape=[jax.ShapeDtypeStruct(shape, dtype) for shape, dtype in outs],
        in_specs=[SMEM] * scalars + [VMEM] * (len(operands) - scalars),
        out_specs=[VMEM] * len(outs),
        scratch_shapes=[pltpu.VMEM(shape, dtype) for shape, dtype in scratch],
        compiler_params=pltpu.CompilerParams(vmem_limit_bytes=VMEM_LIMIT),
        cost_estimate=pl.CostEstimate(flops=flops, bytes_accessed=moved, transcendentals=0),
    )(*operands)


CONV_FLOPS = 2 * F * POS * 27 * C * C


def main(core, past, following, frames, cache, cot, cot_next, weight1, weight2):
    return call(
        main_kernel,
        (core, past, following, frames, cache, cot, cot_next, weight1, weight2),
        3,
        [
            ((F, POS, C), BF16),
            ((F, POS, C), BF16),
            ((2, 16, 108, C), F32),
            ((2, 16, 108, C), BF16),
        ],
        [
            ((F + 3, POS, C), BF16),
            ((F + 3, POS, C), BF16),
            ((9 * C, 3 * C), BF16),
            ((9 * C, 3 * C), BF16),
            ((F, POS, C), F32),
            ((F, POS, C), F32),
            ((F + 3, POS, 3 * C), BF16),
            ((F * POS, 9 * C), BF16),
            ((F + 3, 3 * C, POS), BF16),
            ((9 * C, F * POS), BF16),
            ((3 * C, F * POS), BF16),
            ((F * POS, 3 * C), BF16),
            ((2, 27 * C, C), F32),
        ],
        flops=4 * CONV_FLOPS,
        moved=9 << 20,
    )


def conv(adjoint, slots, frames, cache, weight, base):
    return call(
        functools.partial(conv_kernel, adjoint),
        (slots, frames, cache, weight, base),
        1,
        [((F, POS, C), BF16)],
        [((F + 3, POS, C), BF16), ((9 * C, 3 * C), BF16)],
        flops=CONV_FLOPS,
        moved=3 << 20,
    )[0]


def add_stage(own, keep, received, outer):
    return call(
        add_kernel,
        (own, keep, *received),
        1,
        [((2, outer, 108, C), F32)] + [((2, outer, 108, C), BF16)] * 3,
        flops=0,
        moved=2 << 20,
    )


def shifted(value, steps):
    count = lax.axis_size("seq")
    first, last = (max(0, -steps), min(count, count - steps))
    return lax.ppermute(value, "seq", [(source, source + steps) for source in range(first, last)])


def dp_permute(value, target):
    return lax.ppermute(value, "dp", [(source, target(source)) for source in range(32)])


def slot_tables(clips, first_frame):
    padded = jnp.concatenate(
        [jnp.full((2,), -1, jnp.int32), clips, jnp.full((2,), -1, jnp.int32)]
    )
    near = lax.dynamic_slice_in_dim(padded, first_frame, F + 4)
    frame = jnp.arange(F, dtype=jnp.int32)
    current = near[2 : 2 + F]
    past = jnp.stack(
        [jnp.where(near[k : k + F] == current, frame + k, NONE) for k in range(3)], axis=1
    )
    following = jnp.stack(
        [jnp.where(near[2 + q : 2 + q + F] == current, frame + q, NONE) for q in range(3)], axis=1
    )
    return past, following


def per_device(frames, clip_ids, cotangent, conv1_weight, conv2_weight):
    own_frames = frames.reshape(F, POS, C)
    own_cot = cotangent.reshape(F, POS, C)
    index = lax.axis_index("dp")
    core, x, y = index % 2, (index // 2) % 4, index // 8
    past, following = slot_tables(clip_ids[0], lax.axis_index("seq") * F)
    cache = shifted(own_frames[F - 2 :], 1)
    cot_next = shifted(own_cot[:2], -1)
    hidden, act_grad, keep, send = main(
        core[None], past, following, own_frames, cache, own_cot, cot_next, conv1_weight, conv2_weight
    )
    hidden_cache = shifted(hidden[F - 2 :], 1)
    act_grad_next = shifted(act_grad[:2], -1)
    recv = dp_permute(send, lambda d: d ^ 1)
    block_out = conv(False, past, hidden, hidden_cache, conv2_weight, own_frames)
    input_grad = conv(True, following, act_grad, act_grad_next, conv1_weight, own_cot)

    keep, *sent = add_stage(
        x[None], keep.reshape(2, 4, 4, 108, C), [recv.reshape(2, 4, 4, 108, C)], 4
    )
    recv = [
        dp_permute(part, lambda d, s=s: (d // 8) * 8 + (d % 8 + 2 * s) % 8)
        for s, part in zip((1, 2, 3), sent)
    ]
    keep, *sent = add_stage(
        y[None], keep.reshape(2, 1, 4, 108, C), [part.reshape(2, 1, 4, 108, C) for part in recv], 1
    )
    recv = [dp_permute(part, lambda d, s=s: (d + 8 * s) % 32) for s, part in zip((1, 2, 3), sent)]
    total = keep + recv[0].astype(F32) + recv[1].astype(F32) + recv[2].astype(F32)
    near = [
        lax.ppermute(total, "seq", [(z, (z // 4) * 4 + (z + s) % 4) for z in range(8)])
        for s in (1, 2, 3)
    ]
    total = (total + near[1]) + (near[0] + near[2])
    total = total + lax.ppermute(total, "seq", [(z, z ^ 4) for z in range(8)])
    rows = lax.axis_size("dp") * lax.axis_size("seq") * F * POS
    total = total.reshape(2, 108, C) * (F32(1.0) / jnp.sqrt(F32(rows)))
    return (
        block_out.reshape(frames.shape),
        input_grad.reshape(frames.shape),
        total[0],
        total[1],
    )


def solution(mesh):
    return jax.shard_map(
        per_device,
        mesh=mesh,
        in_specs=(
            P("dp", "seq", None, None, None),
            P("dp", None),
            P("dp", "seq", None, None, None),
            P(),
            P(),
        ),
        out_specs=(
            P("dp", "seq", None, None, None),
            P("dp", "seq", None, None, None),
            P("dp", None),
            P("dp", None),
        ),
        check_vma=False,
    )
```

```python
import functools

import jax
import jax.numpy as jnp
from jax import lax
from jax.experimental import pallas as pl
from jax.experimental.pallas import tpu as pltpu
from jax.sharding import PartitionSpec as P

C = 128
GROUP = 4
F = 8
HT = 8
WT = 32
POS = HT * WT
NONE = F + 2
BF16 = jnp.bfloat16
F32 = jnp.float32
BLOCK = 108
PADDED = 112


def past_slots(clips, first, t):
    slots = []
    for k in range(3):
        frame = first + t + k - 2
        same = clips[0, jnp.maximum(frame, 0)] == clips[0, first + t]
        slots.append(jnp.where(same & (frame >= 0), t + k, NONE))
    return slots


def next_slots(clips, first, t):
    last = clips.shape[1] - 1
    slots = []
    for q in range(3):
        frame = first + t + q
        same = clips[0, jnp.minimum(frame, last)] == clips[0, first + t]
        slots.append(jnp.where(same & (frame <= last), t + q, NONE))
    return slots


def column(rows):
    return lax.broadcasted_iota(jnp.int32, (rows, C), 0) % WT


def shift_down(value):
    return jnp.where(column(POS) == 0, 0.0, pltpu.roll(value, 1, 0))


def shift_up(value):
    return jnp.where(column(POS) == WT - 1, 0.0, pltpu.roll(value, POS - 1, 0))


def row_pieces(frame):
    edge = jnp.zeros((WT, C), frame.dtype)
    return [
        jnp.concatenate([edge, frame[: POS - WT]], axis=0),
        frame,
        jnp.concatenate([frame[WT:], edge], axis=0),
    ]


def conv_frame(window, slots, weight):
    pieces = []
    for slot in slots:
        pieces += row_pieces(window[slot])
    taps = jnp.dot(jnp.concatenate(pieces, axis=1), weight[...], preferred_element_type=F32)
    return shift_down(taps[:, :C]) + taps[:, C : 2 * C] + shift_up(taps[:, 2 * C :])


def forward_weight(weight_ref, out_ref):
    for outer in range(9):
        for b in range(3):
            out_ref[outer * C : (outer + 1) * C, b * C : (b + 1) * C] = weight_ref[
                (outer * 3 + b) * C : (outer * 3 + b + 1) * C, :
            ]


def adjoint_weight(weight_ref, out_ref):
    for outer in range(9):
        for b in range(3):
            tap = 26 - (outer * 3 + b)
            out_ref[outer * C : (outer + 1) * C, b * C : (b + 1) * C] = weight_ref[
                tap * C : (tap + 1) * C, :
            ].T


def group_mean(sums):
    lane = lax.broadcasted_iota(jnp.int32, sums.shape, 1)
    pairs = sums + jnp.where(lane % 2 == 0, pltpu.roll(sums, C - 1, 1), pltpu.roll(sums, 1, 1))
    quads = pairs + jnp.where(lane % 4 < 2, pltpu.roll(pairs, C - 2, 1), pltpu.roll(pairs, 2, 1))
    return quads * (1.0 / (GROUP * POS))


def main_kernel(
    clips,
    frames_ref,
    cache_ref,
    cot_ref,
    cot_next_ref,
    weight1_ref,
    weight2_ref,
    hidden_ref,
    act_grad_ref,
    hidden_tail_ref,
    act_grad_head_ref,
    keep_ref,
    send_ref,
    window,
    cot_window,
    conv_weight,
    back_weight,
    act,
    slope,
    cot_shifted,
    cot_taps,
    frame_t,
    frame_taps,
    hidden_t,
    grad_shifted,
    grads,
):
    first_frame = lax.axis_index("seq") * F
    past = [past_slots(clips, first_frame, t) for t in range(F)]
    following = [next_slots(clips, first_frame, t) for t in range(F)]
    zero = jnp.zeros((POS, C), BF16)
    for f in range(2):
        window[f] = cache_ref[f]
        cot_window[F + f] = cot_next_ref[f]
    for f in range(F):
        window[2 + f] = frames_ref[f]
        cot_window[f] = cot_ref[f]
    window[NONE] = zero
    cot_window[NONE] = zero
    forward_weight(weight1_ref, conv_weight)
    adjoint_weight(weight2_ref, back_weight)

    sums = []
    for t in range(F):
        out = conv_frame(window, past[t], conv_weight)
        act[t] = out
        sums.append(jnp.sum(out, axis=0, keepdims=True))
    center = group_mean(jnp.concatenate(sums, axis=0))
    sums = []
    for t in range(F):
        away = act[t] - center[t : t + 1]
        sums.append(jnp.sum(away * away, axis=0, keepdims=True))
    scale = lax.rsqrt(group_mean(jnp.concatenate(sums, axis=0)) + 1e-06)
    for t in range(F):
        normed = (act[t] - center[t : t + 1]) * scale[t : t + 1]
        gate = 1.0 / (1.0 + jnp.exp(-normed))
        hidden = (normed * gate).astype(BF16)
        hidden_ref[t] = hidden
        if t >= F - 2:
            hidden_tail_ref[t - F + 2] = hidden
        act[t] = normed
        slope[t] = gate * (1.0 + normed * (1.0 - gate))
        for a, piece in enumerate(row_pieces(hidden)):
            hidden_t[a * C : (a + 1) * C, t * POS : (t + 1) * POS] = piece.T

    first, second = [], []
    for t in range(F):
        grad = conv_frame(cot_window, following[t], back_weight) * slope[t]
        slope[t] = grad
        first.append(jnp.sum(grad, axis=0, keepdims=True))
        second.append(jnp.sum(grad * act[t], axis=0, keepdims=True))
    first = group_mean(jnp.concatenate(first, axis=0))
    second = group_mean(jnp.concatenate(second, axis=0))
    for t in range(F):
        grad = scale[t : t + 1] * (slope[t] - first[t : t + 1] - act[t] * second[t : t + 1])
        rounded = grad.astype(BF16)
        act_grad_ref[t] = rounded
        if t < 2:
            act_grad_head_ref[t] = rounded
        wide = rounded.astype(F32)
        grad_shifted[t * POS : (t + 1) * POS, :C] = shift_up(wide).astype(BF16)
        grad_shifted[t * POS : (t + 1) * POS, C : 2 * C] = rounded
        grad_shifted[t * POS : (t + 1) * POS, 2 * C :] = shift_down(wide).astype(BF16)

    for f in range(F + 2):
        wide = cot_window[f].astype(F32)
        cot_shifted[f, :, :C] = shift_up(wide).astype(BF16)
        cot_shifted[f, :, C : 2 * C] = cot_window[f]
        cot_shifted[f, :, 2 * C :] = shift_down(wide).astype(BF16)
    cot_shifted[NONE] = jnp.zeros((POS, 3 * C), BF16)
    for s in range(F):
        for k in range(3):
            cot_taps[s * POS : (s + 1) * POS, 3 * C * k : 3 * C * (k + 1)] = cot_shifted[
                following[s][2 - k]
            ]
    second_grad = jnp.dot(hidden_t[...], cot_taps[...], preferred_element_type=F32)
    for k in range(3):
        for a in range(3):
            for b in range(3):
                tap = (k * 3 + a) * 3 + b
                grads[1, tap * C : (tap + 1) * C] = second_grad[
                    a * C : (a + 1) * C, (k * 3 + b) * C : (k * 3 + b + 1) * C
                ]

    for f in range(F + 2):
        for a, piece in enumerate(row_pieces(window[f])):
            frame_t[f, a * C : (a + 1) * C, :] = piece.T
    frame_t[NONE] = jnp.zeros((3 * C, POS), BF16)
    for t in range(F):
        for k in range(3):
            frame_taps[3 * C * k : 3 * C * (k + 1), t * POS : (t + 1) * POS] = frame_t[
                past[t][k]
            ]
    first_grad = jnp.dot(frame_taps[...], grad_shifted[...], preferred_element_type=F32)
    for outer in range(9):
        for b in range(3):
            tap = outer * 3 + b
            grads[0, tap * C : (tap + 1) * C] = first_grad[
                outer * C : (outer + 1) * C, b * C : (b + 1) * C
            ]

    own = lax.rem(lax.axis_index("dp"), 2) == 0
    for g in range(2):
        for m in range(16):
            low = grads[g, 2 * BLOCK * m : 2 * BLOCK * m + BLOCK]
            high = grads[g, 2 * BLOCK * m + BLOCK : 2 * BLOCK * (m + 1)]
            keep_ref[g, m, :BLOCK] = jnp.where(own, low, high)
            keep_ref[g, m, BLOCK:] = jnp.zeros((PADDED - BLOCK, C), F32)
            send_ref[g, m, :BLOCK] = jnp.where(own, high, low).astype(BF16)
            send_ref[g, m, BLOCK:] = jnp.zeros((PADDED - BLOCK, C), BF16)


def head_kernel(frames_ref, cot_ref, tail_ref, head_ref):
    tail_ref[...] = frames_ref[...]
    head_ref[...] = cot_ref[...]


def conv_kernel(adjoint, clips, frames_ref, cache_ref, weight_ref, base_ref, out_ref, window, weight):
    for f in range(2):
        window[F + f if adjoint else f] = cache_ref[f]
    for f in range(F):
        window[f if adjoint else 2 + f] = frames_ref[f]
    window[NONE] = jnp.zeros((POS, C), BF16)
    first_frame = lax.axis_index("seq") * F
    (adjoint_weight if adjoint else forward_weight)(weight_ref, weight)
    for t in range(F):
        slots = (next_slots if adjoint else past_slots)(clips, first_frame, t)
        out = conv_frame(window, slots, weight)
        out_ref[t] = (base_ref[t].astype(F32) + out).astype(BF16)


def add_kernel(axis, keep_ref, *refs):
    received, (kept_ref, *sent_refs) = refs[:-4], refs[-4:]
    index = lax.axis_index("dp")
    own = lax.rem(lax.div(index, 2), 4) if axis == "x" else lax.div(index, 8)
    for g in range(2):
        for m in range(keep_ref.shape[1]):
            for step in range(4):
                block = lax.rem(own + step, 4)
                total = keep_ref[g, m, block]
                for part in received:
                    total = total + part[g, m, block].astype(F32)
                if step == 0:
                    kept_ref[g, m] = total
                else:
                    sent_refs[step - 1][g, m] = total.astype(BF16)


SMEM = pl.BlockSpec(memory_space=pltpu.SMEM)
VMEM = pl.BlockSpec(memory_space=pltpu.VMEM)


def call(kernel, operands, scalars, outs, scratch=(), flops=0, moved=0, limit=16):
    return pl.pallas_call(
        kernel,
        out_shape=[jax.ShapeDtypeStruct(shape, dtype) for shape, dtype in outs],
        in_specs=[SMEM] * scalars + [VMEM] * (len(operands) - scalars),
        out_specs=[VMEM] * len(outs),
        scratch_shapes=[pltpu.VMEM(shape, dtype) for shape, dtype in scratch],
        compiler_params=pltpu.CompilerParams(vmem_limit_bytes=limit << 20),
        cost_estimate=pl.CostEstimate(flops=flops, bytes_accessed=moved, transcendentals=0),
    )(*operands)


CONV_FLOPS = 2 * F * POS * 27 * C * C


def main(clips, frames, cache, cot, cot_next, weight1, weight2):
    return call(
        main_kernel,
        (clips, frames, cache, cot, cot_next, weight1, weight2),
        1,
        [
            ((F, POS, C), BF16),
            ((F, POS, C), BF16),
            ((2, POS, C), BF16),
            ((2, POS, C), BF16),
            ((2, 16, PADDED, C), F32),
            ((2, 16, PADDED, C), BF16),
        ],
        [
            ((F + 3, POS, C), BF16),
            ((F + 3, POS, C), BF16),
            ((9 * C, 3 * C), BF16),
            ((9 * C, 3 * C), BF16),
            ((F, POS, C), F32),
            ((F, POS, C), F32),
            ((F + 3, POS, 3 * C), BF16),
            ((F * POS, 9 * C), BF16),
            ((F + 3, 3 * C, POS), BF16),
            ((9 * C, F * POS), BF16),
            ((3 * C, F * POS), BF16),
            ((F * POS, 3 * C), BF16),
            ((2, 27 * C, C), F32),
        ],
        flops=4 * CONV_FLOPS,
        moved=9 << 20,
        limit=44,
    )


def conv(adjoint, clips, frames, cache, weight, base):
    return call(
        functools.partial(conv_kernel, adjoint),
        (clips, frames, cache, weight, base),
        1,
        [((F, POS, C), BF16)],
        [((F + 3, POS, C), BF16), ((9 * C, 3 * C), BF16)],
        flops=CONV_FLOPS,
        moved=3 << 20,
    )[0]


def add_stage(axis, keep, received, outer):
    return call(
        functools.partial(add_kernel, axis),
        (keep, *received),
        0,
        [((2, outer, PADDED, C), F32)] + [((2, outer, PADDED, C), BF16)] * 3,
        moved=1 << 20,
    )


def halos(frames, cot):
    pair = (2, POS, C)
    return pl.pallas_call(
        head_kernel,
        grid=(1,),
        out_shape=[jax.ShapeDtypeStruct(pair, BF16)] * 2,
        in_specs=[pl.BlockSpec(pair, lambda i: (F // 2 - 1, 0, 0)), pl.BlockSpec(pair, lambda i: (0, 0, 0))],
        out_specs=[pl.BlockSpec(pair, lambda i: (0, 0, 0))] * 2,
        compiler_params=pltpu.CompilerParams(vmem_limit_bytes=4 << 20),
    )(frames, cot)


def shifted(value, steps):
    count = lax.axis_size("seq")
    first, last = (max(0, -steps), min(count, count - steps))
    return lax.ppermute(value, "seq", [(source, source + steps) for source in range(first, last)])


def dp_permute(value, target):
    return lax.ppermute(value, "dp", [(source, target(source)) for source in range(32)])


def per_device(frames, clip_ids, cotangent, conv1_weight, conv2_weight):
    own_frames = frames.reshape(F, POS, C)
    own_cot = cotangent.reshape(F, POS, C)
    tail, head = halos(own_frames, own_cot)
    cache = shifted(tail, 1)
    cot_next = shifted(head, -1)
    hidden, act_grad, tail, head, keep, send = main(
        clip_ids, own_frames, cache, own_cot, cot_next, conv1_weight, conv2_weight
    )
    recv = dp_permute(send, lambda d: d ^ 1)
    hidden_cache = shifted(tail, 1)
    act_grad_next = shifted(head, -1)
    keep, *sent = add_stage(
        "x", keep.reshape(2, 4, 4, PADDED, C), [recv.reshape(2, 4, 4, PADDED, C)], 4
    )
    sent, hidden, act_grad = lax.optimization_barrier((sent, hidden, act_grad))
    recv = [
        dp_permute(part, lambda d, s=s: (d // 8) * 8 + (d % 8 + 2 * s) % 8)
        for s, part in zip((1, 2, 3), sent)
    ]
    block_out = conv(False, clip_ids, hidden, hidden_cache, conv2_weight, own_frames)
    input_grad = conv(True, clip_ids, act_grad, act_grad_next, conv1_weight, own_cot)
    recv, block_out, input_grad = lax.optimization_barrier((recv, block_out, input_grad))
    keep, *sent = add_stage(
        "y",
        keep.reshape(2, 1, 4, PADDED, C),
        [part.reshape(2, 1, 4, PADDED, C) for part in recv],
        1,
    )
    recv = [dp_permute(part, lambda d, s=s: (d + 8 * s) % 32) for s, part in zip((1, 2, 3), sent)]
    total = keep + recv[0].astype(F32) + recv[1].astype(F32) + recv[2].astype(F32)
    near = [
        lax.ppermute(total, "seq", [(z, (z // 4) * 4 + (z + s) % 4) for z in range(8)])
        for s in (1, 2, 3)
    ]
    total = (total + near[1]) + (near[0] + near[2])
    total = total + lax.ppermute(total, "seq", [(z, z ^ 4) for z in range(8)])
    rows = lax.axis_size("dp") * lax.axis_size("seq") * F * POS
    total = total.reshape(2, PADDED, C)[:, :BLOCK] * (F32(1.0) / jnp.sqrt(F32(rows)))
    return (
        block_out.reshape(frames.shape),
        input_grad.reshape(frames.shape),
        total[0],
        total[1],
    )


def solution(mesh):
    return jax.shard_map(
        per_device,
        mesh=mesh,
        in_specs=(
            P("dp", "seq", None, None, None),
            P("dp", None),
            P("dp", "seq", None, None, None),
            P(),
            P(),
        ),
        out_specs=(
            P("dp", "seq", None, None, None),
            P("dp", "seq", None, None, None),
            P("dp", None),
            P("dp", None),
        ),
        check_vma=False,
    )
```

```python
import jax
import jax.numpy as jnp
from jax import lax
from jax.experimental import pallas as pl
from jax.experimental.pallas import tpu as pltpu
from jax.sharding import PartitionSpec as P

C = 128
GROUP = 4
F = 8
HT = 8
WT = 32
POS = HT * WT
BLOCK = 108
PADDED = 112
BF16 = jnp.bfloat16
F32 = jnp.float32


def clip_at(clips, frame):
    return clips[0, jnp.clip(frame, 0, clips.shape[1] - 1)]


def past_slots(clips, first, t, base, none):
    slots = []
    for k in range(3):
        frame = first + t + k - 2
        same = clip_at(clips, frame) == clip_at(clips, first + t)
        slots.append(jnp.where(same & (frame >= 0), t + k - 2 + base, none))
    return slots


def next_slots(clips, first, t, base, none):
    slots = []
    for q in range(3):
        frame = first + t + q
        same = clip_at(clips, frame) == clip_at(clips, first + t)
        slots.append(jnp.where(same & (frame < clips.shape[1]), t + q + base, none))
    return slots


def column(rows):
    return lax.broadcasted_iota(jnp.int32, (rows, C), 0) % WT


def shift_down(value):
    return jnp.where(column(POS) == 0, 0.0, pltpu.roll(value, 1, 0))


def shift_up(value):
    return jnp.where(column(POS) == WT - 1, 0.0, pltpu.roll(value, POS - 1, 0))


def row_pieces(frame):
    edge = jnp.zeros((WT, C), frame.dtype)
    return [
        jnp.concatenate([edge, frame[: POS - WT]], axis=0),
        frame,
        jnp.concatenate([frame[WT:], edge], axis=0),
    ]


def column_pieces(frame):
    wide = frame.astype(F32)
    return jnp.concatenate([shift_up(wide).astype(BF16), frame, shift_down(wide).astype(BF16)], axis=1)


def conv_frame(window, slots, weight):
    pieces = []
    for slot in slots:
        pieces += row_pieces(window[slot])
    taps = jnp.dot(jnp.concatenate(pieces, axis=1), weight[...], preferred_element_type=F32)
    return shift_down(taps[:, :C]) + taps[:, C : 2 * C] + shift_up(taps[:, 2 * C :])


def forward_weight(weight_ref, out_ref):
    for outer in range(9):
        for b in range(3):
            out_ref[outer * C : (outer + 1) * C, b * C : (b + 1) * C] = weight_ref[
                (outer * 3 + b) * C : (outer * 3 + b + 1) * C, :
            ]


def adjoint_weight(weight_ref, out_ref):
    for outer in range(9):
        for b in range(3):
            tap = 26 - (outer * 3 + b)
            out_ref[outer * C : (outer + 1) * C, b * C : (b + 1) * C] = weight_ref[
                tap * C : (tap + 1) * C, :
            ].T


def group_mean(sums):
    count = len(sums)
    sums = jnp.concatenate(sums + [jnp.zeros_like(sums[0])] * (F - count), axis=0)
    lane = lax.broadcasted_iota(jnp.int32, sums.shape, 1)
    pairs = sums + jnp.where(lane % 2 == 0, pltpu.roll(sums, C - 1, 1), pltpu.roll(sums, 1, 1))
    quads = pairs + jnp.where(lane % 4 < 2, pltpu.roll(pairs, C - 2, 1), pltpu.roll(pairs, 2, 1))
    mean = quads * (1.0 / (GROUP * POS))
    return [mean[t : t + 1] for t in range(count)]


def tile_sum(value):
    return jnp.sum(value, axis=0, keepdims=True)


def normalize(act, count):
    center = group_mean([tile_sum(act[t]) for t in range(count)])
    sums = []
    for t in range(count):
        away = act[t] - center[t]
        act[t] = away
        sums.append(tile_sum(away * away))
    scale = [lax.rsqrt(mean + 1e-06) for mean in group_mean(sums)]
    for t in range(count):
        act[t] = act[t] * scale[t]
    return scale


def gate_of(normed):
    return 1.0 / (1.0 + jnp.exp(-normed))


def norm_adjoint(act, back, scale, count):
    first, second = [], []
    for t in range(count):
        gate = gate_of(act[t])
        grad = back[t] * (gate * (1.0 + act[t] * (1.0 - gate)))
        back[t] = grad
        first.append(tile_sum(grad))
        second.append(tile_sum(grad * act[t]))
    first, second = group_mean(first), group_mean(second)
    return [
        (scale[t] * (back[t] - first[t] - act[t] * second[t])).astype(BF16) for t in range(count)
    ]


def first_frame():
    return lax.axis_index("seq") * F


def halo_kernel(frames, cot, tail, head, sems):
    copies = [
        pltpu.make_async_copy(frames.at[F - 4 :], tail, sems.at[0]),
        pltpu.make_async_copy(frames.at[:2], head.at[:2], sems.at[1]),
        pltpu.make_async_copy(cot.at[:4], head.at[2:], sems.at[2]),
    ]
    for copy in copies:
        copy.start()
    for copy in copies:
        copy.wait()


def local_kernel(
    clips,
    frames,
    cot,
    weight1,
    weight2,
    window,
    cot_window,
    weight1_copy,
    weight2_copy,
    conv_weight,
    back_weight,
    act,
    back,
    sems,
):
    copies = [
        pltpu.make_async_copy(weight1, weight1_copy, sems.at[0]),
        pltpu.make_async_copy(frames, window.at[:F], sems.at[1]),
        pltpu.make_async_copy(weight2, weight2_copy, sems.at[2]),
        pltpu.make_async_copy(cot, cot_window.at[:F], sems.at[3]),
    ]
    for copy in copies:
        copy.start()
    window[F] = jnp.zeros((POS, C), BF16)
    cot_window[F] = jnp.zeros((POS, C), BF16)
    first = first_frame()
    copies[0].wait()
    forward_weight(weight1_copy, conv_weight)
    copies[1].wait()
    for t in range(2, F):
        act[t] = conv_frame(window, past_slots(clips, first, t, 0, F), conv_weight)
    copies[2].wait()
    adjoint_weight(weight2_copy, back_weight)
    copies[3].wait()
    for t in range(F - 2):
        back[t] = conv_frame(cot_window, next_slots(clips, first, t, 0, F), back_weight)


def main_kernel(
    clips,
    frames,
    cot,
    tail,
    head,
    conv_weight,
    back_weight,
    act_in,
    back_in,
    hidden_ref,
    act_grad_ref,
    keep_ref,
    send_ref,
    window,
    cot_window,
    act,
    back,
    cot_shifted,
    cot_taps,
    frame_t,
    frame_taps,
    hidden_t,
    grad_shifted,
    grads,
):
    none = F + 2
    first = first_frame()
    past = [past_slots(clips, first, t, 2, none) for t in range(F)]
    following = [next_slots(clips, first, t, 0, none) for t in range(F)]
    for f in range(2):
        window[f] = tail[2 + f]
        cot_window[F + f] = head[2 + f]
    for f in range(F):
        window[2 + f] = frames[f]
        cot_window[f] = cot[f]
    window[none] = jnp.zeros((POS, C), BF16)
    cot_window[none] = jnp.zeros((POS, C), BF16)

    for t in range(F):
        act[t] = conv_frame(window, past[t], conv_weight) if t < 2 else act_in[t]
        back[t] = back_in[t] if t < F - 2 else conv_frame(cot_window, following[t], back_weight)
    scale = normalize(act, F)
    for t in range(F):
        hidden = (act[t] * gate_of(act[t])).astype(BF16)
        hidden_ref[t] = hidden
        for a, piece in enumerate(row_pieces(hidden)):
            hidden_t[a * C : (a + 1) * C, t * POS : (t + 1) * POS] = piece.T
    for t, rounded in enumerate(norm_adjoint(act, back, scale, F)):
        act_grad_ref[t] = rounded
        grad_shifted[t * POS : (t + 1) * POS] = column_pieces(rounded)

    for f in range(F + 2):
        cot_shifted[f] = column_pieces(cot_window[f])
    cot_shifted[none] = jnp.zeros((POS, 3 * C), BF16)
    for s in range(F):
        for k in range(3):
            cot_taps[s * POS : (s + 1) * POS, 3 * C * k : 3 * C * (k + 1)] = cot_shifted[
                following[s][2 - k]
            ]
    second_grad = jnp.dot(hidden_t[...], cot_taps[...], preferred_element_type=F32)
    for k in range(3):
        for a in range(3):
            for b in range(3):
                tap = (k * 3 + a) * 3 + b
                grads[1, tap * C : (tap + 1) * C] = second_grad[
                    a * C : (a + 1) * C, (k * 3 + b) * C : (k * 3 + b + 1) * C
                ]

    for f in range(F + 2):
        for a, piece in enumerate(row_pieces(window[f])):
            frame_t[f, a * C : (a + 1) * C, :] = piece.T
    frame_t[none] = jnp.zeros((3 * C, POS), BF16)
    for t in range(F):
        for k in range(3):
            frame_taps[3 * C * k : 3 * C * (k + 1), t * POS : (t + 1) * POS] = frame_t[past[t][k]]
    first_grad = jnp.dot(frame_taps[...], grad_shifted[...], preferred_element_type=F32)
    for outer in range(9):
        for b in range(3):
            tap = outer * 3 + b
            grads[0, tap * C : (tap + 1) * C] = first_grad[
                outer * C : (outer + 1) * C, b * C : (b + 1) * C
            ]

    own = lax.rem(lax.axis_index("dp"), 2) == 0
    for g in range(2):
        for m in range(16):
            low = grads[g, 2 * BLOCK * m : 2 * BLOCK * m + BLOCK]
            high = grads[g, 2 * BLOCK * m + BLOCK : 2 * BLOCK * (m + 1)]
            keep_ref[g, m, :BLOCK] = jnp.where(own, low, high)
            keep_ref[g, m, BLOCK:] = jnp.zeros((PADDED - BLOCK, C), F32)
            send_ref[g, m, :BLOCK] = jnp.where(own, high, low).astype(BF16)
            send_ref[g, m, BLOCK:] = jnp.zeros((PADDED - BLOCK, C), BF16)


def forward_kernel(
    clips, hidden_in, frames, tail, conv_weight, weight2, out_ref, window, act, hidden, weight
):
    first = first_frame()
    for f in range(4):
        window[f] = tail[f]
    window[4] = jnp.zeros((POS, C), BF16)
    for t in range(2):
        act[t] = conv_frame(window, past_slots(clips, first, t - 2, 4, 4), conv_weight)
    normalize(act, 2)
    for t in range(2):
        hidden[t] = (act[t] * gate_of(act[t])).astype(BF16)
    for f in range(F):
        hidden[2 + f] = hidden_in[f]
    hidden[F + 2] = jnp.zeros((POS, C), BF16)
    forward_weight(weight2, weight)
    for t in range(F):
        out = conv_frame(hidden, past_slots(clips, first, t, 2, F + 2), weight)
        out_ref[t] = (frames[t].astype(F32) + out).astype(BF16)


def backward_kernel(
    clips,
    act_grad_in,
    frames,
    cot,
    head,
    conv_weight,
    back_weight,
    weight1,
    out_ref,
    window,
    cot_window,
    act,
    back,
    act_grad,
    weight,
):
    first = first_frame()
    zero = jnp.zeros((POS, C), BF16)
    for f in range(2):
        window[f] = frames[F - 2 + f]
        window[2 + f] = head[f]
    for f in range(4):
        cot_window[f] = head[2 + f]
    window[4] = zero
    cot_window[4] = zero
    for t in range(2):
        act[t] = conv_frame(window, past_slots(clips, first, F + t, 2 - F, 4), conv_weight)
        back[t] = conv_frame(cot_window, next_slots(clips, first, F + t, -F, 4), back_weight)
    scale = normalize(act, 2)
    for t, rounded in enumerate(norm_adjoint(act, back, scale, 2)):
        act_grad[F + t] = rounded
    for f in range(F):
        act_grad[f] = act_grad_in[f]
    act_grad[F + 2] = zero
    adjoint_weight(weight1, weight)
    for t in range(F):
        out = conv_frame(act_grad, next_slots(clips, first, t, 0, F + 2), weight)
        out_ref[t] = (cot[t].astype(F32) + out).astype(BF16)


def x_kernel(keep_ref, part, kept_ref, *sent_refs):
    own = lax.rem(lax.div(lax.axis_index("dp"), 2), 4)
    for g in range(2):
        for y in range(4):
            for step in range(4):
                block = lax.rem(own + step, 4)
                total = keep_ref[g, y, block] + part[g, y, block].astype(F32)
                if step == 0:
                    kept_ref[g, y] = total
                else:
                    sent_refs[step - 1][g, y] = total.astype(BF16)


def y_kernel(keep_ref, *refs):
    received, (kept_ref, *sent_refs) = refs[:3], refs[3:]
    own = lax.div(lax.axis_index("dp"), 8)
    for g in range(2):
        for step in range(4):
            block = lax.rem(own + step, 4)
            total = keep_ref[g, block]
            for part in received:
                total = total + part[g, block].astype(F32)
            if step == 0:
                kept_ref[g] = total
            else:
                sent_refs[step - 1][g] = total.astype(BF16)


def sum_kernel(keep_ref, *refs):
    received, out_ref = refs[:-1], refs[-1]
    total = keep_ref[...].astype(F32)
    for part in received:
        total = total + part[...].astype(F32)
    out_ref[...] = total.astype(BF16)


def last_kernel(scale, own, near, next_near, far, first_ref, second_ref):
    for g, out_ref in enumerate((first_ref, second_ref)):
        total = (own[g].astype(F32) + far[g].astype(F32)) + (
            near[g].astype(F32) + next_near[g].astype(F32)
        )
        out_ref[...] = (total * scale)[:BLOCK]


VMEM = pl.BlockSpec(memory_space=pltpu.VMEM)
SMEM = pl.BlockSpec(memory_space=pltpu.SMEM)
HBM = pl.BlockSpec(memory_space=pltpu.HBM)


def call(kernel, operands, in_specs, outs, scratch=(), flops=0, moved=1 << 20, limit=4):
    return pl.pallas_call(
        kernel,
        out_shape=[jax.ShapeDtypeStruct(shape, dtype) for shape, dtype in outs],
        in_specs=in_specs,
        out_specs=[VMEM] * len(outs),
        scratch_shapes=[
            pltpu.VMEM(*one) if isinstance(one, tuple) else one for one in scratch
        ],
        compiler_params=pltpu.CompilerParams(vmem_limit_bytes=limit << 20),
        cost_estimate=pl.CostEstimate(flops=flops, bytes_accessed=moved, transcendentals=0),
    )(*operands)


CONV_FLOPS = 2 * F * POS * 27 * C * C
WIDE = ((9 * C, 3 * C), BF16)


def frame_shape(count, dtype=BF16):
    return ((count, POS, C), dtype)


def shifted(value, steps):
    count = lax.axis_size("seq")
    first, last = (max(0, -steps), min(count, count - steps))
    return lax.ppermute(value, "seq", [(source, source + steps) for source in range(first, last)])


def dp_permute(value, target):
    return lax.ppermute(value, "dp", [(source, target(source)) for source in range(32)])


def seq_permute(value, target):
    return lax.ppermute(value, "seq", [(source, target(source) % 8) for source in range(8)])


def per_device(frames, clip_ids, cotangent, conv1_weight, conv2_weight):
    own_frames = frames.reshape(F, POS, C)
    own_cot = cotangent.reshape(F, POS, C)
    own_frames, own_cot, conv1_weight, conv2_weight = (
        pltpu.with_memory_space_constraint(value, pltpu.HBM)
        for value in (own_frames, own_cot, conv1_weight, conv2_weight)
    )
    tail, head = call(
        halo_kernel,
        (own_frames, own_cot),
        [HBM, HBM],
        [frame_shape(4), frame_shape(6)],
        [pltpu.SemaphoreType.DMA((3,))],
    )
    head = shifted(head, -1)
    tail = shifted(tail, 1)
    local = call(
        local_kernel,
        (clip_ids, own_frames, own_cot, conv1_weight, conv2_weight),
        [SMEM, HBM, HBM, HBM, HBM],
        [
            frame_shape(F + 1),
            frame_shape(F + 1),
            ((27 * C, C), BF16),
            ((27 * C, C), BF16),
            WIDE,
            WIDE,
            frame_shape(F, F32),
            frame_shape(F, F32),
        ],
        [pltpu.SemaphoreType.DMA((4,))],
        flops=CONV_FLOPS * 3 // 2,
        limit=16,
    )
    tail, head, local = lax.optimization_barrier((tail, head, local))
    frame_copy, cot_copy, weight1, weight2, conv_weight, back_weight, act, back = local
    block = ((2, 16, PADDED, C), F32)
    hidden, act_grad, keep, send = call(
        main_kernel,
        (clip_ids, frame_copy, cot_copy, tail, head, conv_weight, back_weight, act, back),
        [SMEM] + [VMEM] * 8,
        [frame_shape(F), frame_shape(F), block, (block[0], BF16)],
        [
            frame_shape(F + 3),
            frame_shape(F + 3),
            frame_shape(F, F32),
            frame_shape(F, F32),
            ((F + 3, POS, 3 * C), BF16),
            ((F * POS, 9 * C), BF16),
            ((F + 3, 3 * C, POS), BF16),
            ((9 * C, F * POS), BF16),
            ((3 * C, F * POS), BF16),
            ((F * POS, 3 * C), BF16),
            ((2, 27 * C, C), F32),
        ],
        flops=CONV_FLOPS * 5 // 2,
        limit=40,
    )
    recv = dp_permute(send, lambda d: d ^ 1)
    keep, *sent = call(
        x_kernel,
        (keep.reshape(2, 4, 4, PADDED, C), recv.reshape(2, 4, 4, PADDED, C)),
        [VMEM] * 2,
        [((2, 4, PADDED, C), F32)] + [((2, 4, PADDED, C), BF16)] * 3,
    )
    sent, hidden, act_grad = lax.optimization_barrier((sent, hidden, act_grad))
    recv = [
        dp_permute(part, lambda d, s=s: (d // 8) * 8 + (d % 8 + 2 * s) % 8)
        for s, part in zip((1, 2, 3), sent)
    ]
    (block_out,) = call(
        forward_kernel,
        (clip_ids, hidden, frame_copy, tail, conv_weight, weight2),
        [SMEM] + [VMEM] * 5,
        [frame_shape(F)],
        [frame_shape(5), frame_shape(2, F32), frame_shape(F + 3), WIDE],
        flops=CONV_FLOPS * 5 // 4,
        limit=12,
    )
    (input_grad,) = call(
        backward_kernel,
        (clip_ids, act_grad, frame_copy, cot_copy, head, conv_weight, back_weight, weight1),
        [SMEM] + [VMEM] * 7,
        [frame_shape(F)],
        [
            frame_shape(5),
            frame_shape(5),
            frame_shape(2, F32),
            frame_shape(2, F32),
            frame_shape(F + 3),
            WIDE,
        ],
        flops=CONV_FLOPS * 3 // 2,
        limit=12,
    )
    recv, block_out, input_grad = lax.optimization_barrier((recv, block_out, input_grad))
    pair = (2, PADDED, C)
    keep, *sent = call(y_kernel, (keep, *recv), [VMEM] * 4, [(pair, F32)] + [(pair, BF16)] * 3)
    recv = [dp_permute(part, lambda d, s=s: (d + 8 * s) % 32) for s, part in zip((1, 2, 3), sent)]
    (total,) = call(sum_kernel, (keep, *recv), [VMEM] * 4, [(pair, BF16)])
    other = seq_permute(total, lambda z: z ^ 1)
    (total,) = call(sum_kernel, (total, other), [VMEM] * 2, [(pair, BF16)])
    others = [
        seq_permute(total, lambda z, s=s: z + s if z % 2 else z - s) for s in (1, 2, 3)
    ]
    rows = lax.axis_size("dp") * lax.axis_size("seq") * F * POS
    first_grad, second_grad = call(
        lambda *refs: last_kernel(rows**-0.5, *refs),
        (total, *others),
        [VMEM] * 4,
        [((BLOCK, C), F32)] * 2,
    )
    return (
        block_out.reshape(frames.shape),
        input_grad.reshape(frames.shape),
        first_grad,
        second_grad,
    )


def solution(mesh):
    return jax.shard_map(
        per_device,
        mesh=mesh,
        in_specs=(
            P("dp", "seq", None, None, None),
            P("dp", None),
            P("dp", "seq", None, None, None),
            P(),
            P(),
        ),
        out_specs=(
            P("dp", "seq", None, None, None),
            P("dp", "seq", None, None, None),
            P("dp", None),
            P("dp", None),
        ),
        check_vma=False,
    )
```

```python
import jax
import jax.numpy as jnp
from jax import lax
from jax.experimental import pallas as pl
from jax.experimental.pallas import tpu as pltpu
from jax.sharding import PartitionSpec as P

C = 128
GROUP = 4
F = 8
HT = 8
WT = 32
POS = HT * WT
BLOCK = 108
PADDED = 112
BF16 = jnp.bfloat16
F32 = jnp.float32


def clip_at(clips, frame):
    return clips[0, jnp.clip(frame, 0, clips.shape[1] - 1)]


def past_slots(clips, first, t, base, none):
    slots = []
    for k in range(3):
        frame = first + t + k - 2
        same = clip_at(clips, frame) == clip_at(clips, first + t)
        slots.append(jnp.where(same & (frame >= 0), t + k - 2 + base, none))
    return slots


def next_slots(clips, first, t, base, none):
    slots = []
    for q in range(3):
        frame = first + t + q
        same = clip_at(clips, frame) == clip_at(clips, first + t)
        slots.append(jnp.where(same & (frame < clips.shape[1]), t + q + base, none))
    return slots


def column(rows):
    return lax.broadcasted_iota(jnp.int32, (rows, C), 0) % WT


def shift_down(value):
    return jnp.where(column(POS) == 0, 0.0, pltpu.roll(value, 1, 0))


def shift_up(value):
    return jnp.where(column(POS) == WT - 1, 0.0, pltpu.roll(value, POS - 1, 0))


def row_pieces(frame):
    edge = jnp.zeros((WT, C), frame.dtype)
    return [
        jnp.concatenate([edge, frame[: POS - WT]], axis=0),
        frame,
        jnp.concatenate([frame[WT:], edge], axis=0),
    ]


def column_pieces(frame):
    wide = frame.astype(F32)
    return jnp.concatenate([shift_up(wide).astype(BF16), frame, shift_down(wide).astype(BF16)], axis=1)


def conv_frame(window, slots, weight):
    pieces = []
    for slot in slots:
        pieces += row_pieces(window[slot])
    taps = jnp.dot(jnp.concatenate(pieces, axis=1), weight[...], preferred_element_type=F32)
    return shift_down(taps[:, :C]) + taps[:, C : 2 * C] + shift_up(taps[:, 2 * C :])


def forward_weight(weight_ref, out_ref):
    for outer in range(9):
        for b in range(3):
            out_ref[outer * C : (outer + 1) * C, b * C : (b + 1) * C] = weight_ref[
                (outer * 3 + b) * C : (outer * 3 + b + 1) * C, :
            ]


def adjoint_weight(weight_ref, out_ref):
    for outer in range(9):
        for b in range(3):
            tap = 26 - (outer * 3 + b)
            out_ref[outer * C : (outer + 1) * C, b * C : (b + 1) * C] = weight_ref[
                tap * C : (tap + 1) * C, :
            ].T


def group_mean(sums):
    count = len(sums)
    sums = jnp.concatenate(sums + [jnp.zeros_like(sums[0])] * (F - count), axis=0)
    lane = lax.broadcasted_iota(jnp.int32, sums.shape, 1)
    pairs = sums + jnp.where(lane % 2 == 0, pltpu.roll(sums, C - 1, 1), pltpu.roll(sums, 1, 1))
    quads = pairs + jnp.where(lane % 4 < 2, pltpu.roll(pairs, C - 2, 1), pltpu.roll(pairs, 2, 1))
    mean = quads * (1.0 / (GROUP * POS))
    return [mean[t : t + 1] for t in range(count)]


def tile_sum(value):
    return jnp.sum(value, axis=0, keepdims=True)


def normalize(act, count):
    center = group_mean([tile_sum(act[t]) for t in range(count)])
    sums = []
    for t in range(count):
        away = act[t] - center[t]
        act[t] = away
        sums.append(tile_sum(away * away))
    scale = [lax.rsqrt(mean + 1e-06) for mean in group_mean(sums)]
    for t in range(count):
        act[t] = act[t] * scale[t]
    return scale


def gate_of(normed):
    return 1.0 / (1.0 + jnp.exp(-normed))


def norm_adjoint(act, back, scale, count):
    first, second = [], []
    for t in range(count):
        gate = gate_of(act[t])
        grad = back[t] * (gate * (1.0 + act[t] * (1.0 - gate)))
        back[t] = grad
        first.append(tile_sum(grad))
        second.append(tile_sum(grad * act[t]))
    first, second = group_mean(first), group_mean(second)
    return [
        (scale[t] * (back[t] - first[t] - act[t] * second[t])).astype(BF16) for t in range(count)
    ]


def first_frame():
    return lax.axis_index("seq") * F


def halo_kernel(clips, frames, cot, clips_copy, tail, head, sems):
    copies = [
        pltpu.make_async_copy(clips, clips_copy, sems.at[3]),
        pltpu.make_async_copy(frames.at[F - 4 :], tail, sems.at[0]),
        pltpu.make_async_copy(frames.at[:2], head.at[:2], sems.at[1]),
        pltpu.make_async_copy(cot.at[:4], head.at[2:], sems.at[2]),
    ]
    for copy in copies:
        copy.start()
    for copy in copies:
        copy.wait()


def local_kernel(
    clips,
    frames,
    cot,
    weight1,
    weight2,
    window,
    cot_window,
    weight1_copy,
    weight2_copy,
    conv_weight,
    back_weight,
    act,
    back,
    sems,
):
    copies = [
        pltpu.make_async_copy(weight1, weight1_copy, sems.at[0]),
        pltpu.make_async_copy(frames, window.at[:F], sems.at[1]),
        pltpu.make_async_copy(weight2, weight2_copy, sems.at[2]),
        pltpu.make_async_copy(cot, cot_window.at[:F], sems.at[3]),
    ]
    for copy in copies:
        copy.start()
    window[F] = jnp.zeros((POS, C), BF16)
    cot_window[F] = jnp.zeros((POS, C), BF16)
    first = first_frame()
    copies[0].wait()
    forward_weight(weight1_copy, conv_weight)
    copies[1].wait()
    for t in range(2, F):
        act[t] = conv_frame(window, past_slots(clips, first, t, 0, F), conv_weight)
    copies[2].wait()
    adjoint_weight(weight2_copy, back_weight)
    copies[3].wait()
    for t in range(F - 2):
        back[t] = conv_frame(cot_window, next_slots(clips, first, t, 0, F), back_weight)


def main_kernel(
    clips,
    frames,
    cot,
    tail,
    head,
    conv_weight,
    back_weight,
    act_in,
    back_in,
    hidden_ref,
    act_grad_ref,
    keep_ref,
    send_ref,
    window,
    cot_window,
    act,
    back,
    cot_shifted,
    cot_taps,
    frame_t,
    frame_taps,
    hidden_t,
    grad_shifted,
    grads,
):
    none = F + 2
    first = first_frame()
    past = [past_slots(clips, first, t, 2, none) for t in range(F)]
    following = [next_slots(clips, first, t, 0, none) for t in range(F)]
    for f in range(2):
        window[f] = tail[2 + f]
        cot_window[F + f] = head[2 + f]
    for f in range(F):
        window[2 + f] = frames[f]
        cot_window[f] = cot[f]
    window[none] = jnp.zeros((POS, C), BF16)
    cot_window[none] = jnp.zeros((POS, C), BF16)

    for t in range(F):
        act[t] = conv_frame(window, past[t], conv_weight) if t < 2 else act_in[t]
        back[t] = back_in[t] if t < F - 2 else conv_frame(cot_window, following[t], back_weight)
    scale = normalize(act, F)
    for t in range(F):
        hidden = (act[t] * gate_of(act[t])).astype(BF16)
        hidden_ref[t] = hidden
        for a, piece in enumerate(row_pieces(hidden)):
            hidden_t[a * C : (a + 1) * C, t * POS : (t + 1) * POS] = piece.T
    for t, rounded in enumerate(norm_adjoint(act, back, scale, F)):
        act_grad_ref[t] = rounded
        grad_shifted[t * POS : (t + 1) * POS] = column_pieces(rounded)

    for f in range(F + 2):
        cot_shifted[f] = column_pieces(cot_window[f])
    cot_shifted[none] = jnp.zeros((POS, 3 * C), BF16)
    for s in range(F):
        for k in range(3):
            cot_taps[s * POS : (s + 1) * POS, 3 * C * k : 3 * C * (k + 1)] = cot_shifted[
                following[s][2 - k]
            ]
    second_grad = jnp.dot(hidden_t[...], cot_taps[...], preferred_element_type=F32)
    for k in range(3):
        for a in range(3):
            for b in range(3):
                tap = (k * 3 + a) * 3 + b
                grads[1, tap * C : (tap + 1) * C] = second_grad[
                    a * C : (a + 1) * C, (k * 3 + b) * C : (k * 3 + b + 1) * C
                ]

    for f in range(F + 2):
        for a, piece in enumerate(row_pieces(window[f])):
            frame_t[f, a * C : (a + 1) * C, :] = piece.T
    frame_t[none] = jnp.zeros((3 * C, POS), BF16)
    for t in range(F):
        for k in range(3):
            frame_taps[3 * C * k : 3 * C * (k + 1), t * POS : (t + 1) * POS] = frame_t[past[t][k]]
    first_grad = jnp.dot(frame_taps[...], grad_shifted[...], preferred_element_type=F32)
    for outer in range(9):
        for b in range(3):
            tap = outer * 3 + b
            grads[0, tap * C : (tap + 1) * C] = first_grad[
                outer * C : (outer + 1) * C, b * C : (b + 1) * C
            ]

    own = lax.rem(lax.axis_index("dp"), 2) == 0
    for g in range(2):
        for m in range(16):
            low = grads[g, 2 * BLOCK * m : 2 * BLOCK * m + BLOCK]
            high = grads[g, 2 * BLOCK * m + BLOCK : 2 * BLOCK * (m + 1)]
            keep_ref[g, m, :BLOCK] = jnp.where(own, low, high)
            keep_ref[g, m, BLOCK:] = jnp.zeros((PADDED - BLOCK, C), F32)
            send_ref[g, m, :BLOCK] = jnp.where(own, high, low).astype(BF16)
            send_ref[g, m, BLOCK:] = jnp.zeros((PADDED - BLOCK, C), BF16)


def forward_kernel(
    clips, hidden_in, frames, tail, conv_weight, weight2, out_ref, window, act, hidden, weight
):
    first = first_frame()
    for f in range(4):
        window[f] = tail[f]
    window[4] = jnp.zeros((POS, C), BF16)
    for t in range(2):
        act[t] = conv_frame(window, past_slots(clips, first, t - 2, 4, 4), conv_weight)
    normalize(act, 2)
    for t in range(2):
        hidden[t] = (act[t] * gate_of(act[t])).astype(BF16)
    for f in range(F):
        hidden[2 + f] = hidden_in[f]
    hidden[F + 2] = jnp.zeros((POS, C), BF16)
    forward_weight(weight2, weight)
    for t in range(F):
        out = conv_frame(hidden, past_slots(clips, first, t, 2, F + 2), weight)
        out_ref[t] = (frames[t].astype(F32) + out).astype(BF16)


def next_grad_kernel(
    clips, frames, head, conv_weight, back_weight, out_ref, window, cot_window, act, back
):
    first = first_frame()
    zero = jnp.zeros((POS, C), BF16)
    for f in range(2):
        window[f] = frames[F - 2 + f]
        window[2 + f] = head[f]
    for f in range(4):
        cot_window[f] = head[2 + f]
    window[4] = zero
    cot_window[4] = zero
    for t in range(2):
        act[t] = conv_frame(window, past_slots(clips, first, F + t, 2 - F, 4), conv_weight)
        back[t] = conv_frame(cot_window, next_slots(clips, first, F + t, -F, 4), back_weight)
    scale = normalize(act, 2)
    for t, rounded in enumerate(norm_adjoint(act, back, scale, 2)):
        out_ref[t] = rounded


def backward_kernel(clips, act_grad_in, next_in, cot, weight1, out_ref, act_grad, weight):
    first = first_frame()
    for f in range(F):
        act_grad[f] = act_grad_in[f]
    for f in range(2):
        act_grad[F + f] = next_in[f]
    act_grad[F + 2] = jnp.zeros((POS, C), BF16)
    adjoint_weight(weight1, weight)
    for t in range(F):
        out = conv_frame(act_grad, next_slots(clips, first, t, 0, F + 2), weight)
        out_ref[t] = (cot[t].astype(F32) + out).astype(BF16)


def x_kernel(keep_ref, part, kept_ref, *sent_refs):
    own = lax.rem(lax.div(lax.axis_index("dp"), 2), 4)
    for g in range(2):
        for y in range(4):
            for step in range(4):
                block = lax.rem(own + step, 4)
                total = keep_ref[g, y, block] + part[g, y, block].astype(F32)
                if step == 0:
                    kept_ref[g, y] = total
                else:
                    sent_refs[step - 1][g, y] = total.astype(BF16)


def y_kernel(keep_ref, *refs):
    received, (kept_ref, *sent_refs) = refs[:3], refs[3:]
    own = lax.div(lax.axis_index("dp"), 8)
    for g in range(2):
        for step in range(4):
            block = lax.rem(own + step, 4)
            total = keep_ref[g, block]
            for part in received:
                total = total + part[g, block].astype(F32)
            if step == 0:
                kept_ref[g] = total
            else:
                sent_refs[step - 1][g] = total.astype(BF16)


def sum_kernel(keep_ref, *refs):
    received, out_ref = refs[:-1], refs[-1]
    total = keep_ref[...].astype(F32)
    for part in received:
        total = total + part[...].astype(F32)
    out_ref[...] = total.astype(BF16)


def last_kernel(scale, own, near, next_near, far, first_ref, second_ref):
    for g, out_ref in enumerate((first_ref, second_ref)):
        total = (own[g].astype(F32) + far[g].astype(F32)) + (
            near[g].astype(F32) + next_near[g].astype(F32)
        )
        out_ref[...] = (total * scale)[:BLOCK]


VMEM = pl.BlockSpec(memory_space=pltpu.VMEM)
SMEM = pl.BlockSpec(memory_space=pltpu.SMEM)
HBM = pl.BlockSpec(memory_space=pltpu.HBM)


def call(kernel, operands, in_specs, outs, scratch=(), flops=0, moved=1 << 20, limit=4):
    return pl.pallas_call(
        kernel,
        out_shape=[jax.ShapeDtypeStruct(shape, dtype) for shape, dtype in outs],
        in_specs=in_specs,
        out_specs=[VMEM] * len(outs),
        scratch_shapes=[
            pltpu.VMEM(*one) if isinstance(one, tuple) else one for one in scratch
        ],
        compiler_params=pltpu.CompilerParams(vmem_limit_bytes=limit << 20),
        cost_estimate=pl.CostEstimate(flops=flops, bytes_accessed=moved, transcendentals=0),
    )(*operands)


CONV_FLOPS = 2 * F * POS * 27 * C * C
WIDE = ((9 * C, 3 * C), BF16)


def frame_shape(count, dtype=BF16):
    return ((count, POS, C), dtype)


def shifted(value, steps):
    return seq_permute(value, lambda z: z + steps)


def dp_permute(value, target):
    return lax.ppermute(value, "dp", [(source, target(source)) for source in range(32)])


def seq_permute(value, target):
    return lax.ppermute(value, "seq", [(source, target(source) % 8) for source in range(8)])


def per_device(frames, clip_ids, cotangent, conv1_weight, conv2_weight):
    own_frames = frames.reshape(F, POS, C)
    own_cot = cotangent.reshape(F, POS, C)
    clip_ids, own_frames, own_cot, conv1_weight, conv2_weight = (
        pltpu.with_memory_space_constraint(value, pltpu.HBM)
        for value in (clip_ids, own_frames, own_cot, conv1_weight, conv2_weight)
    )
    clip_ids, tail, head = call(
        halo_kernel,
        (clip_ids, own_frames, own_cot),
        [HBM, HBM, HBM],
        [(clip_ids.shape, jnp.int32), frame_shape(4), frame_shape(6)],
        [pltpu.SemaphoreType.DMA((4,))],
    )
    head = shifted(head, -1)
    tail = shifted(tail, 1)
    local = call(
        local_kernel,
        (clip_ids, own_frames, own_cot, conv1_weight, conv2_weight),
        [SMEM, HBM, HBM, HBM, HBM],
        [
            frame_shape(F + 1),
            frame_shape(F + 1),
            ((27 * C, C), BF16),
            ((27 * C, C), BF16),
            WIDE,
            WIDE,
            frame_shape(F, F32),
            frame_shape(F, F32),
        ],
        [pltpu.SemaphoreType.DMA((4,))],
        flops=CONV_FLOPS * 3 // 2,
        limit=16,
    )
    tail, head, local = lax.optimization_barrier((tail, head, local))
    frame_copy, cot_copy, weight1, weight2, conv_weight, back_weight, act, back = local
    block = ((2, 16, PADDED, C), F32)
    hidden, act_grad, keep, send = call(
        main_kernel,
        (clip_ids, frame_copy, cot_copy, tail, head, conv_weight, back_weight, act, back),
        [SMEM] + [VMEM] * 8,
        [frame_shape(F), frame_shape(F), block, (block[0], BF16)],
        [
            frame_shape(F + 3),
            frame_shape(F + 3),
            frame_shape(F, F32),
            frame_shape(F, F32),
            ((F + 3, POS, 3 * C), BF16),
            ((F * POS, 9 * C), BF16),
            ((F + 3, 3 * C, POS), BF16),
            ((9 * C, F * POS), BF16),
            ((3 * C, F * POS), BF16),
            ((F * POS, 3 * C), BF16),
            ((2, 27 * C, C), F32),
        ],
        flops=CONV_FLOPS * 5 // 2,
        limit=40,
    )
    recv = dp_permute(send, lambda d: d ^ 1)
    head, keep = lax.optimization_barrier((head, keep))
    (act_grad_next,) = call(
        next_grad_kernel,
        (clip_ids, frame_copy, head, conv_weight, back_weight),
        [SMEM] + [VMEM] * 4,
        [frame_shape(2)],
        [frame_shape(5), frame_shape(5), frame_shape(2, F32), frame_shape(2, F32)],
        flops=CONV_FLOPS // 2,
        limit=8,
    )
    recv, act_grad_next = lax.optimization_barrier((recv, act_grad_next))
    keep, *sent = call(
        x_kernel,
        (keep.reshape(2, 4, 4, PADDED, C), recv.reshape(2, 4, 4, PADDED, C)),
        [VMEM] * 2,
        [((2, 4, PADDED, C), F32)] + [((2, 4, PADDED, C), BF16)] * 3,
    )
    sent, hidden = lax.optimization_barrier((sent, hidden))
    recv = [
        dp_permute(part, lambda d, s=s: (d // 8) * 8 + (d % 8 + 2 * s) % 8)
        for s, part in zip((1, 2, 3), sent)
    ]
    (block_out,) = call(
        forward_kernel,
        (clip_ids, hidden, frame_copy, tail, conv_weight, weight2),
        [SMEM] + [VMEM] * 5,
        [frame_shape(F)],
        [frame_shape(5), frame_shape(2, F32), frame_shape(F + 3), WIDE],
        flops=CONV_FLOPS * 5 // 4,
        limit=12,
    )
    recv, block_out = lax.optimization_barrier((recv, block_out))
    pair = (2, PADDED, C)
    keep, *sent = call(y_kernel, (keep, *recv), [VMEM] * 4, [(pair, F32)] + [(pair, BF16)] * 3)
    sent, act_grad = lax.optimization_barrier((sent, act_grad))
    recv = [dp_permute(part, lambda d, s=s: (d + 8 * s) % 32) for s, part in zip((1, 2, 3), sent)]
    (input_grad,) = call(
        backward_kernel,
        (clip_ids, act_grad, act_grad_next, cot_copy, weight1),
        [SMEM] + [VMEM] * 4,
        [frame_shape(F)],
        [frame_shape(F + 3), WIDE],
        flops=CONV_FLOPS,
        limit=8,
    )
    recv, input_grad = lax.optimization_barrier((recv, input_grad))
    (total,) = call(sum_kernel, (keep, *recv), [VMEM] * 4, [(pair, BF16)])
    other = seq_permute(total, lambda z: z ^ 1)
    (total,) = call(sum_kernel, (total, other), [VMEM] * 2, [(pair, BF16)])
    others = [
        seq_permute(total, lambda z, s=s: z + s if z % 2 else z - s) for s in (1, 2, 3)
    ]
    rows = lax.axis_size("dp") * lax.axis_size("seq") * F * POS
    first_grad, second_grad = call(
        lambda *refs: last_kernel(rows**-0.5, *refs),
        (total, *others),
        [VMEM] * 4,
        [((BLOCK, C), F32)] * 2,
    )
    return (
        block_out.reshape(frames.shape),
        input_grad.reshape(frames.shape),
        first_grad,
        second_grad,
    )


def solution(mesh):
    return jax.shard_map(
        per_device,
        mesh=mesh,
        in_specs=(
            P("dp", "seq", None, None, None),
            P("dp", None),
            P("dp", "seq", None, None, None),
            P(),
            P(),
        ),
        out_specs=(
            P("dp", "seq", None, None, None),
            P("dp", "seq", None, None, None),
            P("dp", None),
            P("dp", None),
        ),
        check_vma=False,
    )
```

```python
import jax
import jax.numpy as jnp
from jax import lax
from jax.experimental import pallas as pl
from jax.experimental.pallas import tpu as pltpu
from jax.sharding import PartitionSpec as P

C = 128
GROUP = 4
F = 8
HT = 8
WT = 32
POS = HT * WT
BLOCK = 108
PADDED = 112
BF16 = jnp.bfloat16
F32 = jnp.float32


def clip_at(clips, frame):
    return clips[0, jnp.clip(frame, 0, clips.shape[1] - 1)]


def past_slots(clips, first, t, base, none):
    slots = []
    for k in range(3):
        frame = first + t + k - 2
        same = clip_at(clips, frame) == clip_at(clips, first + t)
        slots.append(jnp.where(same & (frame >= 0), t + k - 2 + base, none))
    return slots


def next_slots(clips, first, t, base, none):
    slots = []
    for q in range(3):
        frame = first + t + q
        same = clip_at(clips, frame) == clip_at(clips, first + t)
        slots.append(jnp.where(same & (frame < clips.shape[1]), t + q + base, none))
    return slots


def column(rows):
    return lax.broadcasted_iota(jnp.int32, (rows, C), 0) % WT


def shift_down(value):
    return jnp.where(column(POS) == 0, 0.0, pltpu.roll(value, 1, 0))


def shift_up(value):
    return jnp.where(column(POS) == WT - 1, 0.0, pltpu.roll(value, POS - 1, 0))


def row_pieces(frame):
    edge = jnp.zeros((WT, C), frame.dtype)
    return [
        jnp.concatenate([edge, frame[: POS - WT]], axis=0),
        frame,
        jnp.concatenate([frame[WT:], edge], axis=0),
    ]


def column_pieces(frame):
    wide = frame.astype(F32)
    return jnp.concatenate([shift_up(wide).astype(BF16), frame, shift_down(wide).astype(BF16)], axis=1)


def conv_frame(window, slots, weight):
    pieces = []
    for slot in slots:
        pieces += row_pieces(window[slot])
    taps = jnp.dot(jnp.concatenate(pieces, axis=1), weight[...], preferred_element_type=F32)
    return shift_down(taps[:, :C]) + taps[:, C : 2 * C] + shift_up(taps[:, 2 * C :])


def forward_weight(weight_ref, out_ref):
    for outer in range(9):
        for b in range(3):
            out_ref[outer * C : (outer + 1) * C, b * C : (b + 1) * C] = weight_ref[
                (outer * 3 + b) * C : (outer * 3 + b + 1) * C, :
            ]


def adjoint_weight(weight_ref, out_ref):
    for outer in range(9):
        for b in range(3):
            tap = 26 - (outer * 3 + b)
            out_ref[outer * C : (outer + 1) * C, b * C : (b + 1) * C] = weight_ref[
                tap * C : (tap + 1) * C, :
            ].T


def group_mean(sums):
    count = len(sums)
    sums = jnp.concatenate(sums + [jnp.zeros_like(sums[0])] * (F - count), axis=0)
    lane = lax.broadcasted_iota(jnp.int32, sums.shape, 1)
    pairs = sums + jnp.where(lane % 2 == 0, pltpu.roll(sums, C - 1, 1), pltpu.roll(sums, 1, 1))
    quads = pairs + jnp.where(lane % 4 < 2, pltpu.roll(pairs, C - 2, 1), pltpu.roll(pairs, 2, 1))
    mean = quads * (1.0 / (GROUP * POS))
    return [mean[t : t + 1] for t in range(count)]


def tile_sum(value):
    return jnp.sum(value, axis=0, keepdims=True)


def normalize(act, count):
    center = group_mean([tile_sum(act[t]) for t in range(count)])
    sums = []
    for t in range(count):
        away = act[t] - center[t]
        act[t] = away
        sums.append(tile_sum(away * away))
    scale = [lax.rsqrt(mean + 1e-06) for mean in group_mean(sums)]
    for t in range(count):
        act[t] = act[t] * scale[t]
    return scale


def gate_of(normed):
    return 1.0 / (1.0 + jnp.exp(-normed))


def norm_adjoint(act, back, scale, count):
    first, second = [], []
    for t in range(count):
        gate = gate_of(act[t])
        grad = back[t] * (gate * (1.0 + act[t] * (1.0 - gate)))
        back[t] = grad
        first.append(tile_sum(grad))
        second.append(tile_sum(grad * act[t]))
    first, second = group_mean(first), group_mean(second)
    return [
        (scale[t] * (back[t] - first[t] - act[t] * second[t])).astype(BF16) for t in range(count)
    ]


def first_frame():
    return lax.axis_index("seq") * F


def halo_kernel(clips, frames, cot, clips_copy, tail, head, sems):
    copies = [
        pltpu.make_async_copy(clips, clips_copy, sems.at[3]),
        pltpu.make_async_copy(frames.at[F - 4 :], tail, sems.at[0]),
        pltpu.make_async_copy(frames.at[:2], head.at[:2], sems.at[1]),
        pltpu.make_async_copy(cot.at[:4], head.at[2:], sems.at[2]),
    ]
    for copy in copies:
        copy.start()
    for copy in copies:
        copy.wait()


def local_kernel(
    clips,
    frames,
    cot,
    weight1,
    weight2,
    window,
    cot_window,
    weight1_copy,
    weight2_copy,
    conv_weight,
    back_weight,
    act,
    back,
    sems,
):
    copies = [
        pltpu.make_async_copy(weight1, weight1_copy, sems.at[0]),
        pltpu.make_async_copy(frames, window.at[:F], sems.at[1]),
        pltpu.make_async_copy(weight2, weight2_copy, sems.at[2]),
        pltpu.make_async_copy(cot, cot_window.at[:F], sems.at[3]),
    ]
    for copy in copies:
        copy.start()
    window[F] = jnp.zeros((POS, C), BF16)
    cot_window[F] = jnp.zeros((POS, C), BF16)
    first = first_frame()
    copies[0].wait()
    forward_weight(weight1_copy, conv_weight)
    copies[1].wait()
    for t in range(2, F):
        act[t] = conv_frame(window, past_slots(clips, first, t, 0, F), conv_weight)
    copies[2].wait()
    adjoint_weight(weight2_copy, back_weight)
    copies[3].wait()
    for t in range(F - 2):
        back[t] = conv_frame(cot_window, next_slots(clips, first, t, 0, F), back_weight)


def main_kernel(
    clips,
    frames,
    cot,
    tail,
    head,
    conv_weight,
    back_weight,
    act_in,
    back_in,
    hidden_ref,
    act_grad_ref,
    keep_ref,
    send_ref,
    window,
    cot_window,
    act,
    back,
    cot_shifted,
    cot_taps,
    frame_t,
    frame_taps,
    hidden_t,
    grad_shifted,
    grads,
):
    none = F + 2
    first = first_frame()
    past = [past_slots(clips, first, t, 2, none) for t in range(F)]
    following = [next_slots(clips, first, t, 0, none) for t in range(F)]
    for f in range(2):
        window[f] = tail[2 + f]
        cot_window[F + f] = head[2 + f]
    for f in range(F):
        window[2 + f] = frames[f]
        cot_window[f] = cot[f]
    window[none] = jnp.zeros((POS, C), BF16)
    cot_window[none] = jnp.zeros((POS, C), BF16)

    for t in range(F):
        act[t] = conv_frame(window, past[t], conv_weight) if t < 2 else act_in[t]
        back[t] = back_in[t] if t < F - 2 else conv_frame(cot_window, following[t], back_weight)
    scale = normalize(act, F)
    for t in range(F):
        hidden = (act[t] * gate_of(act[t])).astype(BF16)
        hidden_ref[t] = hidden
        for a, piece in enumerate(row_pieces(hidden)):
            hidden_t[a * C : (a + 1) * C, t * POS : (t + 1) * POS] = piece.T
    for t, rounded in enumerate(norm_adjoint(act, back, scale, F)):
        act_grad_ref[t] = rounded
        grad_shifted[t * POS : (t + 1) * POS] = column_pieces(rounded)

    for f in range(F + 2):
        cot_shifted[f] = column_pieces(cot_window[f])
    cot_shifted[none] = jnp.zeros((POS, 3 * C), BF16)
    for s in range(F):
        for k in range(3):
            cot_taps[s * POS : (s + 1) * POS, 3 * C * k : 3 * C * (k + 1)] = cot_shifted[
                following[s][2 - k]
            ]
    second_grad = jnp.dot(hidden_t[...], cot_taps[...], preferred_element_type=F32)
    for k in range(3):
        for a in range(3):
            for b in range(3):
                tap = (k * 3 + a) * 3 + b
                grads[1, tap * C : (tap + 1) * C] = second_grad[
                    a * C : (a + 1) * C, (k * 3 + b) * C : (k * 3 + b + 1) * C
                ]

    for f in range(F + 2):
        for a, piece in enumerate(row_pieces(window[f])):
            frame_t[f, a * C : (a + 1) * C, :] = piece.T
    frame_t[none] = jnp.zeros((3 * C, POS), BF16)
    for t in range(F):
        for k in range(3):
            frame_taps[3 * C * k : 3 * C * (k + 1), t * POS : (t + 1) * POS] = frame_t[past[t][k]]
    first_grad = jnp.dot(frame_taps[...], grad_shifted[...], preferred_element_type=F32)
    for outer in range(9):
        for b in range(3):
            tap = outer * 3 + b
            grads[0, tap * C : (tap + 1) * C] = first_grad[
                outer * C : (outer + 1) * C, b * C : (b + 1) * C
            ]

    own = lax.rem(lax.axis_index("dp"), 2) == 0
    for g in range(2):
        for m in range(16):
            low = grads[g, 2 * BLOCK * m : 2 * BLOCK * m + BLOCK]
            high = grads[g, 2 * BLOCK * m + BLOCK : 2 * BLOCK * (m + 1)]
            keep_ref[g, m, :BLOCK] = jnp.where(own, low, high)
            keep_ref[g, m, BLOCK:] = jnp.zeros((PADDED - BLOCK, C), F32)
            send_ref[g, m, :BLOCK] = jnp.where(own, high, low).astype(BF16)
            send_ref[g, m, BLOCK:] = jnp.zeros((PADDED - BLOCK, C), BF16)


def forward_kernel(
    clips, hidden_in, frames, tail, conv_weight, weight2, out_ref, window, act, hidden, weight
):
    first = first_frame()
    for f in range(4):
        window[f] = tail[f]
    window[4] = jnp.zeros((POS, C), BF16)
    for t in range(2):
        act[t] = conv_frame(window, past_slots(clips, first, t - 2, 4, 4), conv_weight)
    normalize(act, 2)
    for t in range(2):
        hidden[t] = (act[t] * gate_of(act[t])).astype(BF16)
    for f in range(F):
        hidden[2 + f] = hidden_in[f]
    hidden[F + 2] = jnp.zeros((POS, C), BF16)
    forward_weight(weight2, weight)
    for t in range(F):
        out = conv_frame(hidden, past_slots(clips, first, t, 2, F + 2), weight)
        out_ref[t] = (frames[t].astype(F32) + out).astype(BF16)


def next_grad_kernel(
    clips, frames, head, conv_weight, back_weight, out_ref, window, cot_window, act, back
):
    first = first_frame()
    zero = jnp.zeros((POS, C), BF16)
    for f in range(2):
        window[f] = frames[F - 2 + f]
        window[2 + f] = head[f]
    for f in range(4):
        cot_window[f] = head[2 + f]
    window[4] = zero
    cot_window[4] = zero
    for t in range(2):
        act[t] = conv_frame(window, past_slots(clips, first, F + t, 2 - F, 4), conv_weight)
        back[t] = conv_frame(cot_window, next_slots(clips, first, F + t, -F, 4), back_weight)
    scale = normalize(act, 2)
    for t, rounded in enumerate(norm_adjoint(act, back, scale, 2)):
        out_ref[t] = rounded


def backward_kernel(clips, act_grad_in, next_in, cot, weight1, out_ref, act_grad, weight):
    first = first_frame()
    for f in range(F):
        act_grad[f] = act_grad_in[f]
    for f in range(2):
        act_grad[F + f] = next_in[f]
    act_grad[F + 2] = jnp.zeros((POS, C), BF16)
    adjoint_weight(weight1, weight)
    for t in range(F):
        out = conv_frame(act_grad, next_slots(clips, first, t, 0, F + 2), weight)
        out_ref[t] = (cot[t].astype(F32) + out).astype(BF16)


def place():
    index = lax.axis_index("dp")
    return lax.div(index, 8), lax.rem(lax.div(index, 2), 4), lax.rem(index, 2) == 0


def first_kernel(keep_ref, part, kept_ref, *sent_refs):
    y, x, along_x = place()
    for g in range(2):
        for other in range(4):
            for step in range(4):
                block = jnp.where(
                    along_x, 4 * other + lax.rem(x + step, 4), 4 * lax.rem(y + step, 4) + other
                )
                total = keep_ref[g, block] + part[g, block].astype(F32)
                if step == 0:
                    kept_ref[g, other] = total
                else:
                    sent_refs[step - 1][g, other] = total.astype(BF16)


def second_kernel(keep_ref, *refs):
    received, (kept_ref, *sent_refs) = refs[:3], refs[3:]
    y, x, along_x = place()
    own = jnp.where(along_x, y, x)
    for g in range(2):
        for step in range(4):
            block = lax.rem(own + step, 4)
            total = keep_ref[g, block]
            for part in received:
                total = total + part[g, block].astype(F32)
            if step == 0:
                kept_ref[g] = total
            else:
                sent_refs[step - 1][g] = total.astype(BF16)


def sum_kernel(keep_ref, *refs):
    received, out_ref = refs[:-1], refs[-1]
    total = keep_ref[...].astype(F32)
    for part in received:
        total = total + part[...].astype(F32)
    out_ref[...] = total.astype(BF16)


def last_kernel(scale, own, near, next_near, far, first_ref, second_ref):
    for g, out_ref in enumerate((first_ref, second_ref)):
        total = (own[g].astype(F32) + far[g].astype(F32)) + (
            near[g].astype(F32) + next_near[g].astype(F32)
        )
        out_ref[...] = (total * scale)[:BLOCK]


VMEM = pl.BlockSpec(memory_space=pltpu.VMEM)
SMEM = pl.BlockSpec(memory_space=pltpu.SMEM)
HBM = pl.BlockSpec(memory_space=pltpu.HBM)


def call(kernel, operands, in_specs, outs, scratch=(), flops=0, moved=1 << 20, limit=4):
    return pl.pallas_call(
        kernel,
        out_shape=[jax.ShapeDtypeStruct(shape, dtype) for shape, dtype in outs],
        in_specs=in_specs,
        out_specs=[VMEM] * len(outs),
        scratch_shapes=[
            pltpu.VMEM(*one) if isinstance(one, tuple) else one for one in scratch
        ],
        compiler_params=pltpu.CompilerParams(vmem_limit_bytes=limit << 20),
        cost_estimate=pl.CostEstimate(flops=flops, bytes_accessed=moved, transcendentals=0),
    )(*operands)


CONV_FLOPS = 2 * F * POS * 27 * C * C
WIDE = ((9 * C, 3 * C), BF16)


def frame_shape(count, dtype=BF16):
    return ((count, POS, C), dtype)


def shifted(value, steps):
    return seq_permute(value, lambda z: z + steps)


def dp_permute(value, target):
    return lax.ppermute(value, "dp", [(source, target(source)) for source in range(32)])


def along_x(step):
    return lambda d: (d // 8) * 8 + (d % 8 + 2 * step) % 8


def along_y(step):
    return lambda d: (d + 8 * step) % 32


def crossed(first, second):
    return lambda d: second(d) if d % 2 else first(d)


def seq_permute(value, target):
    return lax.ppermute(value, "seq", [(source, target(source) % 8) for source in range(8)])


def per_device(frames, clip_ids, cotangent, conv1_weight, conv2_weight):
    own_frames = frames.reshape(F, POS, C)
    own_cot = cotangent.reshape(F, POS, C)
    clip_ids, own_frames, own_cot, conv1_weight, conv2_weight = (
        pltpu.with_memory_space_constraint(value, pltpu.HBM)
        for value in (clip_ids, own_frames, own_cot, conv1_weight, conv2_weight)
    )
    clip_ids, tail, head = call(
        halo_kernel,
        (clip_ids, own_frames, own_cot),
        [HBM, HBM, HBM],
        [(clip_ids.shape, jnp.int32), frame_shape(4), frame_shape(6)],
        [pltpu.SemaphoreType.DMA((4,))],
    )
    head = shifted(head, -1)
    tail = shifted(tail, 1)
    local = call(
        local_kernel,
        (clip_ids, own_frames, own_cot, conv1_weight, conv2_weight),
        [SMEM, HBM, HBM, HBM, HBM],
        [
            frame_shape(F + 1),
            frame_shape(F + 1),
            ((27 * C, C), BF16),
            ((27 * C, C), BF16),
            WIDE,
            WIDE,
            frame_shape(F, F32),
            frame_shape(F, F32),
        ],
        [pltpu.SemaphoreType.DMA((4,))],
        flops=CONV_FLOPS * 3 // 2,
        limit=16,
    )
    tail, head, local = lax.optimization_barrier((tail, head, local))
    frame_copy, cot_copy, weight1, weight2, conv_weight, back_weight, act, back = local
    block = ((2, 16, PADDED, C), F32)
    hidden, act_grad, keep, send = call(
        main_kernel,
        (clip_ids, frame_copy, cot_copy, tail, head, conv_weight, back_weight, act, back),
        [SMEM] + [VMEM] * 8,
        [frame_shape(F), frame_shape(F), block, (block[0], BF16)],
        [
            frame_shape(F + 3),
            frame_shape(F + 3),
            frame_shape(F, F32),
            frame_shape(F, F32),
            ((F + 3, POS, 3 * C), BF16),
            ((F * POS, 9 * C), BF16),
            ((F + 3, 3 * C, POS), BF16),
            ((9 * C, F * POS), BF16),
            ((3 * C, F * POS), BF16),
            ((F * POS, 3 * C), BF16),
            ((2, 27 * C, C), F32),
        ],
        flops=CONV_FLOPS * 5 // 2,
        limit=40,
    )
    recv = dp_permute(send, lambda d: d ^ 1)
    head, keep = lax.optimization_barrier((head, keep))
    (act_grad_next,) = call(
        next_grad_kernel,
        (clip_ids, frame_copy, head, conv_weight, back_weight),
        [SMEM] + [VMEM] * 4,
        [frame_shape(2)],
        [frame_shape(5), frame_shape(5), frame_shape(2, F32), frame_shape(2, F32)],
        flops=CONV_FLOPS // 2,
        limit=8,
    )
    recv, act_grad_next = lax.optimization_barrier((recv, act_grad_next))
    keep, *sent = call(
        first_kernel,
        (keep, recv),
        [VMEM] * 2,
        [((2, 4, PADDED, C), F32)] + [((2, 4, PADDED, C), BF16)] * 3,
    )
    sent, hidden = lax.optimization_barrier((sent, hidden))
    recv = [
        dp_permute(part, crossed(along_x(s), along_y(s))) for s, part in zip((1, 2, 3), sent)
    ]
    (block_out,) = call(
        forward_kernel,
        (clip_ids, hidden, frame_copy, tail, conv_weight, weight2),
        [SMEM] + [VMEM] * 5,
        [frame_shape(F)],
        [frame_shape(5), frame_shape(2, F32), frame_shape(F + 3), WIDE],
        flops=CONV_FLOPS * 5 // 4,
        limit=12,
    )
    recv, block_out = lax.optimization_barrier((recv, block_out))
    pair = (2, PADDED, C)
    keep, *sent = call(
        second_kernel, (keep, *recv), [VMEM] * 4, [(pair, F32)] + [(pair, BF16)] * 3
    )
    recv = [
        dp_permute(part, crossed(along_y(s), along_x(s))) for s, part in zip((1, 2, 3), sent)
    ]
    (total,) = call(sum_kernel, (keep, *recv), [VMEM] * 4, [(pair, BF16)])
    other = seq_permute(total, lambda z: z ^ 1)
    (total,) = call(sum_kernel, (total, other), [VMEM] * 2, [(pair, BF16)])
    total, act_grad = lax.optimization_barrier((total, act_grad))
    others = [
        seq_permute(total, lambda z, s=s: z + s if z % 2 else z - s) for s in (1, 2, 3)
    ]
    (input_grad,) = call(
        backward_kernel,
        (clip_ids, act_grad, act_grad_next, cot_copy, weight1),
        [SMEM] + [VMEM] * 4,
        [frame_shape(F)],
        [frame_shape(F + 3), WIDE],
        flops=CONV_FLOPS,
        limit=8,
    )
    others, input_grad = lax.optimization_barrier((others, input_grad))
    rows = lax.axis_size("dp") * lax.axis_size("seq") * F * POS
    first_grad, second_grad = call(
        lambda *refs: last_kernel(rows**-0.5, *refs),
        (total, *others),
        [VMEM] * 4,
        [((BLOCK, C), F32)] * 2,
    )
    return (
        block_out.reshape(frames.shape),
        input_grad.reshape(frames.shape),
        first_grad,
        second_grad,
    )


def solution(mesh):
    return jax.shard_map(
        per_device,
        mesh=mesh,
        in_specs=(
            P("dp", "seq", None, None, None),
            P("dp", None),
            P("dp", "seq", None, None, None),
            P(),
            P(),
        ),
        out_specs=(
            P("dp", "seq", None, None, None),
            P("dp", "seq", None, None, None),
            P("dp", None),
            P("dp", None),
        ),
        check_vma=False,
    )
```

```python
import jax
import jax.numpy as jnp
from jax import lax
from jax.experimental import pallas as pl
from jax.experimental.pallas import tpu as pltpu
from jax.sharding import PartitionSpec as P

C = 128
GROUP = 4
F = 8
HT = 8
WT = 32
POS = HT * WT
BLOCK = 108
PADDED = 112
BF16 = jnp.bfloat16
F32 = jnp.float32


def clip_at(clips, frame):
    return clips[0, jnp.clip(frame, 0, clips.shape[1] - 1)]


def past_slots(clips, first, t, base, none):
    slots = []
    for k in range(3):
        frame = first + t + k - 2
        same = clip_at(clips, frame) == clip_at(clips, first + t)
        slots.append(jnp.where(same & (frame >= 0), t + k - 2 + base, none))
    return slots


def next_slots(clips, first, t, base, none):
    slots = []
    for q in range(3):
        frame = first + t + q
        same = clip_at(clips, frame) == clip_at(clips, first + t)
        slots.append(jnp.where(same & (frame < clips.shape[1]), t + q + base, none))
    return slots


def column(rows):
    return lax.broadcasted_iota(jnp.int32, (rows, C), 0) % WT


def shift_down(value):
    return jnp.where(column(POS) == 0, 0.0, pltpu.roll(value, 1, 0))


def shift_up(value):
    return jnp.where(column(POS) == WT - 1, 0.0, pltpu.roll(value, POS - 1, 0))


def row_pieces(frame):
    edge = jnp.zeros((WT, C), frame.dtype)
    return [
        jnp.concatenate([edge, frame[: POS - WT]], axis=0),
        frame,
        jnp.concatenate([frame[WT:], edge], axis=0),
    ]


def column_pieces(frame):
    wide = frame.astype(F32)
    return jnp.concatenate([shift_up(wide).astype(BF16), frame, shift_down(wide).astype(BF16)], axis=1)


def conv_frame(window, slots, weight):
    pieces = []
    for slot in slots:
        pieces += row_pieces(window[slot])
    taps = jnp.dot(jnp.concatenate(pieces, axis=1), weight[...], preferred_element_type=F32)
    return shift_down(taps[:, :C]) + taps[:, C : 2 * C] + shift_up(taps[:, 2 * C :])


def forward_weight(weight_ref, out_ref):
    for outer in range(9):
        for b in range(3):
            out_ref[outer * C : (outer + 1) * C, b * C : (b + 1) * C] = weight_ref[
                (outer * 3 + b) * C : (outer * 3 + b + 1) * C, :
            ]


def adjoint_weight(weight_ref, out_ref):
    for outer in range(9):
        for b in range(3):
            tap = 26 - (outer * 3 + b)
            out_ref[outer * C : (outer + 1) * C, b * C : (b + 1) * C] = weight_ref[
                tap * C : (tap + 1) * C, :
            ].T


def group_mean(sums):
    count = len(sums)
    sums = jnp.concatenate(sums + [jnp.zeros_like(sums[0])] * (F - count), axis=0)
    lane = lax.broadcasted_iota(jnp.int32, sums.shape, 1)
    pairs = sums + jnp.where(lane % 2 == 0, pltpu.roll(sums, C - 1, 1), pltpu.roll(sums, 1, 1))
    quads = pairs + jnp.where(lane % 4 < 2, pltpu.roll(pairs, C - 2, 1), pltpu.roll(pairs, 2, 1))
    mean = quads * (1.0 / (GROUP * POS))
    return [mean[t : t + 1] for t in range(count)]


def tile_sum(value):
    return jnp.sum(value, axis=0, keepdims=True)


def normalize(act, count):
    center = group_mean([tile_sum(act[t]) for t in range(count)])
    sums = []
    for t in range(count):
        away = act[t] - center[t]
        act[t] = away
        sums.append(tile_sum(away * away))
    scale = [lax.rsqrt(mean + 1e-06) for mean in group_mean(sums)]
    for t in range(count):
        act[t] = act[t] * scale[t]
    return scale


def gate_of(normed):
    return 1.0 / (1.0 + jnp.exp(-normed))


def hidden_of(normed):
    return (normed * gate_of(normed)).astype(BF16)


def norm_adjoint(act, back, scale, work):
    count = len(scale)
    first, second = [], []
    for t in range(count):
        normed = act(t)
        gate = gate_of(normed)
        grad = back(t) * (gate * (1.0 + normed * (1.0 - gate)))
        work[t] = grad
        first.append(tile_sum(grad))
        second.append(tile_sum(grad * normed))
    first, second = group_mean(first), group_mean(second)
    return [(scale[t] * (work[t] - first[t] - act(t) * second[t])).astype(BF16) for t in range(count)]


def first_frame():
    return lax.axis_index("seq") * F


def halo_kernel(clips, frames, cot, clips_copy, tail, head, sems):
    copies = [
        pltpu.make_async_copy(clips, clips_copy, sems.at[3]),
        pltpu.make_async_copy(frames.at[F - 4 :], tail, sems.at[0]),
        pltpu.make_async_copy(frames.at[:2], head.at[:2], sems.at[1]),
        pltpu.make_async_copy(cot.at[:4], head.at[2:], sems.at[2]),
    ]
    for copy in copies:
        copy.start()
    for copy in copies:
        copy.wait()


EDGE = F - 2


def local_kernel(
    clips,
    frames,
    cot,
    weight1,
    weight2,
    window,
    cot_window,
    weight1_copy,
    weight2_copy,
    conv_weight,
    back_weight,
    act,
    back,
    scales,
    hidden,
    frame_t,
    cot_shifted,
    second_part,
    hidden_t,
    cot_taps,
    sems,
):
    copies = [
        pltpu.make_async_copy(weight1, weight1_copy, sems.at[0]),
        pltpu.make_async_copy(frames, window.at[:F], sems.at[1]),
        pltpu.make_async_copy(weight2, weight2_copy, sems.at[2]),
        pltpu.make_async_copy(cot, cot_window.at[:F], sems.at[3]),
    ]
    for copy in copies:
        copy.start()
    window[F] = jnp.zeros((POS, C), BF16)
    cot_window[F] = jnp.zeros((POS, C), BF16)
    frame_t[F] = jnp.zeros((3 * C, POS), BF16)
    cot_shifted[F] = jnp.zeros((POS, 3 * C), BF16)
    first = first_frame()
    copies[0].wait()
    forward_weight(weight1_copy, conv_weight)
    for copy in copies[1:]:
        copy.wait()
    for t in range(2, F):
        act[t] = conv_frame(window, past_slots(clips, first, t, 0, F), conv_weight)
    adjoint_weight(weight2_copy, back_weight)
    for f in range(F):
        cot_shifted[f] = column_pieces(cot_window[f])
        for a, piece in enumerate(row_pieces(window[f])):
            frame_t[f, a * C : (a + 1) * C, :] = piece.T
    for t in range(EDGE):
        back[t] = conv_frame(cot_window, next_slots(clips, first, t, 0, F), back_weight)
    for t, scale in enumerate(normalize(act.at[2:F], F - 2)):
        scales[2 + t : 3 + t] = scale
    for t in range(2, F):
        value = hidden_of(act[t])
        hidden[t] = value
        if t < EDGE:
            place = slice((t - 2) * POS, (t - 1) * POS)
            for a, piece in enumerate(row_pieces(value)):
                hidden_t[a * C : (a + 1) * C, place] = piece.T
            slots = next_slots(clips, first, t, 0, F)
            for k in range(3):
                cot_taps[place, 3 * C * k : 3 * C * (k + 1)] = cot_shifted[slots[2 - k]]
    second_part[...] = jnp.dot(hidden_t[...], cot_taps[...], preferred_element_type=F32)


def split_rows(grads, g, keep_ref, send_ref):
    own = lax.rem(lax.axis_index("dp"), 2) == 0
    for m in range(16):
        low = grads[g, 2 * BLOCK * m : 2 * BLOCK * m + BLOCK]
        high = grads[g, 2 * BLOCK * m + BLOCK : 2 * BLOCK * (m + 1)]
        keep_ref[g, m, :BLOCK] = jnp.where(own, low, high)
        keep_ref[g, m, BLOCK:] = jnp.zeros((PADDED - BLOCK, C), F32)
        send_ref[g, m, :BLOCK] = jnp.where(own, high, low).astype(BF16)
        send_ref[g, m, BLOCK:] = jnp.zeros((PADDED - BLOCK, C), BF16)


def main_kernel(
    clips,
    frames,
    cot,
    tail,
    head,
    conv_weight,
    back_weight,
    act_in,
    back_in,
    scales,
    hidden_in,
    frame_t_in,
    cot_shifted_in,
    second_part,
    hidden_ref,
    act_grad_ref,
    keep_ref,
    send_ref,
    window,
    cot_window,
    act,
    back,
    work,
    cot_shifted,
    cot_taps,
    frame_t,
    frame_taps,
    hidden_t,
    grad_shifted,
    grads,
):
    first = first_frame()
    zero = jnp.zeros((POS, C), BF16)
    for f in range(2):
        window[f] = tail[2 + f]
        window[2 + f] = frames[f]
        cot_window[f] = cot[EDGE + f]
        cot_window[2 + f] = head[2 + f]
    window[4] = zero
    cot_window[4] = zero

    for t in range(2):
        act[t] = conv_frame(window, past_slots(clips, first, t, 2, 4), conv_weight)
        back[t] = conv_frame(
            cot_window, next_slots(clips, first, EDGE + t, -EDGE, 4), back_weight
        )
    for f in range(2):
        cot_shifted[f] = column_pieces(cot_window[2 + f])
        for a, piece in enumerate(row_pieces(window[f])):
            frame_t[f, a * C : (a + 1) * C, :] = piece.T
    cot_shifted[2] = jnp.zeros((POS, 3 * C), BF16)
    frame_t[2] = jnp.zeros((3 * C, POS), BF16)
    scale = normalize(act, 2) + [scales[t : t + 1] for t in range(2, F)]
    for t in range(F):
        hidden_ref[t] = hidden_of(act[t]) if t < 2 else hidden_in[t]

    for n, s in enumerate((0, 1, EDGE, EDGE + 1)):
        place = slice(n * POS, (n + 1) * POS)
        for a, piece in enumerate(row_pieces(hidden_ref[s])):
            hidden_t[a * C : (a + 1) * C, place] = piece.T
        near = next_slots(clips, first, s, 0, F)
        far = next_slots(clips, first, s, -F, 2)
        for k in range(3):
            cot_taps[place, 3 * C * k : 3 * C * (k + 1)] = (
                cot_shifted_in[near[2 - k]] if s + 2 - k < F else cot_shifted[far[2 - k]]
            )
    second_grad = second_part[...] + jnp.dot(
        hidden_t[...], cot_taps[...], preferred_element_type=F32
    )
    for k in range(3):
        for a in range(3):
            for b in range(3):
                tap = (k * 3 + a) * 3 + b
                grads[1, tap * C : (tap + 1) * C] = second_grad[
                    a * C : (a + 1) * C, (k * 3 + b) * C : (k * 3 + b + 1) * C
                ]

    rounded = norm_adjoint(
        lambda t: act[t] if t < 2 else act_in[t],
        lambda t: back_in[t] if t < EDGE else back[t - EDGE],
        scale,
        work,
    )
    for t in range(F):
        act_grad_ref[t] = rounded[t]
        grad_shifted[t * POS : (t + 1) * POS] = column_pieces(rounded[t])
        near = past_slots(clips, first, t, 0, F)
        far = past_slots(clips, first, t, 2, 2)
        for k in range(3):
            frame_taps[3 * C * k : 3 * C * (k + 1), t * POS : (t + 1) * POS] = (
                frame_t_in[near[k]] if t + k - 2 >= 0 else frame_t[far[k]]
            )
    split_rows(grads, 1, keep_ref, send_ref)
    first_grad = jnp.dot(frame_taps[...], grad_shifted[...], preferred_element_type=F32)
    for outer in range(9):
        for b in range(3):
            tap = outer * 3 + b
            grads[0, tap * C : (tap + 1) * C] = first_grad[
                outer * C : (outer + 1) * C, b * C : (b + 1) * C
            ]
    split_rows(grads, 0, keep_ref, send_ref)


def forward_kernel(
    clips, hidden_in, frames, tail, conv_weight, weight2, out_ref, window, act, hidden, weight
):
    first = first_frame()
    for f in range(4):
        window[f] = tail[f]
    window[4] = jnp.zeros((POS, C), BF16)
    for t in range(2):
        act[t] = conv_frame(window, past_slots(clips, first, t - 2, 4, 4), conv_weight)
    normalize(act, 2)
    for t in range(2):
        hidden[t] = hidden_of(act[t])
    for f in range(F):
        hidden[2 + f] = hidden_in[f]
    hidden[F + 2] = jnp.zeros((POS, C), BF16)
    forward_weight(weight2, weight)
    for t in range(F):
        out = conv_frame(hidden, past_slots(clips, first, t, 2, F + 2), weight)
        out_ref[t] = (frames[t].astype(F32) + out).astype(BF16)


def next_grad_kernel(
    clips, frames, head, conv_weight, back_weight, out_ref, window, cot_window, act, back
):
    first = first_frame()
    zero = jnp.zeros((POS, C), BF16)
    for f in range(2):
        window[f] = frames[F - 2 + f]
        window[2 + f] = head[f]
    for f in range(4):
        cot_window[f] = head[2 + f]
    window[4] = zero
    cot_window[4] = zero
    for t in range(2):
        act[t] = conv_frame(window, past_slots(clips, first, F + t, 2 - F, 4), conv_weight)
        back[t] = conv_frame(cot_window, next_slots(clips, first, F + t, -F, 4), back_weight)
    scale = normalize(act, 2)
    for t, rounded in enumerate(
        norm_adjoint(lambda t: act[t], lambda t: back[t], scale, back)
    ):
        out_ref[t] = rounded


def backward_kernel(clips, act_grad_in, next_in, cot, weight1, out_ref, act_grad, weight):
    first = first_frame()
    for f in range(F):
        act_grad[f] = act_grad_in[f]
    for f in range(2):
        act_grad[F + f] = next_in[f]
    act_grad[F + 2] = jnp.zeros((POS, C), BF16)
    adjoint_weight(weight1, weight)
    for t in range(F):
        out = conv_frame(act_grad, next_slots(clips, first, t, 0, F + 2), weight)
        out_ref[t] = (cot[t].astype(F32) + out).astype(BF16)


def place():
    index = lax.axis_index("dp")
    return lax.div(index, 8), lax.rem(lax.div(index, 2), 4), lax.rem(index, 2) == 0


def first_kernel(keep_ref, part, kept_ref, *sent_refs):
    y, x, along_x = place()
    for g in range(2):
        for other in range(4):
            for step in range(4):
                block = jnp.where(
                    along_x, 4 * other + lax.rem(x + step, 4), 4 * lax.rem(y + step, 4) + other
                )
                total = keep_ref[g, block] + part[g, block].astype(F32)
                if step == 0:
                    kept_ref[g, other] = total
                else:
                    sent_refs[step - 1][g, other] = total.astype(BF16)


def second_kernel(keep_ref, *refs):
    received, (kept_ref, *sent_refs) = refs[:3], refs[3:]
    y, x, along_x = place()
    own = jnp.where(along_x, y, x)
    for g in range(2):
        for step in range(4):
            block = lax.rem(own + step, 4)
            total = keep_ref[g, block]
            for part in received:
                total = total + part[g, block].astype(F32)
            if step == 0:
                kept_ref[g] = total
            else:
                sent_refs[step - 1][g] = total.astype(BF16)


def sum_kernel(keep_ref, *refs):
    received, out_ref = refs[:-1], refs[-1]
    total = keep_ref[...].astype(F32)
    for part in received:
        total = total + part[...].astype(F32)
    out_ref[...] = total.astype(BF16)


def last_kernel(scale, own, near, next_near, far, first_ref, second_ref):
    for g, out_ref in enumerate((first_ref, second_ref)):
        total = (own[g].astype(F32) + far[g].astype(F32)) + (
            near[g].astype(F32) + next_near[g].astype(F32)
        )
        out_ref[...] = (total * scale)[:BLOCK]


VMEM = pl.BlockSpec(memory_space=pltpu.VMEM)
SMEM = pl.BlockSpec(memory_space=pltpu.SMEM)
HBM = pl.BlockSpec(memory_space=pltpu.HBM)


def call(kernel, operands, in_specs, outs, scratch=(), flops=0, moved=1 << 20, limit=4):
    return pl.pallas_call(
        kernel,
        out_shape=[jax.ShapeDtypeStruct(shape, dtype) for shape, dtype in outs],
        in_specs=in_specs,
        out_specs=[VMEM] * len(outs),
        scratch_shapes=[
            pltpu.VMEM(*one) if isinstance(one, tuple) else one for one in scratch
        ],
        compiler_params=pltpu.CompilerParams(vmem_limit_bytes=limit << 20),
        cost_estimate=pl.CostEstimate(flops=flops, bytes_accessed=moved, transcendentals=0),
    )(*operands)


CONV_FLOPS = 2 * F * POS * 27 * C * C
WIDE = ((9 * C, 3 * C), BF16)


def frame_shape(count, dtype=BF16):
    return ((count, POS, C), dtype)


def shifted(value, steps):
    return seq_permute(value, lambda z: z + steps)


def dp_permute(value, target):
    return lax.ppermute(value, "dp", [(source, target(source)) for source in range(32)])


def along_x(step):
    return lambda d: (d // 8) * 8 + (d % 8 + 2 * step) % 8


def along_y(step):
    return lambda d: (d + 8 * step) % 32


def crossed(first, second):
    return lambda d: second(d) if d % 2 else first(d)


def seq_permute(value, target):
    return lax.ppermute(value, "seq", [(source, target(source) % 8) for source in range(8)])


def per_device(frames, clip_ids, cotangent, conv1_weight, conv2_weight):
    own_frames = frames.reshape(F, POS, C)
    own_cot = cotangent.reshape(F, POS, C)
    clip_ids, own_frames, own_cot, conv1_weight, conv2_weight = (
        pltpu.with_memory_space_constraint(value, pltpu.HBM)
        for value in (clip_ids, own_frames, own_cot, conv1_weight, conv2_weight)
    )
    clip_ids, tail, head = call(
        halo_kernel,
        (clip_ids, own_frames, own_cot),
        [HBM, HBM, HBM],
        [(clip_ids.shape, jnp.int32), frame_shape(4), frame_shape(6)],
        [pltpu.SemaphoreType.DMA((4,))],
    )
    head = shifted(head, -1)
    tail = shifted(tail, 1)
    local = call(
        local_kernel,
        (clip_ids, own_frames, own_cot, conv1_weight, conv2_weight),
        [SMEM, HBM, HBM, HBM, HBM],
        [
            frame_shape(F + 1),
            frame_shape(F + 1),
            ((27 * C, C), BF16),
            ((27 * C, C), BF16),
            WIDE,
            WIDE,
            frame_shape(F, F32),
            frame_shape(F, F32),
            ((F, C), F32),
            frame_shape(F),
            ((F + 1, 3 * C, POS), BF16),
            ((F + 1, POS, 3 * C), BF16),
            ((3 * C, 9 * C), F32),
        ],
        [
            ((3 * C, 4 * POS), BF16),
            ((4 * POS, 9 * C), BF16),
            pltpu.SemaphoreType.DMA((4,)),
        ],
        flops=CONV_FLOPS * 2,
        limit=16,
    )
    tail, head, local = lax.optimization_barrier((tail, head, local))
    frame_copy, cot_copy, weight1, weight2, conv_weight, back_weight, *partial = local
    block = ((2, 16, PADDED, C), F32)
    hidden, act_grad, keep, send = call(
        main_kernel,
        (clip_ids, frame_copy, cot_copy, tail, head, conv_weight, back_weight, *partial),
        [SMEM] + [VMEM] * 13,
        [frame_shape(F), frame_shape(F), block, (block[0], BF16)],
        [
            frame_shape(5),
            frame_shape(5),
            frame_shape(2, F32),
            frame_shape(2, F32),
            frame_shape(F, F32),
            ((3, POS, 3 * C), BF16),
            ((4 * POS, 9 * C), BF16),
            ((3, 3 * C, POS), BF16),
            ((9 * C, F * POS), BF16),
            ((3 * C, 4 * POS), BF16),
            ((F * POS, 3 * C), BF16),
            ((2, 27 * C, C), F32),
        ],
        flops=CONV_FLOPS * 2,
        limit=32,
    )
    recv = dp_permute(send, lambda d: d ^ 1)
    head, keep = lax.optimization_barrier((head, keep))
    (act_grad_next,) = call(
        next_grad_kernel,
        (clip_ids, frame_copy, head, conv_weight, back_weight),
        [SMEM] + [VMEM] * 4,
        [frame_shape(2)],
        [frame_shape(5), frame_shape(5), frame_shape(2, F32), frame_shape(2, F32)],
        flops=CONV_FLOPS // 2,
        limit=8,
    )
    recv, act_grad_next = lax.optimization_barrier((recv, act_grad_next))
    keep, *sent = call(
        first_kernel,
        (keep, recv),
        [VMEM] * 2,
        [((2, 4, PADDED, C), F32)] + [((2, 4, PADDED, C), BF16)] * 3,
    )
    sent, hidden = lax.optimization_barrier((sent, hidden))
    recv = [
        dp_permute(part, crossed(along_x(s), along_y(s))) for s, part in zip((1, 2, 3), sent)
    ]
    (block_out,) = call(
        forward_kernel,
        (clip_ids, hidden, frame_copy, tail, conv_weight, weight2),
        [SMEM] + [VMEM] * 5,
        [frame_shape(F)],
        [frame_shape(5), frame_shape(2, F32), frame_shape(F + 3), WIDE],
        flops=CONV_FLOPS * 5 // 4,
        limit=12,
    )
    recv, block_out = lax.optimization_barrier((recv, block_out))
    pair = (2, PADDED, C)
    keep, *sent = call(
        second_kernel, (keep, *recv), [VMEM] * 4, [(pair, F32)] + [(pair, BF16)] * 3
    )
    recv = [
        dp_permute(part, crossed(along_y(s), along_x(s))) for s, part in zip((1, 2, 3), sent)
    ]
    (total,) = call(sum_kernel, (keep, *recv), [VMEM] * 4, [(pair, BF16)])
    other = seq_permute(total, lambda z: z ^ 1)
    (total,) = call(sum_kernel, (total, other), [VMEM] * 2, [(pair, BF16)])
    total, act_grad = lax.optimization_barrier((total, act_grad))
    others = [
        seq_permute(total, lambda z, s=s: z + s if z % 2 else z - s) for s in (1, 2, 3)
    ]
    (input_grad,) = call(
        backward_kernel,
        (clip_ids, act_grad, act_grad_next, cot_copy, weight1),
        [SMEM] + [VMEM] * 4,
        [frame_shape(F)],
        [frame_shape(F + 3), WIDE],
        flops=CONV_FLOPS,
        limit=8,
    )
    others, input_grad = lax.optimization_barrier((others, input_grad))
    rows = lax.axis_size("dp") * lax.axis_size("seq") * F * POS
    first_grad, second_grad = call(
        lambda *refs: last_kernel(rows**-0.5, *refs),
        (total, *others),
        [VMEM] * 4,
        [((BLOCK, C), F32)] * 2,
    )
    return (
        block_out.reshape(frames.shape),
        input_grad.reshape(frames.shape),
        first_grad,
        second_grad,
    )


def solution(mesh):
    return jax.shard_map(
        per_device,
        mesh=mesh,
        in_specs=(
            P("dp", "seq", None, None, None),
            P("dp", None),
            P("dp", "seq", None, None, None),
            P(),
            P(),
        ),
        out_specs=(
            P("dp", "seq", None, None, None),
            P("dp", "seq", None, None, None),
            P("dp", None),
            P("dp", None),
        ),
        check_vma=False,
    )
```

```python
import jax
import jax.numpy as jnp
from jax import lax
from jax.experimental import pallas as pl
from jax.experimental.pallas import tpu as pltpu
from jax.sharding import PartitionSpec as P

C = 128
GROUP = 4
F = 8
HT = 8
WT = 32
POS = HT * WT
BLOCK = 108
PADDED = 112
BF16 = jnp.bfloat16
F32 = jnp.float32


def clip_at(clips, frame):
    return clips[0, jnp.clip(frame, 0, clips.shape[1] - 1)]


def past_slots(clips, first, t, base, none):
    slots = []
    for k in range(3):
        frame = first + t + k - 2
        same = clip_at(clips, frame) == clip_at(clips, first + t)
        slots.append(jnp.where(same & (frame >= 0), t + k - 2 + base, none))
    return slots


def next_slots(clips, first, t, base, none):
    slots = []
    for q in range(3):
        frame = first + t + q
        same = clip_at(clips, frame) == clip_at(clips, first + t)
        slots.append(jnp.where(same & (frame < clips.shape[1]), t + q + base, none))
    return slots


def column(rows):
    return lax.broadcasted_iota(jnp.int32, (rows, C), 0) % WT


def shift_down(value):
    return jnp.where(column(POS) == 0, 0.0, pltpu.roll(value, 1, 0))


def shift_up(value):
    return jnp.where(column(POS) == WT - 1, 0.0, pltpu.roll(value, POS - 1, 0))


def row_pieces(frame):
    edge = jnp.zeros((WT, C), frame.dtype)
    return [
        jnp.concatenate([edge, frame[: POS - WT]], axis=0),
        frame,
        jnp.concatenate([frame[WT:], edge], axis=0),
    ]


def column_pieces(frame):
    wide = frame.astype(F32)
    return jnp.concatenate([shift_up(wide).astype(BF16), frame, shift_down(wide).astype(BF16)], axis=1)


def conv_frame(window, slots, weight):
    pieces = []
    for slot in slots:
        pieces += row_pieces(window[slot])
    taps = jnp.dot(jnp.concatenate(pieces, axis=1), weight[...], preferred_element_type=F32)
    return shift_down(taps[:, :C]) + taps[:, C : 2 * C] + shift_up(taps[:, 2 * C :])


def forward_weight(weight_ref, out_ref):
    for outer in range(9):
        for b in range(3):
            out_ref[outer * C : (outer + 1) * C, b * C : (b + 1) * C] = weight_ref[
                (outer * 3 + b) * C : (outer * 3 + b + 1) * C, :
            ]


def adjoint_weight(weight_ref, out_ref):
    for outer in range(9):
        for b in range(3):
            tap = 26 - (outer * 3 + b)
            out_ref[outer * C : (outer + 1) * C, b * C : (b + 1) * C] = weight_ref[
                tap * C : (tap + 1) * C, :
            ].T


def group_mean(sums):
    count = len(sums)
    sums = jnp.concatenate(sums + [jnp.zeros_like(sums[0])] * (F - count), axis=0)
    lane = lax.broadcasted_iota(jnp.int32, sums.shape, 1)
    pairs = sums + jnp.where(lane % 2 == 0, pltpu.roll(sums, C - 1, 1), pltpu.roll(sums, 1, 1))
    quads = pairs + jnp.where(lane % 4 < 2, pltpu.roll(pairs, C - 2, 1), pltpu.roll(pairs, 2, 1))
    mean = quads * (1.0 / (GROUP * POS))
    return [mean[t : t + 1] for t in range(count)]


def tile_sum(value):
    return jnp.sum(value, axis=0, keepdims=True)


def normalize(act, count):
    center = group_mean([tile_sum(act[t]) for t in range(count)])
    sums = []
    for t in range(count):
        away = act[t] - center[t]
        act[t] = away
        sums.append(tile_sum(away * away))
    scale = [lax.rsqrt(mean + 1e-06) for mean in group_mean(sums)]
    for t in range(count):
        act[t] = act[t] * scale[t]
    return scale


def gate_of(normed):
    return 1.0 / (1.0 + jnp.exp(-normed))


def hidden_of(normed):
    return (normed * gate_of(normed)).astype(BF16)


def norm_adjoint(act, back, scale, work):
    count = len(scale)
    first, second = [], []
    for t in range(count):
        normed = act(t)
        gate = gate_of(normed)
        grad = back(t) * (gate * (1.0 + normed * (1.0 - gate)))
        work[t] = grad
        first.append(tile_sum(grad))
        second.append(tile_sum(grad * normed))
    first, second = group_mean(first), group_mean(second)
    return [(scale[t] * (work[t] - first[t] - act(t) * second[t])).astype(BF16) for t in range(count)]


def first_frame():
    return lax.axis_index("seq") * F


def halo_kernel(clips, frames, cot, weight1, clips_copy, tail, head, weight1_copy, sems):
    copies = [
        pltpu.make_async_copy(weight1, weight1_copy, sems.at[4]),
        pltpu.make_async_copy(clips, clips_copy, sems.at[3]),
        pltpu.make_async_copy(frames.at[F - 4 :], tail, sems.at[0]),
        pltpu.make_async_copy(frames.at[:2], head.at[:2], sems.at[1]),
        pltpu.make_async_copy(cot.at[:4], head.at[2:], sems.at[2]),
    ]
    for copy in copies:
        copy.start()
    for copy in copies:
        copy.wait()


EDGE = F - 2


def local_kernel(
    clips,
    frames,
    cot,
    weight1,
    weight2,
    window,
    cot_window,
    weight2_copy,
    conv_weight,
    back_weight,
    act,
    back,
    scales,
    hidden,
    frame_t,
    cot_shifted,
    second_part,
    hidden_t,
    cot_taps,
    sems,
):
    copies = [
        pltpu.make_async_copy(frames, window.at[:F], sems.at[0]),
        pltpu.make_async_copy(weight2, weight2_copy, sems.at[1]),
        pltpu.make_async_copy(cot, cot_window.at[:F], sems.at[2]),
    ]
    for copy in copies:
        copy.start()
    window[F] = jnp.zeros((POS, C), BF16)
    cot_window[F] = jnp.zeros((POS, C), BF16)
    frame_t[F] = jnp.zeros((3 * C, POS), BF16)
    cot_shifted[F] = jnp.zeros((POS, 3 * C), BF16)
    first = first_frame()
    forward_weight(weight1, conv_weight)
    for copy in copies:
        copy.wait()
    for t in range(2, F):
        act[t] = conv_frame(window, past_slots(clips, first, t, 0, F), conv_weight)
    adjoint_weight(weight2_copy, back_weight)
    for f in range(F):
        cot_shifted[f] = column_pieces(cot_window[f])
        for a, piece in enumerate(row_pieces(window[f])):
            frame_t[f, a * C : (a + 1) * C, :] = piece.T
    for t in range(EDGE):
        back[t] = conv_frame(cot_window, next_slots(clips, first, t, 0, F), back_weight)
    for t, scale in enumerate(normalize(act.at[2:F], F - 2)):
        scales[2 + t : 3 + t] = scale
    for t in range(2, F):
        value = hidden_of(act[t])
        hidden[t] = value
        if t < EDGE:
            place = slice((t - 2) * POS, (t - 1) * POS)
            for a, piece in enumerate(row_pieces(value)):
                hidden_t[a * C : (a + 1) * C, place] = piece.T
            slots = next_slots(clips, first, t, 0, F)
            for k in range(3):
                cot_taps[place, 3 * C * k : 3 * C * (k + 1)] = cot_shifted[slots[2 - k]]
    second_part[...] = jnp.dot(hidden_t[...], cot_taps[...], preferred_element_type=F32)


def split_rows(grads, g, keep_ref, send_ref):
    own = lax.rem(lax.axis_index("dp"), 2) == 0
    for m in range(16):
        low = grads[g, 2 * BLOCK * m : 2 * BLOCK * m + BLOCK]
        high = grads[g, 2 * BLOCK * m + BLOCK : 2 * BLOCK * (m + 1)]
        keep_ref[g, m, :BLOCK] = jnp.where(own, low, high)
        keep_ref[g, m, BLOCK:] = jnp.zeros((PADDED - BLOCK, C), F32)
        send_ref[g, m, :BLOCK] = jnp.where(own, high, low).astype(BF16)
        send_ref[g, m, BLOCK:] = jnp.zeros((PADDED - BLOCK, C), BF16)


def main_kernel(
    clips,
    frames,
    cot,
    tail,
    head,
    conv_weight,
    back_weight,
    act_in,
    back_in,
    scales,
    hidden_in,
    frame_t_in,
    cot_shifted_in,
    second_part,
    hidden_ref,
    act_grad_ref,
    keep_ref,
    send_ref,
    window,
    cot_window,
    act,
    back,
    work,
    cot_shifted,
    cot_taps,
    frame_t,
    frame_taps,
    hidden_t,
    grad_shifted,
    grads,
):
    first = first_frame()
    zero = jnp.zeros((POS, C), BF16)
    for f in range(2):
        window[f] = tail[2 + f]
        window[2 + f] = frames[f]
        cot_window[f] = cot[EDGE + f]
        cot_window[2 + f] = head[2 + f]
    window[4] = zero
    cot_window[4] = zero

    for t in range(2):
        act[t] = conv_frame(window, past_slots(clips, first, t, 2, 4), conv_weight)
        back[t] = conv_frame(
            cot_window, next_slots(clips, first, EDGE + t, -EDGE, 4), back_weight
        )
    for f in range(2):
        cot_shifted[f] = column_pieces(cot_window[2 + f])
        for a, piece in enumerate(row_pieces(window[f])):
            frame_t[f, a * C : (a + 1) * C, :] = piece.T
    cot_shifted[2] = jnp.zeros((POS, 3 * C), BF16)
    frame_t[2] = jnp.zeros((3 * C, POS), BF16)
    scale = normalize(act, 2) + [scales[t : t + 1] for t in range(2, F)]
    for t in range(F):
        hidden_ref[t] = hidden_of(act[t]) if t < 2 else hidden_in[t]

    for n, s in enumerate((0, 1, EDGE, EDGE + 1)):
        place = slice(n * POS, (n + 1) * POS)
        for a, piece in enumerate(row_pieces(hidden_ref[s])):
            hidden_t[a * C : (a + 1) * C, place] = piece.T
        near = next_slots(clips, first, s, 0, F)
        far = next_slots(clips, first, s, -F, 2)
        for k in range(3):
            cot_taps[place, 3 * C * k : 3 * C * (k + 1)] = (
                cot_shifted_in[near[2 - k]] if s + 2 - k < F else cot_shifted[far[2 - k]]
            )
    second_grad = second_part[...] + jnp.dot(
        hidden_t[...], cot_taps[...], preferred_element_type=F32
    )
    for k in range(3):
        for a in range(3):
            for b in range(3):
                tap = (k * 3 + a) * 3 + b
                grads[1, tap * C : (tap + 1) * C] = second_grad[
                    a * C : (a + 1) * C, (k * 3 + b) * C : (k * 3 + b + 1) * C
                ]

    rounded = norm_adjoint(
        lambda t: act[t] if t < 2 else act_in[t],
        lambda t: back_in[t] if t < EDGE else back[t - EDGE],
        scale,
        work,
    )
    for t in range(F):
        act_grad_ref[t] = rounded[t]
        grad_shifted[t * POS : (t + 1) * POS] = column_pieces(rounded[t])
        near = past_slots(clips, first, t, 0, F)
        far = past_slots(clips, first, t, 2, 2)
        for k in range(3):
            frame_taps[3 * C * k : 3 * C * (k + 1), t * POS : (t + 1) * POS] = (
                frame_t_in[near[k]] if t + k - 2 >= 0 else frame_t[far[k]]
            )
    split_rows(grads, 1, keep_ref, send_ref)
    first_grad = jnp.dot(frame_taps[...], grad_shifted[...], preferred_element_type=F32)
    for outer in range(9):
        for b in range(3):
            tap = outer * 3 + b
            grads[0, tap * C : (tap + 1) * C] = first_grad[
                outer * C : (outer + 1) * C, b * C : (b + 1) * C
            ]
    split_rows(grads, 0, keep_ref, send_ref)


HALF = F // 2


def residual_frames(clips, frames, hidden, weight, out_ref, start):
    first = first_frame()
    for t in range(HALF):
        slots = past_slots(clips, first, start + t, 2 - start, HALF + 2)
        out = conv_frame(hidden, slots, weight)
        out_ref[start + t] = (frames[start + t].astype(F32) + out).astype(BF16)


def fill(window, parts):
    count = 0
    for part in parts:
        for f in range(part.shape[0]):
            window[count] = part[f]
            count += 1
    window[count] = jnp.zeros((POS, C), BF16)


def forward_kernel(
    clips, hidden_in, frames, tail, conv_weight, weight2, out_ref, weight, window, act, hidden
):
    first = first_frame()
    fill(window, [tail])
    for t in range(2):
        act[t] = conv_frame(window, past_slots(clips, first, t - 2, 4, 4), conv_weight)
    normalize(act, 2)
    for t in range(2):
        hidden[t] = hidden_of(act[t])
    fill(hidden.at[2:], [hidden_in.at[:HALF]])
    forward_weight(weight2, weight)
    residual_frames(clips, frames, hidden, weight, out_ref, 0)


def rest_kernel(clips, hidden_in, frames, weight, half, out_ref, hidden):
    fill(hidden, [hidden_in.at[HALF - 2 :]])
    for t in range(HALF):
        out_ref[t] = half[t]
    residual_frames(clips, frames, hidden, weight, out_ref, HALF)


def next_grad_kernel(
    clips, frames, head, conv_weight, back_weight, out_ref, window, cot_window, act, back
):
    first = first_frame()
    zero = jnp.zeros((POS, C), BF16)
    for f in range(2):
        window[f] = frames[F - 2 + f]
        window[2 + f] = head[f]
    for f in range(4):
        cot_window[f] = head[2 + f]
    window[4] = zero
    cot_window[4] = zero
    for t in range(2):
        act[t] = conv_frame(window, past_slots(clips, first, F + t, 2 - F, 4), conv_weight)
        back[t] = conv_frame(cot_window, next_slots(clips, first, F + t, -F, 4), back_weight)
    scale = normalize(act, 2)
    for t, rounded in enumerate(
        norm_adjoint(lambda t: act[t], lambda t: back[t], scale, back)
    ):
        out_ref[t] = rounded


def backward_kernel(clips, act_grad_in, next_in, cot, weight1, out_ref, act_grad, weight):
    first = first_frame()
    for f in range(F):
        act_grad[f] = act_grad_in[f]
    for f in range(2):
        act_grad[F + f] = next_in[f]
    act_grad[F + 2] = jnp.zeros((POS, C), BF16)
    adjoint_weight(weight1, weight)
    for t in range(F):
        out = conv_frame(act_grad, next_slots(clips, first, t, 0, F + 2), weight)
        out_ref[t] = (cot[t].astype(F32) + out).astype(BF16)


STEPS = (2, 1, 3)


def place():
    index = lax.axis_index("dp")
    return lax.div(index, 8), lax.rem(lax.div(index, 2), 4), lax.rem(index, 2) == 0


def first_kernel(keep_ref, part, kept_ref, *sent_refs):
    y, x, along_x = place()
    for g in range(2):
        for other in range(4):
            for n, step in enumerate((0, *STEPS)):
                block = jnp.where(
                    along_x, 4 * other + lax.rem(x + step, 4), 4 * lax.rem(y + step, 4) + other
                )
                total = keep_ref[g, block] + part[g, block].astype(F32)
                if step == 0:
                    kept_ref[g, other] = total
                else:
                    sent_refs[n - 1][g, other] = total.astype(BF16)


def second_kernel(keep_ref, *refs):
    received, (kept_ref, *sent_refs) = refs[:3], refs[3:]
    y, x, along_x = place()
    own = jnp.where(along_x, y, x)
    for g in range(2):
        for n, step in enumerate((0, *STEPS)):
            block = lax.rem(own + step, 4)
            total = keep_ref[g, block]
            for part in received:
                total = total + part[g, block].astype(F32)
            if step == 0:
                kept_ref[g] = total
            else:
                sent_refs[n - 1][g] = total.astype(BF16)


def sum_kernel(keep_ref, *refs):
    received, out_ref = refs[:-1], refs[-1]
    total = keep_ref[...].astype(F32)
    for part in received:
        total = total + part[...].astype(F32)
    out_ref[...] = total.astype(BF16)


def last_kernel(scale, own, near, next_near, far, first_ref, second_ref):
    for g, out_ref in enumerate((first_ref, second_ref)):
        total = (own[g].astype(F32) + far[g].astype(F32)) + (
            near[g].astype(F32) + next_near[g].astype(F32)
        )
        out_ref[...] = (total * scale)[:BLOCK]


VMEM = pl.BlockSpec(memory_space=pltpu.VMEM)
SMEM = pl.BlockSpec(memory_space=pltpu.SMEM)
HBM = pl.BlockSpec(memory_space=pltpu.HBM)


def call(kernel, operands, in_specs, outs, scratch=(), flops=0, moved=1 << 20, limit=4):
    return pl.pallas_call(
        kernel,
        out_shape=[jax.ShapeDtypeStruct(shape, dtype) for shape, dtype in outs],
        in_specs=in_specs,
        out_specs=[VMEM] * len(outs),
        scratch_shapes=[
            pltpu.VMEM(*one) if isinstance(one, tuple) else one for one in scratch
        ],
        compiler_params=pltpu.CompilerParams(vmem_limit_bytes=limit << 20),
        cost_estimate=pl.CostEstimate(flops=flops, bytes_accessed=moved, transcendentals=0),
    )(*operands)


CONV_FLOPS = 2 * F * POS * 27 * C * C
WIDE = ((9 * C, 3 * C), BF16)


def frame_shape(count, dtype=BF16):
    return ((count, POS, C), dtype)


def shifted(value, steps):
    return seq_permute(value, lambda z: z + steps)


def dp_permute(value, target):
    return lax.ppermute(value, "dp", [(source, target(source)) for source in range(32)])


def along_x(step):
    return lambda d: (d // 8) * 8 + (d % 8 + 2 * step) % 8


def along_y(step):
    return lambda d: (d + 8 * step) % 32


def crossed(first, second):
    return lambda d: second(d) if d % 2 else first(d)


def seq_permute(value, target):
    return lax.ppermute(value, "seq", [(source, target(source) % 8) for source in range(8)])


def per_device(frames, clip_ids, cotangent, conv1_weight, conv2_weight):
    own_frames = frames.reshape(F, POS, C)
    own_cot = cotangent.reshape(F, POS, C)
    clip_ids, own_frames, own_cot, conv1_weight, conv2_weight = (
        pltpu.with_memory_space_constraint(value, pltpu.HBM)
        for value in (clip_ids, own_frames, own_cot, conv1_weight, conv2_weight)
    )
    clip_ids, tail, head, weight1 = call(
        halo_kernel,
        (clip_ids, own_frames, own_cot, conv1_weight),
        [HBM] * 4,
        [(clip_ids.shape, jnp.int32), frame_shape(4), frame_shape(6), ((27 * C, C), BF16)],
        [pltpu.SemaphoreType.DMA((5,))],
    )
    head = shifted(head, -1)
    tail = shifted(tail, 1)
    local = call(
        local_kernel,
        (clip_ids, own_frames, own_cot, weight1, conv2_weight),
        [SMEM, HBM, HBM, VMEM, HBM],
        [
            frame_shape(F + 1),
            frame_shape(F + 1),
            ((27 * C, C), BF16),
            WIDE,
            WIDE,
            frame_shape(F, F32),
            frame_shape(F, F32),
            ((F, C), F32),
            frame_shape(F),
            ((F + 1, 3 * C, POS), BF16),
            ((F + 1, POS, 3 * C), BF16),
            ((3 * C, 9 * C), F32),
        ],
        [
            ((3 * C, 4 * POS), BF16),
            ((4 * POS, 9 * C), BF16),
            pltpu.SemaphoreType.DMA((3,)),
        ],
        flops=CONV_FLOPS * 2,
        limit=16,
    )
    tail, head, local = lax.optimization_barrier((tail, head, local))
    frame_copy, cot_copy, weight2, conv_weight, back_weight, *partial = local
    block = ((2, 16, PADDED, C), F32)
    hidden, act_grad, keep, send = call(
        main_kernel,
        (clip_ids, frame_copy, cot_copy, tail, head, conv_weight, back_weight, *partial),
        [SMEM] + [VMEM] * 13,
        [frame_shape(F), frame_shape(F), block, (block[0], BF16)],
        [
            frame_shape(5),
            frame_shape(5),
            frame_shape(2, F32),
            frame_shape(2, F32),
            frame_shape(F, F32),
            ((3, POS, 3 * C), BF16),
            ((4 * POS, 9 * C), BF16),
            ((3, 3 * C, POS), BF16),
            ((9 * C, F * POS), BF16),
            ((3 * C, 4 * POS), BF16),
            ((F * POS, 3 * C), BF16),
            ((2, 27 * C, C), F32),
        ],
        flops=CONV_FLOPS * 2,
        limit=32,
    )
    recv = dp_permute(send, lambda d: d ^ 1)
    head, keep = lax.optimization_barrier((head, keep))
    (act_grad_next,) = call(
        next_grad_kernel,
        (clip_ids, frame_copy, head, conv_weight, back_weight),
        [SMEM] + [VMEM] * 4,
        [frame_shape(2)],
        [frame_shape(5), frame_shape(5), frame_shape(2, F32), frame_shape(2, F32)],
        flops=CONV_FLOPS // 2,
        limit=8,
    )
    recv, act_grad_next = lax.optimization_barrier((recv, act_grad_next))
    keep, *sent = call(
        first_kernel,
        (keep, recv),
        [VMEM] * 2,
        [((2, 4, PADDED, C), F32)] + [((2, 4, PADDED, C), BF16)] * 3,
    )
    sent, hidden = lax.optimization_barrier((sent, hidden))
    recv = [
        dp_permute(part, crossed(along_x(s), along_y(s))) for s, part in zip(STEPS, sent)
    ]
    half_out, wide_weight = call(
        forward_kernel,
        (clip_ids, hidden, frame_copy, tail, conv_weight, weight2),
        [SMEM] + [VMEM] * 5,
        [frame_shape(HALF), WIDE],
        [frame_shape(5), frame_shape(2, F32), frame_shape(HALF + 3)],
        flops=CONV_FLOPS * 3 // 4,
        limit=12,
    )
    recv, half_out = lax.optimization_barrier((recv, half_out))
    pair = (2, PADDED, C)
    keep, *sent = call(
        second_kernel, (keep, *recv), [VMEM] * 4, [(pair, F32)] + [(pair, BF16)] * 3
    )
    sent, half_out = lax.optimization_barrier((sent, half_out))
    recv = [
        dp_permute(part, crossed(along_y(s), along_x(s))) for s, part in zip(STEPS, sent)
    ]
    (block_out,) = call(
        rest_kernel,
        (clip_ids, hidden, frame_copy, wide_weight, half_out),
        [SMEM] + [VMEM] * 4,
        [frame_shape(F)],
        [frame_shape(HALF + 3)],
        flops=CONV_FLOPS // 2,
        limit=8,
    )
    recv, block_out = lax.optimization_barrier((recv, block_out))
    (total,) = call(sum_kernel, (keep, *recv), [VMEM] * 4, [(pair, BF16)])
    other = seq_permute(total, lambda z: z ^ 1)
    (total,) = call(sum_kernel, (total, other), [VMEM] * 2, [(pair, BF16)])
    total, act_grad = lax.optimization_barrier((total, act_grad))
    others = [
        seq_permute(total, lambda z, s=s: z + s if z % 2 else z - s) for s in (1, 2, 3)
    ]
    (input_grad,) = call(
        backward_kernel,
        (clip_ids, act_grad, act_grad_next, cot_copy, weight1),
        [SMEM] + [VMEM] * 4,
        [frame_shape(F)],
        [frame_shape(F + 3), WIDE],
        flops=CONV_FLOPS,
        limit=8,
    )
    others, input_grad = lax.optimization_barrier((others, input_grad))
    rows = lax.axis_size("dp") * lax.axis_size("seq") * F * POS
    first_grad, second_grad = call(
        lambda *refs: last_kernel(rows**-0.5, *refs),
        (total, *others),
        [VMEM] * 4,
        [((BLOCK, C), F32)] * 2,
    )
    return (
        block_out.reshape(frames.shape),
        input_grad.reshape(frames.shape),
        first_grad,
        second_grad,
    )


def solution(mesh):
    return jax.shard_map(
        per_device,
        mesh=mesh,
        in_specs=(
            P("dp", "seq", None, None, None),
            P("dp", None),
            P("dp", "seq", None, None, None),
            P(),
            P(),
        ),
        out_specs=(
            P("dp", "seq", None, None, None),
            P("dp", "seq", None, None, None),
            P("dp", None),
            P("dp", None),
        ),
        check_vma=False,
    )
```

```python
import jax
import jax.numpy as jnp
from jax import lax
from jax.experimental import pallas as pl
from jax.experimental.pallas import tpu as pltpu
from jax.sharding import PartitionSpec as P

C = 128
GROUP = 4
F = 8
HT = 8
WT = 32
POS = HT * WT
BLOCK = 108
PADDED = 112
BF16 = jnp.bfloat16
F32 = jnp.float32


def clip_at(clips, frame):
    return clips[0, jnp.clip(frame, 0, clips.shape[1] - 1)]


def past_slots(clips, first, t, base, none):
    slots = []
    for k in range(3):
        frame = first + t + k - 2
        same = clip_at(clips, frame) == clip_at(clips, first + t)
        slots.append(jnp.where(same & (frame >= 0), t + k - 2 + base, none))
    return slots


def next_slots(clips, first, t, base, none):
    slots = []
    for q in range(3):
        frame = first + t + q
        same = clip_at(clips, frame) == clip_at(clips, first + t)
        slots.append(jnp.where(same & (frame < clips.shape[1]), t + q + base, none))
    return slots


def column(rows):
    return lax.broadcasted_iota(jnp.int32, (rows, C), 0) % WT


def shift_down(value):
    return jnp.where(column(POS) == 0, 0.0, pltpu.roll(value, 1, 0))


def shift_up(value):
    return jnp.where(column(POS) == WT - 1, 0.0, pltpu.roll(value, POS - 1, 0))


def row_pieces(frame):
    edge = jnp.zeros((WT, C), frame.dtype)
    return [
        jnp.concatenate([edge, frame[: POS - WT]], axis=0),
        frame,
        jnp.concatenate([frame[WT:], edge], axis=0),
    ]


def column_pieces(frame):
    wide = frame.astype(F32)
    return jnp.concatenate([shift_up(wide).astype(BF16), frame, shift_down(wide).astype(BF16)], axis=1)


def conv_frame(window, slots, weight):
    pieces = []
    for slot in slots:
        pieces += row_pieces(window[slot])
    taps = jnp.dot(jnp.concatenate(pieces, axis=1), weight[...], preferred_element_type=F32)
    return shift_down(taps[:, :C]) + taps[:, C : 2 * C] + shift_up(taps[:, 2 * C :])


def forward_weight(weight_ref, out_ref):
    for outer in range(9):
        for b in range(3):
            out_ref[outer * C : (outer + 1) * C, b * C : (b + 1) * C] = weight_ref[
                (outer * 3 + b) * C : (outer * 3 + b + 1) * C, :
            ]


def adjoint_weight(weight_ref, out_ref):
    for outer in range(9):
        for b in range(3):
            tap = 26 - (outer * 3 + b)
            out_ref[outer * C : (outer + 1) * C, b * C : (b + 1) * C] = weight_ref[
                tap * C : (tap + 1) * C, :
            ].T


def group_mean(sums):
    count = len(sums)
    sums = jnp.concatenate(sums + [jnp.zeros_like(sums[0])] * (F - count), axis=0)
    lane = lax.broadcasted_iota(jnp.int32, sums.shape, 1)
    pairs = sums + jnp.where(lane % 2 == 0, pltpu.roll(sums, C - 1, 1), pltpu.roll(sums, 1, 1))
    quads = pairs + jnp.where(lane % 4 < 2, pltpu.roll(pairs, C - 2, 1), pltpu.roll(pairs, 2, 1))
    mean = quads * (1.0 / (GROUP * POS))
    return [mean[t : t + 1] for t in range(count)]


def tile_sum(value):
    return jnp.sum(value, axis=0, keepdims=True)


def normalize(act, count):
    center = group_mean([tile_sum(act[t]) for t in range(count)])
    sums = []
    for t in range(count):
        away = act[t] - center[t]
        act[t] = away
        sums.append(tile_sum(away * away))
    scale = [lax.rsqrt(mean + 1e-06) for mean in group_mean(sums)]
    for t in range(count):
        act[t] = act[t] * scale[t]
    return scale


def gate_of(normed):
    return 1.0 / (1.0 + jnp.exp(-normed))


def hidden_of(normed):
    return (normed * gate_of(normed)).astype(BF16)


def norm_adjoint(act, back, scale, work):
    count = len(scale)
    first, second = [], []
    for t in range(count):
        normed = act(t)
        gate = gate_of(normed)
        grad = back(t) * (gate * (1.0 + normed * (1.0 - gate)))
        work[t] = grad
        first.append(tile_sum(grad))
        second.append(tile_sum(grad * normed))
    first, second = group_mean(first), group_mean(second)
    return [(scale[t] * (work[t] - first[t] - act(t) * second[t])).astype(BF16) for t in range(count)]


def first_frame():
    return lax.axis_index("seq") * F


def halo_kernel(
    clips, frames, cot, weight1, clips_copy, tail, head, weight1_copy, window, sems
):
    copies = [
        pltpu.make_async_copy(weight1, weight1_copy, sems.at[4]),
        pltpu.make_async_copy(frames, window.at[:F], sems.at[5]),
        pltpu.make_async_copy(clips, clips_copy, sems.at[3]),
        pltpu.make_async_copy(frames.at[F - 4 :], tail, sems.at[0]),
        pltpu.make_async_copy(frames.at[:2], head.at[:2], sems.at[1]),
        pltpu.make_async_copy(cot.at[:4], head.at[2:], sems.at[2]),
    ]
    for copy in copies:
        copy.start()
    window[F] = jnp.zeros((POS, C), BF16)
    for copy in copies:
        copy.wait()


SIDES = (0, 1, F - 2, F - 1)
EDGE = F - 2


def local_kernel(
    clips,
    window,
    cot,
    weight1,
    weight2,
    cot_window,
    weight2_copy,
    conv_weight,
    back_weight,
    act,
    back,
    scales,
    hidden,
    frame_t,
    cot_shifted,
    second_part,
    act_grad,
    first_part,
    hidden_t,
    cot_taps,
    frame_taps,
    grad_shifted,
    work,
    sems,
):
    copies = [
        pltpu.make_async_copy(weight2, weight2_copy, sems.at[0]),
        pltpu.make_async_copy(cot, cot_window.at[:F], sems.at[1]),
    ]
    for copy in copies:
        copy.start()
    cot_window[F] = jnp.zeros((POS, C), BF16)
    frame_t[F] = jnp.zeros((3 * C, POS), BF16)
    cot_shifted[F] = jnp.zeros((POS, 3 * C), BF16)
    first = first_frame()
    forward_weight(weight1, conv_weight)
    for t in range(2, F):
        if t == 4:
            for copy in copies:
                copy.wait()
        act[t] = conv_frame(window, past_slots(clips, first, t, 0, F), conv_weight)
    adjoint_weight(weight2_copy, back_weight)
    for f in range(F):
        cot_shifted[f] = column_pieces(cot_window[f])
        for a, piece in enumerate(row_pieces(window[f])):
            frame_t[f, a * C : (a + 1) * C, :] = piece.T
    for t in range(EDGE):
        back[t] = conv_frame(cot_window, next_slots(clips, first, t, 0, F), back_weight)
    scale = normalize(act.at[2:F], F - 2)
    for t in range(2, F):
        scales[t : t + 1] = scale[t - 2]
    for t in range(2, F):
        value = hidden_of(act[t])
        hidden[t] = value
        if t < EDGE:
            place = slice((t - 2) * POS, (t - 1) * POS)
            for a, piece in enumerate(row_pieces(value)):
                hidden_t[a * C : (a + 1) * C, place] = piece.T
            slots = next_slots(clips, first, t, 0, F)
            for k in range(3):
                cot_taps[place, 3 * C * k : 3 * C * (k + 1)] = cot_shifted[slots[2 - k]]
    second_part[...] = jnp.dot(hidden_t[...], cot_taps[...], preferred_element_type=F32)
    rounded = norm_adjoint(lambda n: act[2 + n], lambda n: back[2 + n], scale[: EDGE - 2], work)
    for n, value in enumerate(rounded):
        act_grad[2 + n] = value
        place = slice(n * POS, (n + 1) * POS)
        grad_shifted[place] = column_pieces(value)
        slots = past_slots(clips, first, 2 + n, 0, F)
        for k in range(3):
            frame_taps[3 * C * k : 3 * C * (k + 1), place] = frame_t[slots[k]]
    first_part[...] = jnp.dot(frame_taps[...], grad_shifted[...], preferred_element_type=F32)


def split_rows(grads, g, keep_ref, send_ref):
    own = lax.rem(lax.axis_index("dp"), 2) == 0
    for m in range(16):
        low = grads[g, 2 * BLOCK * m : 2 * BLOCK * m + BLOCK]
        high = grads[g, 2 * BLOCK * m + BLOCK : 2 * BLOCK * (m + 1)]
        keep_ref[g, m, :BLOCK] = jnp.where(own, low, high)
        keep_ref[g, m, BLOCK:] = jnp.zeros((PADDED - BLOCK, C), F32)
        send_ref[g, m, :BLOCK] = jnp.where(own, high, low).astype(BF16)
        send_ref[g, m, BLOCK:] = jnp.zeros((PADDED - BLOCK, C), BF16)


def main_kernel(
    clips,
    frames,
    cot,
    tail,
    head,
    conv_weight,
    back_weight,
    act_in,
    back_in,
    scales,
    hidden_in,
    frame_t_in,
    cot_shifted_in,
    second_part,
    act_grad_in,
    first_part,
    hidden_ref,
    act_grad_ref,
    keep_ref,
    send_ref,
    window,
    cot_window,
    act,
    back,
    work,
    cot_shifted,
    cot_taps,
    frame_t,
    frame_taps,
    hidden_t,
    grad_shifted,
    grads,
):
    first = first_frame()
    zero = jnp.zeros((POS, C), BF16)
    for f in range(2):
        window[f] = tail[2 + f]
        window[2 + f] = frames[f]
        cot_window[f] = cot[EDGE + f]
        cot_window[2 + f] = head[2 + f]
    window[4] = zero
    cot_window[4] = zero

    for t in range(2):
        act[t] = conv_frame(window, past_slots(clips, first, t, 2, 4), conv_weight)
        back[t] = conv_frame(
            cot_window, next_slots(clips, first, EDGE + t, -EDGE, 4), back_weight
        )
    for f in range(2):
        cot_shifted[f] = column_pieces(cot_window[2 + f])
        for a, piece in enumerate(row_pieces(window[f])):
            frame_t[f, a * C : (a + 1) * C, :] = piece.T
    cot_shifted[2] = jnp.zeros((POS, 3 * C), BF16)
    frame_t[2] = jnp.zeros((3 * C, POS), BF16)
    scale = normalize(act, 2) + [scales[t : t + 1] for t in SIDES[2:]]
    for t in range(F):
        hidden_ref[t] = hidden_of(act[t]) if t < 2 else hidden_in[t]

    for n, s in enumerate(SIDES):
        place = slice(n * POS, (n + 1) * POS)
        for a, piece in enumerate(row_pieces(hidden_ref[s])):
            hidden_t[a * C : (a + 1) * C, place] = piece.T
        near = next_slots(clips, first, s, 0, F)
        far = next_slots(clips, first, s, -F, 2)
        for k in range(3):
            cot_taps[place, 3 * C * k : 3 * C * (k + 1)] = (
                cot_shifted_in[near[2 - k]] if s + 2 - k < F else cot_shifted[far[2 - k]]
            )
    second_grad = second_part[...] + jnp.dot(
        hidden_t[...], cot_taps[...], preferred_element_type=F32
    )
    for k in range(3):
        for a in range(3):
            for b in range(3):
                tap = (k * 3 + a) * 3 + b
                grads[1, tap * C : (tap + 1) * C] = second_grad[
                    a * C : (a + 1) * C, (k * 3 + b) * C : (k * 3 + b + 1) * C
                ]

    rounded = norm_adjoint(
        lambda n: act[n] if n < 2 else act_in[SIDES[n]],
        lambda n: back_in[n] if n < 2 else back[n - 2],
        scale,
        work,
    )
    for t in range(2, EDGE):
        act_grad_ref[t] = act_grad_in[t]
    for n, t in enumerate(SIDES):
        act_grad_ref[t] = rounded[n]
        place = slice(n * POS, (n + 1) * POS)
        grad_shifted[place] = column_pieces(rounded[n])
        near = past_slots(clips, first, t, 0, F)
        far = past_slots(clips, first, t, 2, 2)
        for k in range(3):
            frame_taps[3 * C * k : 3 * C * (k + 1), place] = (
                frame_t_in[near[k]] if t + k - 2 >= 0 else frame_t[far[k]]
            )
    split_rows(grads, 1, keep_ref, send_ref)
    first_grad = first_part[...] + jnp.dot(
        frame_taps[...], grad_shifted[...], preferred_element_type=F32
    )
    for outer in range(9):
        for b in range(3):
            tap = outer * 3 + b
            grads[0, tap * C : (tap + 1) * C] = first_grad[
                outer * C : (outer + 1) * C, b * C : (b + 1) * C
            ]
    split_rows(grads, 0, keep_ref, send_ref)


HALF = F // 2


def residual_frames(clips, frames, hidden, weight, out_ref, start):
    first = first_frame()
    for t in range(HALF):
        slots = past_slots(clips, first, start + t, 2 - start, HALF + 2)
        out = conv_frame(hidden, slots, weight)
        out_ref[start + t] = (frames[start + t].astype(F32) + out).astype(BF16)


def fill(window, parts):
    count = 0
    for part in parts:
        for f in range(part.shape[0]):
            window[count] = part[f]
            count += 1
    window[count] = jnp.zeros((POS, C), BF16)


def forward_kernel(
    clips, hidden_in, frames, tail, conv_weight, weight2, out_ref, weight, window, act, hidden
):
    first = first_frame()
    fill(window, [tail])
    for t in range(2):
        act[t] = conv_frame(window, past_slots(clips, first, t - 2, 4, 4), conv_weight)
    normalize(act, 2)
    for t in range(2):
        hidden[t] = hidden_of(act[t])
    fill(hidden.at[2:], [hidden_in.at[:HALF]])
    forward_weight(weight2, weight)
    residual_frames(clips, frames, hidden, weight, out_ref, 0)


def rest_kernel(clips, hidden_in, frames, weight, half, out_ref, hidden):
    fill(hidden, [hidden_in.at[HALF - 2 :]])
    for t in range(HALF):
        out_ref[t] = half[t]
    residual_frames(clips, frames, hidden, weight, out_ref, HALF)


def next_grad_kernel(
    clips, frames, head, conv_weight, back_weight, out_ref, window, cot_window, act, back
):
    first = first_frame()
    zero = jnp.zeros((POS, C), BF16)
    for f in range(2):
        window[f] = frames[F - 2 + f]
        window[2 + f] = head[f]
    for f in range(4):
        cot_window[f] = head[2 + f]
    window[4] = zero
    cot_window[4] = zero
    for t in range(2):
        act[t] = conv_frame(window, past_slots(clips, first, F + t, 2 - F, 4), conv_weight)
        back[t] = conv_frame(cot_window, next_slots(clips, first, F + t, -F, 4), back_weight)
    scale = normalize(act, 2)
    for t, rounded in enumerate(
        norm_adjoint(lambda t: act[t], lambda t: back[t], scale, back)
    ):
        out_ref[t] = rounded


def backward_kernel(clips, act_grad_in, next_in, cot, weight1, out_ref, act_grad, weight):
    first = first_frame()
    for f in range(F):
        act_grad[f] = act_grad_in[f]
    for f in range(2):
        act_grad[F + f] = next_in[f]
    act_grad[F + 2] = jnp.zeros((POS, C), BF16)
    adjoint_weight(weight1, weight)
    for t in range(F):
        out = conv_frame(act_grad, next_slots(clips, first, t, 0, F + 2), weight)
        out_ref[t] = (cot[t].astype(F32) + out).astype(BF16)


STEPS = (2, 1, 3)


def place():
    index = lax.axis_index("dp")
    return lax.div(index, 8), lax.rem(lax.div(index, 2), 4), lax.rem(index, 2) == 0


def first_kernel(keep_ref, part, kept_ref, *sent_refs):
    y, x, along_x = place()
    for g in range(2):
        for other in range(4):
            for n, step in enumerate((0, *STEPS)):
                block = jnp.where(
                    along_x, 4 * other + lax.rem(x + step, 4), 4 * lax.rem(y + step, 4) + other
                )
                total = keep_ref[g, block] + part[g, block].astype(F32)
                if step == 0:
                    kept_ref[g, other] = total
                else:
                    sent_refs[n - 1][g, other] = total.astype(BF16)


def second_kernel(keep_ref, *refs):
    received, (kept_ref, *sent_refs) = refs[:3], refs[3:]
    y, x, along_x = place()
    own = jnp.where(along_x, y, x)
    for g in range(2):
        for n, step in enumerate((0, *STEPS)):
            block = lax.rem(own + step, 4)
            total = keep_ref[g, block]
            for part in received:
                total = total + part[g, block].astype(F32)
            if step == 0:
                kept_ref[g] = total
            else:
                sent_refs[n - 1][g] = total.astype(BF16)


def sum_kernel(keep_ref, *refs):
    received, out_ref = refs[:-1], refs[-1]
    total = keep_ref[...].astype(F32)
    for part in received:
        total = total + part[...].astype(F32)
    out_ref[...] = total.astype(BF16)


def last_kernel(scale, own, near, next_near, far, first_ref, second_ref):
    for g, out_ref in enumerate((first_ref, second_ref)):
        total = (own[g].astype(F32) + far[g].astype(F32)) + (
            near[g].astype(F32) + next_near[g].astype(F32)
        )
        out_ref[...] = (total * scale)[:BLOCK]


VMEM = pl.BlockSpec(memory_space=pltpu.VMEM)
SMEM = pl.BlockSpec(memory_space=pltpu.SMEM)
HBM = pl.BlockSpec(memory_space=pltpu.HBM)


def call(kernel, operands, in_specs, outs, scratch=(), flops=0, moved=1 << 20, limit=4):
    return pl.pallas_call(
        kernel,
        out_shape=[jax.ShapeDtypeStruct(shape, dtype) for shape, dtype in outs],
        in_specs=in_specs,
        out_specs=[VMEM] * len(outs),
        scratch_shapes=[
            pltpu.VMEM(*one) if isinstance(one, tuple) else one for one in scratch
        ],
        compiler_params=pltpu.CompilerParams(vmem_limit_bytes=limit << 20),
        cost_estimate=pl.CostEstimate(flops=flops, bytes_accessed=moved, transcendentals=0),
    )(*operands)


CONV_FLOPS = 2 * F * POS * 27 * C * C
WIDE = ((9 * C, 3 * C), BF16)


def frame_shape(count, dtype=BF16):
    return ((count, POS, C), dtype)


def shifted(value, steps):
    return seq_permute(value, lambda z: z + steps)


def dp_permute(value, target):
    return lax.ppermute(value, "dp", [(source, target(source)) for source in range(32)])


def along_x(step):
    return lambda d: (d // 8) * 8 + (d % 8 + 2 * step) % 8


def along_y(step):
    return lambda d: (d + 8 * step) % 32


def crossed(first, second):
    return lambda d: second(d) if d % 2 else first(d)


def seq_permute(value, target):
    return lax.ppermute(value, "seq", [(source, target(source) % 8) for source in range(8)])


def per_device(frames, clip_ids, cotangent, conv1_weight, conv2_weight):
    own_frames = frames.reshape(F, POS, C)
    own_cot = cotangent.reshape(F, POS, C)
    clip_ids, own_frames, own_cot, conv1_weight, conv2_weight = (
        pltpu.with_memory_space_constraint(value, pltpu.HBM)
        for value in (clip_ids, own_frames, own_cot, conv1_weight, conv2_weight)
    )
    clip_ids, tail, head, weight1, frame_copy = call(
        halo_kernel,
        (clip_ids, own_frames, own_cot, conv1_weight),
        [HBM] * 4,
        [
            (clip_ids.shape, jnp.int32),
            frame_shape(4),
            frame_shape(6),
            ((27 * C, C), BF16),
            frame_shape(F + 1),
        ],
        [pltpu.SemaphoreType.DMA((6,))],
    )
    head = shifted(head, -1)
    tail = shifted(tail, 1)
    local = call(
        local_kernel,
        (clip_ids, frame_copy, own_cot, weight1, conv2_weight),
        [SMEM, VMEM, HBM, VMEM, HBM],
        [
            frame_shape(F + 1),
            ((27 * C, C), BF16),
            WIDE,
            WIDE,
            frame_shape(F, F32),
            frame_shape(F, F32),
            ((F, C), F32),
            frame_shape(F),
            ((F + 1, 3 * C, POS), BF16),
            ((F + 1, POS, 3 * C), BF16),
            ((3 * C, 9 * C), F32),
            frame_shape(F),
            ((9 * C, 3 * C), F32),
        ],
        [
            ((3 * C, 4 * POS), BF16),
            ((4 * POS, 9 * C), BF16),
            ((9 * C, 4 * POS), BF16),
            ((4 * POS, 3 * C), BF16),
            frame_shape(4, F32),
            pltpu.SemaphoreType.DMA((2,)),
        ],
        flops=CONV_FLOPS * 5 // 2,
        limit=24,
    )
    tail, head, local = lax.optimization_barrier((tail, head, local))
    cot_copy, weight2, conv_weight, back_weight, *partial = local
    block = ((2, 16, PADDED, C), F32)
    hidden, act_grad, keep, send = call(
        main_kernel,
        (clip_ids, frame_copy, cot_copy, tail, head, conv_weight, back_weight, *partial),
        [SMEM] + [VMEM] * 15,
        [frame_shape(F), frame_shape(F), block, (block[0], BF16)],
        [
            frame_shape(5),
            frame_shape(5),
            frame_shape(2, F32),
            frame_shape(2, F32),
            frame_shape(4, F32),
            ((3, POS, 3 * C), BF16),
            ((4 * POS, 9 * C), BF16),
            ((3, 3 * C, POS), BF16),
            ((9 * C, 4 * POS), BF16),
            ((3 * C, 4 * POS), BF16),
            ((4 * POS, 3 * C), BF16),
            ((2, 27 * C, C), F32),
        ],
        flops=CONV_FLOPS * 3 // 2,
        limit=28,
    )
    recv = dp_permute(send, lambda d: d ^ 1)
    keep, *sent = call(
        first_kernel,
        (keep, recv),
        [VMEM] * 2,
        [((2, 4, PADDED, C), F32)] + [((2, 4, PADDED, C), BF16)] * 3,
    )
    sent, hidden = lax.optimization_barrier((sent, hidden))
    recv = [
        dp_permute(part, crossed(along_x(s), along_y(s))) for s, part in zip(STEPS, sent)
    ]
    half_out, wide_weight = call(
        forward_kernel,
        (clip_ids, hidden, frame_copy, tail, conv_weight, weight2),
        [SMEM] + [VMEM] * 5,
        [frame_shape(HALF), WIDE],
        [frame_shape(5), frame_shape(2, F32), frame_shape(HALF + 3)],
        flops=CONV_FLOPS * 3 // 4,
        limit=12,
    )
    recv, half_out = lax.optimization_barrier((recv, half_out))
    pair = (2, PADDED, C)
    keep, *sent = call(
        second_kernel, (keep, *recv), [VMEM] * 4, [(pair, F32)] + [(pair, BF16)] * 3
    )
    sent, half_out = lax.optimization_barrier((sent, half_out))
    recv = [
        dp_permute(part, crossed(along_y(s), along_x(s))) for s, part in zip(STEPS, sent)
    ]
    (block_out,) = call(
        rest_kernel,
        (clip_ids, hidden, frame_copy, wide_weight, half_out),
        [SMEM] + [VMEM] * 4,
        [frame_shape(F)],
        [frame_shape(HALF + 3)],
        flops=CONV_FLOPS // 2,
        limit=8,
    )
    recv, block_out = lax.optimization_barrier((recv, block_out))
    (total,) = call(sum_kernel, (keep, *recv), [VMEM] * 4, [(pair, BF16)])
    head, total = lax.optimization_barrier((head, total))
    other = seq_permute(total, lambda z: z ^ 1)
    (act_grad_next,) = call(
        next_grad_kernel,
        (clip_ids, frame_copy, head, conv_weight, back_weight),
        [SMEM] + [VMEM] * 4,
        [frame_shape(2)],
        [frame_shape(5), frame_shape(5), frame_shape(2, F32), frame_shape(2, F32)],
        flops=CONV_FLOPS // 2,
        limit=8,
    )
    other, act_grad_next = lax.optimization_barrier((other, act_grad_next))
    (total,) = call(sum_kernel, (total, other), [VMEM] * 2, [(pair, BF16)])
    total, act_grad = lax.optimization_barrier((total, act_grad))
    others = [
        seq_permute(total, lambda z, s=s: z + s if z % 2 else z - s) for s in (1, 2, 3)
    ]
    (input_grad,) = call(
        backward_kernel,
        (clip_ids, act_grad, act_grad_next, cot_copy, weight1),
        [SMEM] + [VMEM] * 4,
        [frame_shape(F)],
        [frame_shape(F + 3), WIDE],
        flops=CONV_FLOPS,
        limit=8,
    )
    others, input_grad = lax.optimization_barrier((others, input_grad))
    rows = lax.axis_size("dp") * lax.axis_size("seq") * F * POS
    first_grad, second_grad = call(
        lambda *refs: last_kernel(rows**-0.5, *refs),
        (total, *others),
        [VMEM] * 4,
        [((BLOCK, C), F32)] * 2,
    )
    return (
        block_out.reshape(frames.shape),
        input_grad.reshape(frames.shape),
        first_grad,
        second_grad,
    )


def solution(mesh):
    return jax.shard_map(
        per_device,
        mesh=mesh,
        in_specs=(
            P("dp", "seq", None, None, None),
            P("dp", None),
            P("dp", "seq", None, None, None),
            P(),
            P(),
        ),
        out_specs=(
            P("dp", "seq", None, None, None),
            P("dp", "seq", None, None, None),
            P("dp", None),
            P("dp", None),
        ),
        check_vma=False,
    )
```

```python
import jax
import jax.numpy as jnp
from jax import lax
from jax.experimental import pallas as pl
from jax.experimental.pallas import tpu as pltpu
from jax.sharding import PartitionSpec as P

C = 128
GROUP = 4
F = 8
HT = 8
WT = 32
POS = HT * WT
BLOCK = 108
PADDED = 112
BF16 = jnp.bfloat16
F32 = jnp.float32


def clip_at(clips, frame):
    return clips[0, jnp.clip(frame, 0, clips.shape[1] - 1)]


def past_slots(clips, first, t, base, none):
    slots = []
    for k in range(3):
        frame = first + t + k - 2
        same = clip_at(clips, frame) == clip_at(clips, first + t)
        slots.append(jnp.where(same & (frame >= 0), t + k - 2 + base, none))
    return slots


def next_slots(clips, first, t, base, none):
    slots = []
    for q in range(3):
        frame = first + t + q
        same = clip_at(clips, frame) == clip_at(clips, first + t)
        slots.append(jnp.where(same & (frame < clips.shape[1]), t + q + base, none))
    return slots


def column(rows):
    return lax.broadcasted_iota(jnp.int32, (rows, C), 0) % WT


def shift_down(value):
    return jnp.where(column(POS) == 0, 0.0, pltpu.roll(value, 1, 0))


def shift_up(value):
    return jnp.where(column(POS) == WT - 1, 0.0, pltpu.roll(value, POS - 1, 0))


def row_pieces(frame):
    edge = jnp.zeros((WT, C), frame.dtype)
    return [
        jnp.concatenate([edge, frame[: POS - WT]], axis=0),
        frame,
        jnp.concatenate([frame[WT:], edge], axis=0),
    ]


def column_pieces(frame):
    wide = frame.astype(F32)
    return jnp.concatenate([shift_up(wide).astype(BF16), frame, shift_down(wide).astype(BF16)], axis=1)


def conv_frame(window, slots, weight):
    pieces = []
    for slot in slots:
        pieces += row_pieces(window[slot])
    taps = jnp.dot(jnp.concatenate(pieces, axis=1), weight[...], preferred_element_type=F32)
    return shift_down(taps[:, :C]) + taps[:, C : 2 * C] + shift_up(taps[:, 2 * C :])


def forward_weight(weight_ref, out_ref):
    for outer in range(9):
        for b in range(3):
            out_ref[outer * C : (outer + 1) * C, b * C : (b + 1) * C] = weight_ref[
                (outer * 3 + b) * C : (outer * 3 + b + 1) * C, :
            ]


def adjoint_weight(weight_ref, out_ref):
    for outer in range(9):
        for b in range(3):
            tap = 26 - (outer * 3 + b)
            out_ref[outer * C : (outer + 1) * C, b * C : (b + 1) * C] = weight_ref[
                tap * C : (tap + 1) * C, :
            ].T


def group_mean(sums):
    count = len(sums)
    sums = jnp.concatenate(sums + [jnp.zeros_like(sums[0])] * (F - count), axis=0)
    lane = lax.broadcasted_iota(jnp.int32, sums.shape, 1)
    pairs = sums + jnp.where(lane % 2 == 0, pltpu.roll(sums, C - 1, 1), pltpu.roll(sums, 1, 1))
    quads = pairs + jnp.where(lane % 4 < 2, pltpu.roll(pairs, C - 2, 1), pltpu.roll(pairs, 2, 1))
    mean = quads * (1.0 / (GROUP * POS))
    return [mean[t : t + 1] for t in range(count)]


def tile_sum(value):
    return jnp.sum(value, axis=0, keepdims=True)


def normalize(act, count):
    center = group_mean([tile_sum(act[t]) for t in range(count)])
    sums = []
    for t in range(count):
        away = act[t] - center[t]
        act[t] = away
        sums.append(tile_sum(away * away))
    scale = [lax.rsqrt(mean + 1e-06) for mean in group_mean(sums)]
    for t in range(count):
        act[t] = act[t] * scale[t]
    return scale


def gate_of(normed):
    return 1.0 / (1.0 + jnp.exp(-normed))


def hidden_of(normed):
    return (normed * gate_of(normed)).astype(BF16)


def norm_adjoint(act, back, scale, work):
    count = len(scale)
    first, second = [], []
    for t in range(count):
        normed = act(t)
        gate = gate_of(normed)
        grad = back(t) * (gate * (1.0 + normed * (1.0 - gate)))
        work[t] = grad
        first.append(tile_sum(grad))
        second.append(tile_sum(grad * normed))
    first, second = group_mean(first), group_mean(second)
    return [(scale[t] * (work[t] - first[t] - act(t) * second[t])).astype(BF16) for t in range(count)]


def first_frame():
    return lax.axis_index("seq") * F


def halo_kernel(
    clips, frames, cot, weight1, clips_copy, tail, head, weight1_copy, window, sems
):
    copies = [
        pltpu.make_async_copy(weight1, weight1_copy, sems.at[4]),
        pltpu.make_async_copy(frames, window.at[:F], sems.at[5]),
        pltpu.make_async_copy(clips, clips_copy, sems.at[3]),
        pltpu.make_async_copy(frames.at[F - 4 :], tail, sems.at[0]),
        pltpu.make_async_copy(frames.at[:2], head.at[:2], sems.at[1]),
        pltpu.make_async_copy(cot.at[:4], head.at[2:], sems.at[2]),
    ]
    for copy in copies:
        copy.start()
    window[F] = jnp.zeros((POS, C), BF16)
    for copy in copies:
        copy.wait()


SIDES = (0, 1, F - 2, F - 1)
EDGE = F - 2


def local_kernel(
    clips,
    window,
    cot,
    weight1,
    weight2,
    cot_window,
    weight2_copy,
    conv_weight,
    back_weight,
    act,
    back,
    scales,
    hidden,
    frame_t,
    cot_shifted,
    second_part,
    act_grad,
    first_part,
    hidden_t,
    cot_taps,
    frame_taps,
    grad_shifted,
    work,
    sems,
):
    copies = [
        pltpu.make_async_copy(weight2, weight2_copy, sems.at[0]),
        pltpu.make_async_copy(cot, cot_window.at[:F], sems.at[1]),
    ]
    for copy in copies:
        copy.start()
    cot_window[F] = jnp.zeros((POS, C), BF16)
    frame_t[F] = jnp.zeros((3 * C, POS), BF16)
    cot_shifted[F] = jnp.zeros((POS, 3 * C), BF16)
    first = first_frame()
    forward_weight(weight1, conv_weight)
    for t in range(2, F):
        if t == 4:
            for copy in copies:
                copy.wait()
        act[t] = conv_frame(window, past_slots(clips, first, t, 0, F), conv_weight)
    adjoint_weight(weight2_copy, back_weight)
    for f in range(F):
        cot_shifted[f] = column_pieces(cot_window[f])
        for a, piece in enumerate(row_pieces(window[f])):
            frame_t[f, a * C : (a + 1) * C, :] = piece.T
    for t in range(EDGE):
        back[t] = conv_frame(cot_window, next_slots(clips, first, t, 0, F), back_weight)
    scale = normalize(act.at[2:F], F - 2)
    for t in range(2, F):
        scales[t : t + 1] = scale[t - 2]
    for t in range(2, F):
        value = hidden_of(act[t])
        hidden[t] = value
        if t < EDGE:
            place = slice((t - 2) * POS, (t - 1) * POS)
            for a, piece in enumerate(row_pieces(value)):
                hidden_t[a * C : (a + 1) * C, place] = piece.T
            slots = next_slots(clips, first, t, 0, F)
            for k in range(3):
                cot_taps[place, 3 * C * k : 3 * C * (k + 1)] = cot_shifted[slots[2 - k]]
    second_part[...] = jnp.dot(hidden_t[...], cot_taps[...], preferred_element_type=F32)
    rounded = norm_adjoint(lambda n: act[2 + n], lambda n: back[2 + n], scale[: EDGE - 2], work)
    for n, value in enumerate(rounded):
        act_grad[2 + n] = value
        place = slice(n * POS, (n + 1) * POS)
        grad_shifted[place] = column_pieces(value)
        slots = past_slots(clips, first, 2 + n, 0, F)
        for k in range(3):
            frame_taps[3 * C * k : 3 * C * (k + 1), place] = frame_t[slots[k]]
    first_part[...] = jnp.dot(frame_taps[...], grad_shifted[...], preferred_element_type=F32)


def split_rows(grads, g, keep_ref, send_ref):
    own = lax.rem(lax.axis_index("dp"), 2) == 0
    for m in range(16):
        low = grads[g, 2 * BLOCK * m : 2 * BLOCK * m + BLOCK]
        high = grads[g, 2 * BLOCK * m + BLOCK : 2 * BLOCK * (m + 1)]
        keep_ref[g, m, :BLOCK] = jnp.where(own, low, high)
        keep_ref[g, m, BLOCK:] = jnp.zeros((PADDED - BLOCK, C), F32)
        send_ref[g, m, :BLOCK] = jnp.where(own, high, low).astype(BF16)
        send_ref[g, m, BLOCK:] = jnp.zeros((PADDED - BLOCK, C), BF16)


def main_kernel(
    clips,
    frames,
    cot,
    tail,
    head,
    conv_weight,
    back_weight,
    act_in,
    back_in,
    scales,
    hidden_in,
    frame_t_in,
    cot_shifted_in,
    second_part,
    act_grad_in,
    first_part,
    hidden_ref,
    act_grad_ref,
    keep_ref,
    send_ref,
    window,
    cot_window,
    act,
    back,
    work,
    cot_shifted,
    cot_taps,
    frame_t,
    frame_taps,
    hidden_t,
    grad_shifted,
    grads,
):
    first = first_frame()
    zero = jnp.zeros((POS, C), BF16)
    for f in range(2):
        window[f] = tail[2 + f]
        window[2 + f] = frames[f]
        cot_window[f] = cot[EDGE + f]
        cot_window[2 + f] = head[2 + f]
    window[4] = zero
    cot_window[4] = zero

    for t in range(2):
        act[t] = conv_frame(window, past_slots(clips, first, t, 2, 4), conv_weight)
        back[t] = conv_frame(
            cot_window, next_slots(clips, first, EDGE + t, -EDGE, 4), back_weight
        )
    for f in range(2):
        cot_shifted[f] = column_pieces(cot_window[2 + f])
        for a, piece in enumerate(row_pieces(window[f])):
            frame_t[f, a * C : (a + 1) * C, :] = piece.T
    cot_shifted[2] = jnp.zeros((POS, 3 * C), BF16)
    frame_t[2] = jnp.zeros((3 * C, POS), BF16)
    scale = normalize(act, 2) + [scales[t : t + 1] for t in SIDES[2:]]
    for t in range(F):
        hidden_ref[t] = hidden_of(act[t]) if t < 2 else hidden_in[t]

    for n, s in enumerate(SIDES):
        place = slice(n * POS, (n + 1) * POS)
        for a, piece in enumerate(row_pieces(hidden_ref[s])):
            hidden_t[a * C : (a + 1) * C, place] = piece.T
        near = next_slots(clips, first, s, 0, F)
        far = next_slots(clips, first, s, -F, 2)
        for k in range(3):
            cot_taps[place, 3 * C * k : 3 * C * (k + 1)] = (
                cot_shifted_in[near[2 - k]] if s + 2 - k < F else cot_shifted[far[2 - k]]
            )
    second_grad = second_part[...] + jnp.dot(
        hidden_t[...], cot_taps[...], preferred_element_type=F32
    )
    for k in range(3):
        for a in range(3):
            for b in range(3):
                tap = (k * 3 + a) * 3 + b
                grads[1, tap * C : (tap + 1) * C] = second_grad[
                    a * C : (a + 1) * C, (k * 3 + b) * C : (k * 3 + b + 1) * C
                ]

    rounded = norm_adjoint(
        lambda n: act[n] if n < 2 else act_in[SIDES[n]],
        lambda n: back_in[n] if n < 2 else back[n - 2],
        scale,
        work,
    )
    for t in range(2, EDGE):
        act_grad_ref[t] = act_grad_in[t]
    for n, t in enumerate(SIDES):
        act_grad_ref[t] = rounded[n]
        place = slice(n * POS, (n + 1) * POS)
        grad_shifted[place] = column_pieces(rounded[n])
        near = past_slots(clips, first, t, 0, F)
        far = past_slots(clips, first, t, 2, 2)
        for k in range(3):
            frame_taps[3 * C * k : 3 * C * (k + 1), place] = (
                frame_t_in[near[k]] if t + k - 2 >= 0 else frame_t[far[k]]
            )
    split_rows(grads, 1, keep_ref, send_ref)
    first_grad = first_part[...] + jnp.dot(
        frame_taps[...], grad_shifted[...], preferred_element_type=F32
    )
    for outer in range(9):
        for b in range(3):
            tap = outer * 3 + b
            grads[0, tap * C : (tap + 1) * C] = first_grad[
                outer * C : (outer + 1) * C, b * C : (b + 1) * C
            ]
    split_rows(grads, 0, keep_ref, send_ref)


HALF = F // 2


def residual_frames(clips, frames, hidden, weight, out_ref, start):
    first = first_frame()
    for t in range(HALF):
        slots = past_slots(clips, first, start + t, 2 - start, HALF + 2)
        out = conv_frame(hidden, slots, weight)
        out_ref[start + t] = (frames[start + t].astype(F32) + out).astype(BF16)


def fill(window, parts):
    count = 0
    for part in parts:
        for f in range(part.shape[0]):
            window[count] = part[f]
            count += 1
    window[count] = jnp.zeros((POS, C), BF16)


def forward_kernel(
    clips, hidden_in, frames, tail, conv_weight, weight2, out_ref, weight, window, act, hidden
):
    first = first_frame()
    fill(window, [tail])
    for t in range(2):
        act[t] = conv_frame(window, past_slots(clips, first, t - 2, 4, 4), conv_weight)
    normalize(act, 2)
    for t in range(2):
        hidden[t] = hidden_of(act[t])
    fill(hidden.at[2:], [hidden_in.at[:HALF]])
    forward_weight(weight2, weight)
    residual_frames(clips, frames, hidden, weight, out_ref, 0)


def rest_kernel(clips, hidden_in, frames, weight, half, out_ref, hidden):
    fill(hidden, [hidden_in.at[HALF - 2 :]])
    for t in range(HALF):
        out_ref[t] = half[t]
    residual_frames(clips, frames, hidden, weight, out_ref, HALF)


def next_grad_kernel(
    clips, frames, head, conv_weight, back_weight, out_ref, window, cot_window, act, back
):
    first = first_frame()
    zero = jnp.zeros((POS, C), BF16)
    for f in range(2):
        window[f] = frames[F - 2 + f]
        window[2 + f] = head[f]
    for f in range(4):
        cot_window[f] = head[2 + f]
    window[4] = zero
    cot_window[4] = zero
    for t in range(2):
        act[t] = conv_frame(window, past_slots(clips, first, F + t, 2 - F, 4), conv_weight)
        back[t] = conv_frame(cot_window, next_slots(clips, first, F + t, -F, 4), back_weight)
    scale = normalize(act, 2)
    for t, rounded in enumerate(
        norm_adjoint(lambda t: act[t], lambda t: back[t], scale, back)
    ):
        out_ref[t] = rounded


def backward_kernel(clips, act_grad_in, next_in, cot, weight1, out_ref, act_grad, weight):
    first = first_frame()
    for f in range(F):
        act_grad[f] = act_grad_in[f]
    for f in range(2):
        act_grad[F + f] = next_in[f]
    act_grad[F + 2] = jnp.zeros((POS, C), BF16)
    adjoint_weight(weight1, weight)
    for t in range(F):
        out = conv_frame(act_grad, next_slots(clips, first, t, 0, F + 2), weight)
        out_ref[t] = (cot[t].astype(F32) + out).astype(BF16)


STEPS = (2, 1, 3)


def place():
    index = lax.axis_index("dp")
    return lax.div(index, 8), lax.rem(lax.div(index, 2), 4), lax.rem(index, 2) == 0


def first_kernel(keep_ref, part, kept_ref, *sent_refs):
    y, x, along_x = place()
    for g in range(2):
        for other in range(4):
            for n, step in enumerate((0, *STEPS)):
                block = jnp.where(
                    along_x, 4 * other + lax.rem(x + step, 4), 4 * lax.rem(y + step, 4) + other
                )
                total = keep_ref[g, block] + part[g, block].astype(F32)
                if step == 0:
                    kept_ref[g, other] = total
                else:
                    sent_refs[n - 1][g, other] = total.astype(BF16)


def second_kernel(keep_ref, *refs):
    received, (kept_ref, *sent_refs) = refs[:3], refs[3:]
    y, x, along_x = place()
    own = jnp.where(along_x, y, x)
    for g in range(2):
        for n, step in enumerate((0, *STEPS)):
            block = lax.rem(own + step, 4)
            total = keep_ref[g, block]
            for part in received:
                total = total + part[g, block].astype(F32)
            if step == 0:
                kept_ref[g] = total
            else:
                sent_refs[n - 1][g] = total.astype(BF16)


def sum_kernel(keep_ref, *refs):
    received, out_ref = refs[:-1], refs[-1]
    total = keep_ref[...].astype(F32)
    for part in received:
        total = total + part[...].astype(F32)
    out_ref[...] = total.astype(BF16)


def last_kernel(scale, own, near, next_near, far, first_ref, second_ref):
    for g, out_ref in enumerate((first_ref, second_ref)):
        total = (own[g].astype(F32) + far[g].astype(F32)) + (
            near[g].astype(F32) + next_near[g].astype(F32)
        )
        out_ref[...] = (total * scale)[:BLOCK]


VMEM = pl.BlockSpec(memory_space=pltpu.VMEM)
SMEM = pl.BlockSpec(memory_space=pltpu.SMEM)
HBM = pl.BlockSpec(memory_space=pltpu.HBM)


def call(kernel, operands, in_specs, outs, scratch=(), flops=0, moved=1 << 20, limit=4):
    return pl.pallas_call(
        kernel,
        out_shape=[jax.ShapeDtypeStruct(shape, dtype) for shape, dtype in outs],
        in_specs=in_specs,
        out_specs=[VMEM] * len(outs),
        scratch_shapes=[
            pltpu.VMEM(*one) if isinstance(one, tuple) else one for one in scratch
        ],
        compiler_params=pltpu.CompilerParams(vmem_limit_bytes=limit << 20),
        cost_estimate=pl.CostEstimate(flops=flops, bytes_accessed=moved, transcendentals=0),
    )(*operands)


CONV_FLOPS = 2 * F * POS * 27 * C * C
WIDE = ((9 * C, 3 * C), BF16)


def frame_shape(count, dtype=BF16):
    return ((count, POS, C), dtype)


def shifted(value, steps):
    return seq_permute(value, lambda z: z + steps)


def dp_permute(value, target):
    return lax.ppermute(value, "dp", [(source, target(source)) for source in range(32)])


def along_x(step):
    return lambda d: (d // 8) * 8 + (d % 8 + 2 * step) % 8


def along_y(step):
    return lambda d: (d + 8 * step) % 32


def crossed(first, second):
    return lambda d: second(d) if d % 2 else first(d)


def seq_permute(value, target):
    return lax.ppermute(value, "seq", [(source, target(source) % 8) for source in range(8)])


def per_device(frames, clip_ids, cotangent, conv1_weight, conv2_weight):
    own_frames = frames.reshape(F, POS, C)
    own_cot = cotangent.reshape(F, POS, C)
    clip_ids, own_frames, own_cot, conv1_weight, conv2_weight = (
        pltpu.with_memory_space_constraint(value, pltpu.HBM)
        for value in (clip_ids, own_frames, own_cot, conv1_weight, conv2_weight)
    )
    clip_ids, tail, head, weight1, frame_copy = call(
        halo_kernel,
        (clip_ids, own_frames, own_cot, conv1_weight),
        [HBM] * 4,
        [
            (clip_ids.shape, jnp.int32),
            frame_shape(4),
            frame_shape(6),
            ((27 * C, C), BF16),
            frame_shape(F + 1),
        ],
        [pltpu.SemaphoreType.DMA((6,))],
    )
    head = shifted(head, -1)
    tail = shifted(tail, 1)
    local = call(
        local_kernel,
        (clip_ids, frame_copy, own_cot, weight1, conv2_weight),
        [SMEM, VMEM, HBM, VMEM, HBM],
        [
            frame_shape(F + 1),
            ((27 * C, C), BF16),
            WIDE,
            WIDE,
            frame_shape(F, F32),
            frame_shape(F, F32),
            ((F, C), F32),
            frame_shape(F),
            ((F + 1, 3 * C, POS), BF16),
            ((F + 1, POS, 3 * C), BF16),
            ((3 * C, 9 * C), F32),
            frame_shape(F),
            ((9 * C, 3 * C), F32),
        ],
        [
            ((3 * C, 4 * POS), BF16),
            ((4 * POS, 9 * C), BF16),
            ((9 * C, 4 * POS), BF16),
            ((4 * POS, 3 * C), BF16),
            frame_shape(4, F32),
            pltpu.SemaphoreType.DMA((2,)),
        ],
        flops=CONV_FLOPS * 2,
        limit=24,
    )
    tail, head, local = lax.optimization_barrier((tail, head, local))
    cot_copy, weight2, conv_weight, back_weight, *partial = local
    block = ((2, 16, PADDED, C), F32)
    hidden, act_grad, keep, send = call(
        main_kernel,
        (clip_ids, frame_copy, cot_copy, tail, head, conv_weight, back_weight, *partial),
        [SMEM] + [VMEM] * 15,
        [frame_shape(F), frame_shape(F), block, (block[0], BF16)],
        [
            frame_shape(5),
            frame_shape(5),
            frame_shape(2, F32),
            frame_shape(2, F32),
            frame_shape(4, F32),
            ((3, POS, 3 * C), BF16),
            ((4 * POS, 9 * C), BF16),
            ((3, 3 * C, POS), BF16),
            ((9 * C, 4 * POS), BF16),
            ((3 * C, 4 * POS), BF16),
            ((4 * POS, 3 * C), BF16),
            ((2, 27 * C, C), F32),
        ],
        flops=CONV_FLOPS * 3 // 2,
        limit=28,
    )
    recv = dp_permute(send, lambda d: d ^ 1)
    keep, *sent = call(
        first_kernel,
        (keep, recv),
        [VMEM] * 2,
        [((2, 4, PADDED, C), F32)] + [((2, 4, PADDED, C), BF16)] * 3,
    )
    sent, hidden = lax.optimization_barrier((sent, hidden))
    recv = [
        dp_permute(part, crossed(along_x(s), along_y(s))) for s, part in zip(STEPS, sent)
    ]
    half_out, wide_weight = call(
        forward_kernel,
        (clip_ids, hidden, frame_copy, tail, conv_weight, weight2),
        [SMEM] + [VMEM] * 5,
        [frame_shape(HALF), WIDE],
        [frame_shape(5), frame_shape(2, F32), frame_shape(HALF + 3)],
        flops=CONV_FLOPS * 3 // 4,
        limit=12,
    )
    recv, half_out = lax.optimization_barrier((recv, half_out))
    pair = (2, PADDED, C)
    keep, *sent = call(
        second_kernel, (keep, *recv), [VMEM] * 4, [(pair, F32)] + [(pair, BF16)] * 3
    )
    sent, half_out = lax.optimization_barrier((sent, half_out))
    recv = [
        dp_permute(part, crossed(along_y(s), along_x(s))) for s, part in zip(STEPS, sent)
    ]
    (block_out,) = call(
        rest_kernel,
        (clip_ids, hidden, frame_copy, wide_weight, half_out),
        [SMEM] + [VMEM] * 4,
        [frame_shape(F)],
        [frame_shape(HALF + 3)],
        flops=CONV_FLOPS // 2,
        limit=8,
    )
    recv, block_out = lax.optimization_barrier((recv, block_out))
    (total,) = call(sum_kernel, (keep, *recv), [VMEM] * 4, [(pair, BF16)])
    head, total = lax.optimization_barrier((head, total))
    other = seq_permute(total, lambda z: z ^ 1)
    (act_grad_next,) = call(
        next_grad_kernel,
        (clip_ids, frame_copy, head, conv_weight, back_weight),
        [SMEM] + [VMEM] * 4,
        [frame_shape(2)],
        [frame_shape(5), frame_shape(5), frame_shape(2, F32), frame_shape(2, F32)],
        flops=CONV_FLOPS // 2,
        limit=8,
    )
    other, act_grad_next = lax.optimization_barrier((other, act_grad_next))
    (total,) = call(sum_kernel, (total, other), [VMEM] * 2, [(pair, BF16)])
    total, act_grad = lax.optimization_barrier((total, act_grad))
    others = [
        seq_permute(total, lambda z, s=s: z + s if z % 2 else z - s) for s in (1, 2, 3)
    ]
    (input_grad,) = call(
        backward_kernel,
        (clip_ids, act_grad, act_grad_next, cot_copy, weight1),
        [SMEM] + [VMEM] * 4,
        [frame_shape(F)],
        [frame_shape(F + 3), WIDE],
        flops=CONV_FLOPS,
        limit=8,
    )
    others, input_grad = lax.optimization_barrier((others, input_grad))
    rows = lax.axis_size("dp") * lax.axis_size("seq") * F * POS
    first_grad, second_grad = call(
        lambda *refs: last_kernel(rows**-0.5, *refs),
        (total, *others),
        [VMEM] * 4,
        [((BLOCK, C), F32)] * 2,
    )
    return (
        block_out.reshape(frames.shape),
        input_grad.reshape(frames.shape),
        first_grad,
        second_grad,
    )


def solution(mesh):
    return jax.shard_map(
        per_device,
        mesh=mesh,
        in_specs=(
            P("dp", "seq", None, None, None),
            P("dp", None),
            P("dp", "seq", None, None, None),
            P(),
            P(),
        ),
        out_specs=(
            P("dp", "seq", None, None, None),
            P("dp", "seq", None, None, None),
            P("dp", None),
            P("dp", None),
        ),
        check_vma=False,
    )
```

```python
import jax
import jax.numpy as jnp
from jax import lax
from jax.experimental import pallas as pl
from jax.experimental.pallas import tpu as pltpu
from jax.sharding import PartitionSpec as P

C = 128
GROUP = 4
F = 8
HT = 8
WT = 32
POS = HT * WT
BLOCK = 108
PADDED = 112
BF16 = jnp.bfloat16
F32 = jnp.float32


def clip_at(clips, frame):
    return clips[0, jnp.clip(frame, 0, clips.shape[1] - 1)]


def past_slots(clips, first, t, base, none):
    slots = []
    for k in range(3):
        frame = first + t + k - 2
        same = clip_at(clips, frame) == clip_at(clips, first + t)
        slots.append(jnp.where(same & (frame >= 0), t + k - 2 + base, none))
    return slots


def next_slots(clips, first, t, base, none):
    slots = []
    for q in range(3):
        frame = first + t + q
        same = clip_at(clips, frame) == clip_at(clips, first + t)
        slots.append(jnp.where(same & (frame < clips.shape[1]), t + q + base, none))
    return slots


def column(rows):
    return lax.broadcasted_iota(jnp.int32, (rows, C), 0) % WT


def shift_down(value):
    return jnp.where(column(POS) == 0, 0.0, pltpu.roll(value, 1, 0))


def shift_up(value):
    return jnp.where(column(POS) == WT - 1, 0.0, pltpu.roll(value, POS - 1, 0))


def row_pieces(frame):
    edge = jnp.zeros((WT, C), frame.dtype)
    return [
        jnp.concatenate([edge, frame[: POS - WT]], axis=0),
        frame,
        jnp.concatenate([frame[WT:], edge], axis=0),
    ]


def column_pieces(frame):
    wide = frame.astype(F32)
    return jnp.concatenate([shift_up(wide).astype(BF16), frame, shift_down(wide).astype(BF16)], axis=1)


def conv_frame(window, slots, weight):
    pieces = []
    for slot in slots:
        pieces += row_pieces(window[slot])
    taps = jnp.dot(jnp.concatenate(pieces, axis=1), weight[...], preferred_element_type=F32)
    return shift_down(taps[:, :C]) + taps[:, C : 2 * C] + shift_up(taps[:, 2 * C :])


def forward_weight(weight_ref, out_ref):
    for outer in range(9):
        for b in range(3):
            out_ref[outer * C : (outer + 1) * C, b * C : (b + 1) * C] = weight_ref[
                (outer * 3 + b) * C : (outer * 3 + b + 1) * C, :
            ]


def adjoint_weight(weight_ref, out_ref):
    for outer in range(9):
        for b in range(3):
            tap = 26 - (outer * 3 + b)
            out_ref[outer * C : (outer + 1) * C, b * C : (b + 1) * C] = weight_ref[
                tap * C : (tap + 1) * C, :
            ].T


def group_mean(sums):
    count = len(sums)
    sums = jnp.concatenate(sums + [jnp.zeros_like(sums[0])] * (F - count), axis=0)
    lane = lax.broadcasted_iota(jnp.int32, sums.shape, 1)
    pairs = sums + jnp.where(lane % 2 == 0, pltpu.roll(sums, C - 1, 1), pltpu.roll(sums, 1, 1))
    quads = pairs + jnp.where(lane % 4 < 2, pltpu.roll(pairs, C - 2, 1), pltpu.roll(pairs, 2, 1))
    mean = quads * (1.0 / (GROUP * POS))
    return [mean[t : t + 1] for t in range(count)]


def tile_sum(value):
    return jnp.sum(value, axis=0, keepdims=True)


def normalize(act, count):
    center = group_mean([tile_sum(act[t]) for t in range(count)])
    sums = []
    for t in range(count):
        away = act[t] - center[t]
        act[t] = away
        sums.append(tile_sum(away * away))
    scale = [lax.rsqrt(mean + 1e-06) for mean in group_mean(sums)]
    for t in range(count):
        act[t] = act[t] * scale[t]
    return scale


def gate_of(normed):
    return 1.0 / (1.0 + jnp.exp(-normed))


def hidden_of(normed):
    return (normed * gate_of(normed)).astype(BF16)


def norm_adjoint(act, back, scale, work):
    count = len(scale)
    first, second = [], []
    for t in range(count):
        normed = act(t)
        gate = gate_of(normed)
        grad = back(t) * (gate * (1.0 + normed * (1.0 - gate)))
        work[t] = grad
        first.append(tile_sum(grad))
        second.append(tile_sum(grad * normed))
    first, second = group_mean(first), group_mean(second)
    return [(scale[t] * (work[t] - first[t] - act(t) * second[t])).astype(BF16) for t in range(count)]


def first_frame():
    return lax.axis_index("seq") * F


def halo_kernel(
    clips, frames, cot, weight1, clips_copy, tail, head, weight1_copy, window, sems
):
    copies = [
        pltpu.make_async_copy(weight1, weight1_copy, sems.at[4]),
        pltpu.make_async_copy(frames, window.at[:F], sems.at[5]),
        pltpu.make_async_copy(clips, clips_copy, sems.at[3]),
        pltpu.make_async_copy(frames.at[F - 4 :], tail, sems.at[0]),
        pltpu.make_async_copy(frames.at[:2], head.at[:2], sems.at[1]),
        pltpu.make_async_copy(cot.at[:4], head.at[2:], sems.at[2]),
    ]
    for copy in copies:
        copy.start()
    window[F] = jnp.zeros((POS, C), BF16)
    for copy in copies:
        copy.wait()


SIDES = (0, 1, F - 2, F - 1)
EDGE = F - 2


def local_kernel(
    clips,
    window,
    cot,
    weight1,
    weight2,
    cot_window,
    weight2_copy,
    conv_weight,
    back_weight,
    act,
    back,
    scales,
    hidden,
    frame_t,
    cot_shifted,
    second_part,
    act_grad,
    first_part,
    hidden_t,
    cot_taps,
    frame_taps,
    grad_shifted,
    work,
    sems,
):
    copies = [
        pltpu.make_async_copy(weight2, weight2_copy, sems.at[0]),
        pltpu.make_async_copy(cot, cot_window.at[:F], sems.at[1]),
    ]
    for copy in copies:
        copy.start()
    cot_window[F] = jnp.zeros((POS, C), BF16)
    frame_t[F] = jnp.zeros((3 * C, POS), BF16)
    cot_shifted[F] = jnp.zeros((POS, 3 * C), BF16)
    first = first_frame()
    forward_weight(weight1, conv_weight)
    for t in range(2, F):
        if t == 4:
            for copy in copies:
                copy.wait()
        act[t] = conv_frame(window, past_slots(clips, first, t, 0, F), conv_weight)
    adjoint_weight(weight2_copy, back_weight)
    for f in range(F):
        cot_shifted[f] = column_pieces(cot_window[f])
        for a, piece in enumerate(row_pieces(window[f])):
            frame_t[f, a * C : (a + 1) * C, :] = piece.T
    for t in range(EDGE):
        back[t] = conv_frame(cot_window, next_slots(clips, first, t, 0, F), back_weight)
    scale = normalize(act.at[2:F], F - 2)
    for t in range(2, F):
        scales[t : t + 1] = scale[t - 2]
    for t in range(2, F):
        value = hidden_of(act[t])
        hidden[t] = value
        if t < EDGE:
            place = slice((t - 2) * POS, (t - 1) * POS)
            for a, piece in enumerate(row_pieces(value)):
                hidden_t[a * C : (a + 1) * C, place] = piece.T
            slots = next_slots(clips, first, t, 0, F)
            for k in range(3):
                cot_taps[place, 3 * C * k : 3 * C * (k + 1)] = cot_shifted[slots[2 - k]]
    second_part[...] = jnp.dot(hidden_t[...], cot_taps[...], preferred_element_type=F32)
    rounded = norm_adjoint(lambda n: act[2 + n], lambda n: back[2 + n], scale[: EDGE - 2], work)
    for n, value in enumerate(rounded):
        act_grad[2 + n] = value
        place = slice(n * POS, (n + 1) * POS)
        grad_shifted[place] = column_pieces(value)
        slots = past_slots(clips, first, 2 + n, 0, F)
        for k in range(3):
            frame_taps[3 * C * k : 3 * C * (k + 1), place] = frame_t[slots[k]]
    first_part[...] = jnp.dot(frame_taps[...], grad_shifted[...], preferred_element_type=F32)


def split_rows(grads, g, keep_ref, send_ref):
    own = lax.rem(lax.axis_index("dp"), 2) == 0
    for m in range(16):
        low = grads[g, 2 * BLOCK * m : 2 * BLOCK * m + BLOCK]
        high = grads[g, 2 * BLOCK * m + BLOCK : 2 * BLOCK * (m + 1)]
        keep_ref[g, m, :BLOCK] = jnp.where(own, low, high)
        keep_ref[g, m, BLOCK:] = jnp.zeros((PADDED - BLOCK, C), F32)
        send_ref[g, m, :BLOCK] = jnp.where(own, high, low).astype(BF16)
        send_ref[g, m, BLOCK:] = jnp.zeros((PADDED - BLOCK, C), BF16)


def main_kernel(
    clips,
    frames,
    cot,
    tail,
    head,
    conv_weight,
    back_weight,
    act_in,
    back_in,
    scales,
    hidden_in,
    frame_t_in,
    cot_shifted_in,
    second_part,
    act_grad_in,
    first_part,
    hidden_ref,
    act_grad_ref,
    keep_ref,
    send_ref,
    window,
    cot_window,
    act,
    back,
    work,
    cot_shifted,
    cot_taps,
    frame_t,
    frame_taps,
    hidden_t,
    grad_shifted,
    grads,
):
    first = first_frame()
    zero = jnp.zeros((POS, C), BF16)
    for f in range(2):
        window[f] = tail[2 + f]
        window[2 + f] = frames[f]
        cot_window[f] = cot[EDGE + f]
        cot_window[2 + f] = head[2 + f]
    window[4] = zero
    cot_window[4] = zero

    for t in range(2):
        act[t] = conv_frame(window, past_slots(clips, first, t, 2, 4), conv_weight)
        back[t] = conv_frame(
            cot_window, next_slots(clips, first, EDGE + t, -EDGE, 4), back_weight
        )
    for f in range(2):
        cot_shifted[f] = column_pieces(cot_window[2 + f])
        for a, piece in enumerate(row_pieces(window[f])):
            frame_t[f, a * C : (a + 1) * C, :] = piece.T
    cot_shifted[2] = jnp.zeros((POS, 3 * C), BF16)
    frame_t[2] = jnp.zeros((3 * C, POS), BF16)
    scale = normalize(act, 2) + [scales[t : t + 1] for t in SIDES[2:]]
    for t in range(F):
        hidden_ref[t] = hidden_of(act[t]) if t < 2 else hidden_in[t]

    for n, s in enumerate(SIDES):
        place = slice(n * POS, (n + 1) * POS)
        for a, piece in enumerate(row_pieces(hidden_ref[s])):
            hidden_t[a * C : (a + 1) * C, place] = piece.T
        near = next_slots(clips, first, s, 0, F)
        far = next_slots(clips, first, s, -F, 2)
        for k in range(3):
            cot_taps[place, 3 * C * k : 3 * C * (k + 1)] = (
                cot_shifted_in[near[2 - k]] if s + 2 - k < F else cot_shifted[far[2 - k]]
            )
    second_grad = second_part[...] + jnp.dot(
        hidden_t[...], cot_taps[...], preferred_element_type=F32
    )
    for k in range(3):
        for a in range(3):
            for b in range(3):
                tap = (k * 3 + a) * 3 + b
                grads[1, tap * C : (tap + 1) * C] = second_grad[
                    a * C : (a + 1) * C, (k * 3 + b) * C : (k * 3 + b + 1) * C
                ]

    rounded = norm_adjoint(
        lambda n: act[n] if n < 2 else act_in[SIDES[n]],
        lambda n: back_in[n] if n < 2 else back[n - 2],
        scale,
        work,
    )
    for t in range(2, EDGE):
        act_grad_ref[t] = act_grad_in[t]
    for n, t in enumerate(SIDES):
        act_grad_ref[t] = rounded[n]
        place = slice(n * POS, (n + 1) * POS)
        grad_shifted[place] = column_pieces(rounded[n])
        near = past_slots(clips, first, t, 0, F)
        far = past_slots(clips, first, t, 2, 2)
        for k in range(3):
            frame_taps[3 * C * k : 3 * C * (k + 1), place] = (
                frame_t_in[near[k]] if t + k - 2 >= 0 else frame_t[far[k]]
            )
    split_rows(grads, 1, keep_ref, send_ref)
    first_grad = first_part[...] + jnp.dot(
        frame_taps[...], grad_shifted[...], preferred_element_type=F32
    )
    for outer in range(9):
        for b in range(3):
            tap = outer * 3 + b
            grads[0, tap * C : (tap + 1) * C] = first_grad[
                outer * C : (outer + 1) * C, b * C : (b + 1) * C
            ]
    split_rows(grads, 0, keep_ref, send_ref)


HALF = F // 2


def residual_frames(clips, frames, hidden, weight, out_ref, start):
    first = first_frame()
    for t in range(HALF):
        slots = past_slots(clips, first, start + t, 2 - start, HALF + 2)
        out = conv_frame(hidden, slots, weight)
        out_ref[start + t] = (frames[start + t].astype(F32) + out).astype(BF16)


def fill(window, parts):
    count = 0
    for part in parts:
        for f in range(part.shape[0]):
            window[count] = part[f]
            count += 1
    window[count] = jnp.zeros((POS, C), BF16)


def forward_kernel(
    clips, hidden_in, frames, tail, conv_weight, weight2, out_ref, weight, window, act, hidden
):
    first = first_frame()
    fill(window, [tail])
    for t in range(2):
        act[t] = conv_frame(window, past_slots(clips, first, t - 2, 4, 4), conv_weight)
    normalize(act, 2)
    for t in range(2):
        hidden[t] = hidden_of(act[t])
    fill(hidden.at[2:], [hidden_in.at[:HALF]])
    forward_weight(weight2, weight)
    residual_frames(clips, frames, hidden, weight, out_ref, 0)


def rest_kernel(clips, hidden_in, frames, weight, half, out_ref, hidden):
    fill(hidden, [hidden_in.at[HALF - 2 :]])
    for t in range(HALF):
        out_ref[t] = half[t]
    residual_frames(clips, frames, hidden, weight, out_ref, HALF)


def next_grad_kernel(
    clips, frames, head, conv_weight, back_weight, out_ref, window, cot_window, act, back
):
    first = first_frame()
    zero = jnp.zeros((POS, C), BF16)
    for f in range(2):
        window[f] = frames[F - 2 + f]
        window[2 + f] = head[f]
    for f in range(4):
        cot_window[f] = head[2 + f]
    window[4] = zero
    cot_window[4] = zero
    for t in range(2):
        act[t] = conv_frame(window, past_slots(clips, first, F + t, 2 - F, 4), conv_weight)
        back[t] = conv_frame(cot_window, next_slots(clips, first, F + t, -F, 4), back_weight)
    scale = normalize(act, 2)
    for t, rounded in enumerate(
        norm_adjoint(lambda t: act[t], lambda t: back[t], scale, back)
    ):
        out_ref[t] = rounded


def adjoint_frames(clips, cot, act_grad, weight, out_ref, start):
    first = first_frame()
    for t in range(HALF):
        slots = next_slots(clips, first, start + t, -start, HALF + 2)
        out = conv_frame(act_grad, slots, weight)
        out_ref[start + t] = (cot[start + t].astype(F32) + out).astype(BF16)


def backward_kernel(clips, act_grad_in, cot, weight1, out_ref, weight, act_grad):
    fill(act_grad, [act_grad_in.at[: HALF + 2]])
    adjoint_weight(weight1, weight)
    adjoint_frames(clips, cot, act_grad, weight, out_ref, 0)


def last_half_kernel(clips, act_grad_in, next_in, cot, weight, half, out_ref, act_grad):
    fill(act_grad, [act_grad_in.at[HALF:], next_in])
    for t in range(HALF):
        out_ref[t] = half[t]
    adjoint_frames(clips, cot, act_grad, weight, out_ref, HALF)


STEPS = (2, 1, 3)


def place():
    index = lax.axis_index("dp")
    return lax.div(index, 8), lax.rem(lax.div(index, 2), 4), lax.rem(index, 2) == 0


def first_kernel(keep_ref, part, kept_ref, *sent_refs):
    y, x, along_x = place()
    for g in range(2):
        for other in range(4):
            for n, step in enumerate((0, *STEPS)):
                block = jnp.where(
                    along_x, 4 * other + lax.rem(x + step, 4), 4 * lax.rem(y + step, 4) + other
                )
                total = keep_ref[g, block] + part[g, block].astype(F32)
                if step == 0:
                    kept_ref[g, other] = total
                else:
                    sent_refs[n - 1][g, other] = total.astype(BF16)


def second_kernel(keep_ref, *refs):
    received, (kept_ref, *sent_refs) = refs[:3], refs[3:]
    y, x, along_x = place()
    own = jnp.where(along_x, y, x)
    for g in range(2):
        for n, step in enumerate((0, *STEPS)):
            block = lax.rem(own + step, 4)
            total = keep_ref[g, block]
            for part in received:
                total = total + part[g, block].astype(F32)
            if step == 0:
                kept_ref[g] = total
            else:
                sent_refs[n - 1][g] = total.astype(BF16)


def sum_kernel(keep_ref, *refs):
    received, out_ref = refs[:-1], refs[-1]
    total = keep_ref[...].astype(F32)
    for part in received:
        total = total + part[...].astype(F32)
    out_ref[...] = total.astype(BF16)


def last_kernel(scale, own, near, next_near, far, first_ref, second_ref):
    for g, out_ref in enumerate((first_ref, second_ref)):
        total = (own[g].astype(F32) + far[g].astype(F32)) + (
            near[g].astype(F32) + next_near[g].astype(F32)
        )
        out_ref[...] = (total * scale)[:BLOCK]


VMEM = pl.BlockSpec(memory_space=pltpu.VMEM)
SMEM = pl.BlockSpec(memory_space=pltpu.SMEM)
HBM = pl.BlockSpec(memory_space=pltpu.HBM)


def call(kernel, operands, in_specs, outs, scratch=(), flops=0, moved=1 << 20, limit=4):
    return pl.pallas_call(
        kernel,
        out_shape=[jax.ShapeDtypeStruct(shape, dtype) for shape, dtype in outs],
        in_specs=in_specs,
        out_specs=[VMEM] * len(outs),
        scratch_shapes=[
            pltpu.VMEM(*one) if isinstance(one, tuple) else one for one in scratch
        ],
        compiler_params=pltpu.CompilerParams(vmem_limit_bytes=limit << 20),
        cost_estimate=pl.CostEstimate(flops=flops, bytes_accessed=moved, transcendentals=0),
    )(*operands)


CONV_FLOPS = 2 * F * POS * 27 * C * C
WIDE = ((9 * C, 3 * C), BF16)


def frame_shape(count, dtype=BF16):
    return ((count, POS, C), dtype)


def shifted(value, steps):
    return seq_permute(value, lambda z: z + steps)


def dp_permute(value, target):
    return lax.ppermute(value, "dp", [(source, target(source)) for source in range(32)])


def along_x(step):
    return lambda d: (d // 8) * 8 + (d % 8 + 2 * step) % 8


def along_y(step):
    return lambda d: (d + 8 * step) % 32


def crossed(first, second):
    return lambda d: second(d) if d % 2 else first(d)


def seq_permute(value, target):
    return lax.ppermute(value, "seq", [(source, target(source) % 8) for source in range(8)])


def per_device(frames, clip_ids, cotangent, conv1_weight, conv2_weight):
    own_frames = frames.reshape(F, POS, C)
    own_cot = cotangent.reshape(F, POS, C)
    clip_ids, own_frames, own_cot, conv1_weight, conv2_weight = (
        pltpu.with_memory_space_constraint(value, pltpu.HBM)
        for value in (clip_ids, own_frames, own_cot, conv1_weight, conv2_weight)
    )
    clip_ids, tail, head, weight1, frame_copy = call(
        halo_kernel,
        (clip_ids, own_frames, own_cot, conv1_weight),
        [HBM] * 4,
        [
            (clip_ids.shape, jnp.int32),
            frame_shape(4),
            frame_shape(6),
            ((27 * C, C), BF16),
            frame_shape(F + 1),
        ],
        [pltpu.SemaphoreType.DMA((6,))],
    )
    head = shifted(head, -1)
    tail = shifted(tail, 1)
    local = call(
        local_kernel,
        (clip_ids, frame_copy, own_cot, weight1, conv2_weight),
        [SMEM, VMEM, HBM, VMEM, HBM],
        [
            frame_shape(F + 1),
            ((27 * C, C), BF16),
            WIDE,
            WIDE,
            frame_shape(F, F32),
            frame_shape(F, F32),
            ((F, C), F32),
            frame_shape(F),
            ((F + 1, 3 * C, POS), BF16),
            ((F + 1, POS, 3 * C), BF16),
            ((3 * C, 9 * C), F32),
            frame_shape(F),
            ((9 * C, 3 * C), F32),
        ],
        [
            ((3 * C, 4 * POS), BF16),
            ((4 * POS, 9 * C), BF16),
            ((9 * C, 4 * POS), BF16),
            ((4 * POS, 3 * C), BF16),
            frame_shape(4, F32),
            pltpu.SemaphoreType.DMA((2,)),
        ],
        flops=CONV_FLOPS * 2,
        limit=24,
    )
    tail, head, local = lax.optimization_barrier((tail, head, local))
    cot_copy, weight2, conv_weight, back_weight, *partial = local
    block = ((2, 16, PADDED, C), F32)
    hidden, act_grad, keep, send = call(
        main_kernel,
        (clip_ids, frame_copy, cot_copy, tail, head, conv_weight, back_weight, *partial),
        [SMEM] + [VMEM] * 15,
        [frame_shape(F), frame_shape(F), block, (block[0], BF16)],
        [
            frame_shape(5),
            frame_shape(5),
            frame_shape(2, F32),
            frame_shape(2, F32),
            frame_shape(4, F32),
            ((3, POS, 3 * C), BF16),
            ((4 * POS, 9 * C), BF16),
            ((3, 3 * C, POS), BF16),
            ((9 * C, 4 * POS), BF16),
            ((3 * C, 4 * POS), BF16),
            ((4 * POS, 3 * C), BF16),
            ((2, 27 * C, C), F32),
        ],
        flops=CONV_FLOPS * 3 // 2,
        limit=28,
    )
    recv = dp_permute(send, lambda d: d ^ 1)
    act_grad, keep = lax.optimization_barrier((act_grad, keep))
    half_grad, wide_adjoint = call(
        backward_kernel,
        (clip_ids, act_grad, cot_copy, weight1),
        [SMEM] + [VMEM] * 3,
        [frame_shape(HALF), WIDE],
        [frame_shape(HALF + 3)],
        flops=CONV_FLOPS // 2,
        limit=8,
    )
    recv, half_grad = lax.optimization_barrier((recv, half_grad))
    keep, *sent = call(
        first_kernel,
        (keep, recv),
        [VMEM] * 2,
        [((2, 4, PADDED, C), F32)] + [((2, 4, PADDED, C), BF16)] * 3,
    )
    sent, hidden = lax.optimization_barrier((sent, hidden))
    recv = [
        dp_permute(part, crossed(along_x(s), along_y(s))) for s, part in zip(STEPS, sent)
    ]
    half_out, wide_weight = call(
        forward_kernel,
        (clip_ids, hidden, frame_copy, tail, conv_weight, weight2),
        [SMEM] + [VMEM] * 5,
        [frame_shape(HALF), WIDE],
        [frame_shape(5), frame_shape(2, F32), frame_shape(HALF + 3)],
        flops=CONV_FLOPS * 3 // 4,
        limit=12,
    )
    recv, half_out = lax.optimization_barrier((recv, half_out))
    pair = (2, PADDED, C)
    keep, *sent = call(
        second_kernel, (keep, *recv), [VMEM] * 4, [(pair, F32)] + [(pair, BF16)] * 3
    )
    sent, half_out = lax.optimization_barrier((sent, half_out))
    recv = [
        dp_permute(part, crossed(along_y(s), along_x(s))) for s, part in zip(STEPS, sent)
    ]
    (block_out,) = call(
        rest_kernel,
        (clip_ids, hidden, frame_copy, wide_weight, half_out),
        [SMEM] + [VMEM] * 4,
        [frame_shape(F)],
        [frame_shape(HALF + 3)],
        flops=CONV_FLOPS // 2,
        limit=8,
    )
    recv, block_out = lax.optimization_barrier((recv, block_out))
    (total,) = call(sum_kernel, (keep, *recv), [VMEM] * 4, [(pair, BF16)])
    head, total = lax.optimization_barrier((head, total))
    other = seq_permute(total, lambda z: z ^ 1)
    (act_grad_next,) = call(
        next_grad_kernel,
        (clip_ids, frame_copy, head, conv_weight, back_weight),
        [SMEM] + [VMEM] * 4,
        [frame_shape(2)],
        [frame_shape(5), frame_shape(5), frame_shape(2, F32), frame_shape(2, F32)],
        flops=CONV_FLOPS // 2,
        limit=8,
    )
    other, act_grad_next = lax.optimization_barrier((other, act_grad_next))
    (total,) = call(sum_kernel, (total, other), [VMEM] * 2, [(pair, BF16)])
    total, act_grad = lax.optimization_barrier((total, act_grad))
    others = [
        seq_permute(total, lambda z, s=s: z + s if z % 2 else z - s) for s in (1, 2, 3)
    ]
    (input_grad,) = call(
        last_half_kernel,
        (clip_ids, act_grad, act_grad_next, cot_copy, wide_adjoint, half_grad),
        [SMEM] + [VMEM] * 5,
        [frame_shape(F)],
        [frame_shape(HALF + 3)],
        flops=CONV_FLOPS // 2,
        limit=8,
    )
    others, input_grad = lax.optimization_barrier((others, input_grad))
    rows = lax.axis_size("dp") * lax.axis_size("seq") * F * POS
    first_grad, second_grad = call(
        lambda *refs: last_kernel(rows**-0.5, *refs),
        (total, *others),
        [VMEM] * 4,
        [((BLOCK, C), F32)] * 2,
    )
    return (
        block_out.reshape(frames.shape),
        input_grad.reshape(frames.shape),
        first_grad,
        second_grad,
    )


def solution(mesh):
    return jax.shard_map(
        per_device,
        mesh=mesh,
        in_specs=(
            P("dp", "seq", None, None, None),
            P("dp", None),
            P("dp", "seq", None, None, None),
            P(),
            P(),
        ),
        out_specs=(
            P("dp", "seq", None, None, None),
            P("dp", "seq", None, None, None),
            P("dp", None),
            P("dp", None),
        ),
        check_vma=False,
    )
```
